32 devices in a mesh: rep: 4 (over z), fsdp: 2 (over x), seq: 4 (over y, core).
Axes of the slice: x: 2, y: 2, z: 4, core: 2. Of those that a mesh axis runs over, the one named last changes fastest.
Arguments:
- tokens: bfloat16 [8, 1024, 640], P(('rep', 'fsdp'), 'seq'), may hold values from -6 to 6
- d_out: bfloat16 [8, 1024, 640], P(('rep', 'fsdp'), 'seq'), may hold values from -6 to 6
- doc_lengths: int32 [8, 3], P(('rep', 'fsdp')), may hold values from 1 to 640, 1024 in all within a row
- w_query: bfloat16 [640, 1024], P('fsdp'), may hold values from -0.25 to 0.25
- w_key: bfloat16 [640, 256], P('fsdp'), may hold values from -0.25 to 0.25
- w_value: bfloat16 [640, 256], P('fsdp'), may hold values from -0.25 to 0.25
- w_out: bfloat16 [1024, 640], P('fsdp'), may hold values from -0.1875 to 0.1875
- w_gate: bfloat16 [640, 2048], P('fsdp'), may hold values from -0.25 to 0.25
- w_up: bfloat16 [640, 2048], P('fsdp'), may hold values from -0.25 to 0.25
- w_down: bfloat16 [2048, 640], P('fsdp'), may hold values from -0.125 to 0.125
- g_input: bfloat16 [640], P('fsdp'), may hold values from 0.5 to 1.5
- g_query: bfloat16 [256], P('fsdp'), may hold values from 0.25 to 1.75
- g_key: bfloat16 [256], P('fsdp'), may hold values from 0.25 to 1.75
- g_attn: bfloat16 [640], P('fsdp'), may hold values from 0.5 to 1.5
- g_ffin: bfloat16 [640], P('fsdp'), may hold values from 0.5 to 1.5
- g_ffout: bfloat16 [640], P('fsdp'), may hold values from 0.5 to 1.5
Outputs:
- result: bfloat16 [8, 1024, 640], P(('rep', 'fsdp'), 'seq')
- d_tokens: bfloat16 [8, 1024, 640], P(('rep', 'fsdp'), 'seq')
- grad_query: float32 [640, 1024], P('fsdp')
- grad_key: float32 [640, 256], P('fsdp')
- grad_value: float32 [640, 256], P('fsdp')
- grad_out: float32 [1024, 640], P('fsdp')
- grad_gate: float32 [640, 2048], P('fsdp')
- grad_up: float32 [640, 2048], P('fsdp')
- grad_down: float32 [2048, 640], P('fsdp')
- grad_ginput: float32 [640], P('fsdp')
- grad_gquery: float32 [256], P('fsdp')
- grad_gkey: float32 [256], P('fsdp')
- grad_gattn: float32 [640], P('fsdp')
- grad_gffin: float32 [640], P('fsdp')
- grad_gffout: float32 [640], P('fsdp')
The draws below stay inside these ranges and needn't reach their ends.
Inputs may be any that keep to these rules, and one draw needn't show every extreme that they name: `doc_lengths`: each row lists the lengths of the 3 documents packed in order into one sequence; a row sums to 1024 and its largest entry is 640.
All inputs are finite; a program needn't handle non-finite values.
Results may differ from the reference program's by a relative error of at most 0.024.
Values may be sent and summed in bfloat16 or wider, within the bound.
A program may use at most 128 MiB of HBM per device.

```python
import math
import jax
import jax.numpy as jnp
import numpy as np
from jax import lax

D = 640
HEADS = 4
HD = 256
FF = 2048
NDOC = 3
SEQ_LEN = 1024
SEQS_ALL = 8
MAX_DOC = 640


def levels(rng, dims, split, smallest, high):
    def one(dim, parts):
        heights = jax.random.uniform(jax.random.fold_in(jax.random.fold_in(rng, 6), dim), (parts,), jnp.float32, smallest / len(split), high / len(split))
        return jnp.repeat(jnp.exp(heights), dims[dim] // parts).reshape((-1,) + (1,) * (len(dims) - dim - 1))

    loudness = one(*split[0])
    for cut in split[1:]:
        loudness = loudness * one(*cut)
    return loudness


def split_up(count, total, limit, lean):
    loads = [(1 << 20) // math.isqrt(grade ** lean) + 1 for grade in range(2, count + 1)]
    spare, given = total - limit - (count - 1), [1] * (count - 1)
    while spare > 0:
        candidates = [i for i in range(count - 1) if given[i] < limit]
        whole, left = sum([loads[i] for i in candidates]), spare
        for i in candidates:
            addition = min(limit - given[i], max(1, left * loads[i] // whole), spare)
            given[i] = given[i] + addition
            spare = spare - addition
    return np.array([limit] + given)


def uneven(rng, count, total, reach, skew):
    if count == 2:
        one = jax.random.randint(rng, (), max(1, total - reach), min(reach, total - 1) + 1)
        return jnp.stack([one, total - one])
    lengths = jnp.asarray(split_up(count, total, reach, skew), jnp.int32)
    twos = (count - 1) // 2
    donor, receiver = lengths[1:1 + 2 * twos:2], lengths[2:2 + 2 * twos:2]
    margin = jnp.minimum(donor - 1, reach - receiver)
    moved = jax.random.randint(jax.random.fold_in(rng, 1), (twos,), 0, 1 << 20) % (margin + 1)
    lengths = lengths.at[1:1 + 2 * twos:2].set(donor - moved).at[2:2 + 2 * twos:2].set(receiver + moved)
    return lengths[jax.random.permutation(jax.random.fold_in(rng, 2), count)]


def noise(own_key, extent, deviation, reach, split=(), held_as=jnp.bfloat16):
    loudness = levels(own_key, extent, split, -0.22, 0.18) if split else 1.0
    entries = jax.random.normal(own_key, extent, jnp.float32) * deviation * loudness
    return jnp.minimum(jnp.maximum(entries, -reach), reach).astype(held_as)


def setup_inputs(seed: int = 0) -> dict:
    streams_of = jax.random.split(jax.random.key(seed), 17)
    tokens = noise(streams_of[0], (SEQS_ALL, SEQ_LEN, D), 1.0, 6.0, ((0, 8), (1, 4)))
    d_out = noise(streams_of[1], (SEQS_ALL, SEQ_LEN, D), 1.0, 6.0, ((0, 8), (1, 4)))
    doc_lengths = jax.vmap(lambda own: uneven(own, NDOC, SEQ_LEN, MAX_DOC, 0))(jax.random.split(streams_of[2], SEQS_ALL)).reshape((SEQS_ALL, NDOC)).astype(jnp.int32)
    w_query = noise(streams_of[3], (D, HEADS * HD), D ** -0.5, 0.25, ((0, 2),))
    w_key = noise(streams_of[4], (D, HD), D ** -0.5, 0.25, ((0, 2),))
    w_value = noise(streams_of[5], (D, HD), D ** -0.5, 0.25, ((0, 2),))
    w_out = noise(streams_of[6], (HEADS * HD, D), (HEADS * HD) ** -0.5, 0.1875, ((0, 2),))
    w_gate = noise(streams_of[7], (D, FF), D ** -0.5, 0.25, ((0, 2),))
    w_up = noise(streams_of[8], (D, FF), D ** -0.5, 0.25, ((0, 2),))
    w_down = noise(streams_of[9], (FF, D), FF ** -0.5, 0.125, ((0, 2),))
    g_input = jnp.clip(1.0 + 0.1 * jax.random.normal(streams_of[10], (D,), jnp.float32), 0.5, 1.5).astype(jnp.bfloat16)
    g_query = jnp.clip(1.0 + 0.15 * jax.random.normal(streams_of[11], (HD,), jnp.float32), 0.25, 1.75).astype(jnp.bfloat16)
    g_key = jnp.clip(1.0 + 0.15 * jax.random.normal(streams_of[12], (HD,), jnp.float32), 0.25, 1.75).astype(jnp.bfloat16)
    g_attn = jnp.clip(1.0 + 0.1 * jax.random.normal(streams_of[13], (D,), jnp.float32), 0.5, 1.5).astype(jnp.bfloat16)
    g_ffin = jnp.clip(1.0 + 0.1 * jax.random.normal(streams_of[14], (D,), jnp.float32), 0.5, 1.5).astype(jnp.bfloat16)
    g_ffout = jnp.clip(1.0 + 0.1 * jax.random.normal(streams_of[15], (D,), jnp.float32), 0.5, 1.5).astype(jnp.bfloat16)
    return dict(tokens=tokens, d_out=d_out, doc_lengths=doc_lengths, w_query=w_query, w_key=w_key, w_value=w_value, w_out=w_out, w_gate=w_gate, w_up=w_up, w_down=w_down, g_input=g_input, g_query=g_query, g_key=g_key, g_attn=g_attn, g_ffin=g_ffin, g_ffout=g_ffout)


EPS = 1e-06
ROPE_BASE = 1000000.0
MASKED = -1e+30
HIGH = lax.Precision.HIGHEST

@jax.custom_vjp
def low(v):
    return lax.optimization_barrier(v.astype(jnp.bfloat16)).astype(jnp.float32)

@jax.custom_vjp
def low_back(v):
    return v

def low_keep(v):
    return (low(v), None)

def low_pass(kept, grad):
    return (grad,)

def back_keep(v):
    return (v, None)

def back_low(kept, grad):
    return (low(grad),)
low.defvjp(low_keep, low_pass)
low_back.defvjp(back_keep, back_low)

def rms_norm(values, gain_vec):
    return values * lax.rsqrt(lax.optimization_barrier(jnp.mean(values * values, axis=-1, keepdims=True)) + EPS) * gain_vec

def rotate(values, angles):
    half_width = values.shape[-1] // 2
    front_half = values[..., :half_width]
    back_half = values[..., half_width:]
    cos_part = jnp.cos(angles)
    sin_part = jnp.sin(angles)
    return jnp.concatenate([front_half * cos_part - back_half * sin_part, back_half * cos_part + front_half * sin_part], axis=-1)

def frequencies(head_size):
    return jnp.power(jnp.float32(ROPE_BASE), -2.0 * jnp.arange(head_size // 2, dtype=jnp.float32) / head_size)

def layout(lengths_row, total_len):
    doc_ends = jnp.cumsum(lengths_row).astype(jnp.int32)
    starts = (doc_ends - lengths_row).astype(jnp.int32)
    indices = jnp.arange(total_len, dtype=jnp.int32)
    segment = lax.optimization_barrier(jnp.sum((indices[:, None] >= doc_ends[None, :]).astype(jnp.int32), axis=1)).astype(jnp.int32)
    onehot = segment[:, None] == jnp.arange(lengths_row.shape[0], dtype=jnp.int32)[None, :]
    doc_begin = lax.optimization_barrier(jnp.sum(jnp.where(onehot, starts[None, :], 0), axis=1)).astype(jnp.int32)
    return (segment, (indices - doc_begin).astype(jnp.int32))

def matmul(left_side, right_side):
    return jnp.dot(left_side, right_side, precision=HIGH)

def gelu_tanh(values):
    return jax.nn.gelu(values, approximate=True)

def sequence_forward(params, inputs, segment, position):
    w_query, w_key, w_value, w_out, w_gate, w_up, w_down, g_input, g_query, g_key, g_attn, g_ffin, g_ffout = params
    length = inputs.shape[0]
    angles = position.astype(jnp.float32)[:, None] * frequencies(HD)[None, :]
    attn_in = low(rms_norm(inputs, g_input))
    q_proj = low_back(matmul(attn_in, w_query))
    k_proj = low_back(matmul(attn_in, w_key))
    values = low(low_back(matmul(attn_in, w_value)))
    queries = low(rotate(rms_norm(q_proj.reshape(length, HEADS, HD), g_query), angles[:, None, :]))
    keys = low(rotate(rms_norm(k_proj, g_key), angles))
    raw_scores = low_back(jnp.einsum('shd,td->sht', queries, keys, precision=HIGH))
    places = jnp.arange(length, dtype=jnp.int32)
    allowed = (segment[:, None] == segment[None, :]) & (places[:, None] >= places[None, :])
    scores = jnp.where(allowed[:, None, :], raw_scores * HD ** (-0.5), MASKED)
    top_score = lax.optimization_barrier(jnp.max(scores, axis=-1, keepdims=True))
    shifted = jnp.exp(scores - top_score)
    probs = low(shifted / lax.optimization_barrier(jnp.sum(shifted, axis=-1, keepdims=True)))
    mixed = jnp.einsum('sht,td->shd', probs, values, precision=HIGH).reshape(length, HEADS * HD)
    mixed = low(low_back(mixed))
    out_proj = low_back(matmul(mixed, w_out))
    hidden_one = inputs + rms_norm(out_proj, g_attn)
    ff_in = low(rms_norm(hidden_one, g_ffin))
    gate_proj = low_back(matmul(ff_in, w_gate))
    up_proj = low_back(matmul(ff_in, w_up))
    hidden = low(gelu_tanh(gate_proj) * up_proj)
    down_proj = low_back(matmul(hidden, w_down))
    return hidden_one + rms_norm(down_proj, g_ffout)

def reference(tokens, d_out, doc_lengths, w_query, w_key, w_value, w_out, w_gate, w_up, w_down, g_input, g_query, g_key, g_attn, g_ffin, g_ffout):
    params = tuple((entry.astype(jnp.float32) for entry in (w_query, w_key, w_value, w_out, w_gate, w_up, w_down, g_input, g_query, g_key, g_attn, g_ffin, g_ffout)))
    segment, position = jax.vmap(lambda lengths_row: layout(lengths_row, SEQ_LEN))(doc_lengths)

    def forward(weights, inputs):
        per_sequence = jax.checkpoint(lambda element: sequence_forward(weights, element[0], element[1], element[2]))
        return lax.map(per_sequence, (inputs, segment, position))
    result, pullback = jax.vjp(forward, params, tokens.astype(jnp.float32))
    grads, d_inputs = pullback(d_out.astype(jnp.float32))
    return (result.astype(jnp.bfloat16), d_inputs.astype(jnp.bfloat16), grads[0], grads[1], grads[2], grads[3], grads[4], grads[5], grads[6], grads[7], grads[8], grads[9], grads[10], grads[11], grads[12])
```

```python
import functools

import jax
import jax.numpy as jnp
import numpy as np
from jax import lax
from jax.experimental import pallas as pl
from jax.experimental.pallas import tpu as pltpu
from jax.sharding import PartitionSpec as P

EPS = 1e-06
ROPE_BASE = 1000000.0
MASKED = -1e30
MESH = pl.DeviceIdType.MESH
BF, F32 = jnp.bfloat16, jnp.float32


def rms_norm(values, gain_vec):
    return values * lax.rsqrt(jnp.mean(values * values, axis=-1, keepdims=True) + EPS) * gain_vec


def rotate(values, angles):
    half_width = values.shape[-1] // 2
    front_half = values[..., :half_width]
    back_half = values[..., half_width:]
    cos_part = jnp.cos(angles)
    sin_part = jnp.sin(angles)
    return jnp.concatenate(
        [
            front_half * cos_part - back_half * sin_part,
            back_half * cos_part + front_half * sin_part,
        ],
        axis=-1,
    )


def frequencies(head_size):
    return jnp.power(
        jnp.float32(ROPE_BASE), -2.0 * jnp.arange(head_size // 2, dtype=jnp.float32) / head_size
    )


def layout(lengths_row, total_len):
    count = lengths_row.shape[0]
    before = jnp.arange(count)[None, :] <= jnp.arange(count)[:, None]
    doc_ends = jnp.sum(jnp.where(before, lengths_row[None, :], 0), axis=1)
    starts = doc_ends - lengths_row
    indices = jnp.arange(total_len, dtype=jnp.int32)
    segment = jnp.sum((indices[:, None] >= doc_ends[None, :]).astype(jnp.int32), axis=1)
    onehot = segment[:, None] == jnp.arange(count, dtype=jnp.int32)[None, :]
    doc_begin = jnp.sum(jnp.where(onehot, starts[None, :], 0), axis=1)
    return (segment, indices - doc_begin)


def matmul(left_side, right_side):
    return jnp.dot(left_side, right_side, preferred_element_type=jnp.float32)


def times_transpose(left_side, right_side):
    return lax.dot_general(
        left_side, right_side, (((1,), (1,)), ((), ())), preferred_element_type=jnp.float32
    )


def transpose_times(left_side, right_side):
    return lax.dot_general(
        left_side, right_side, (((0,), (0,)), ((), ())), preferred_element_type=jnp.float32
    )


def gated(gate_proj, up_proj):
    return jax.nn.gelu(gate_proj, approximate=True) * up_proj


def gather_rows(shard):
    return lax.all_gather(shard, "fsdp", axis=0, tiled=True)


def reduce_rows(grad):
    low = grad.astype(jnp.bfloat16)
    own = lax.psum_scatter(low, "fsdp", scatter_dimension=0, tiled=True)
    return lax.psum(own, ("rep", "seq")).astype(jnp.float32)


def general(
    tokens,
    d_out,
    doc_lengths,
    w_query,
    w_key,
    w_value,
    w_out,
    w_gate,
    w_up,
    w_down,
    g_input,
    g_query,
    g_key,
    g_attn,
    g_ffin,
    g_ffout,
):
    shards = lax.axis_size("fsdp")
    gain_shards = (g_input, g_query, g_key, g_attn, g_ffin, g_ffout)
    widths = [entry.shape[0] for entry in gain_shards]
    starts = [sum(widths[:i]) for i in range(len(widths))]
    gain_rows = lax.all_gather(jnp.concatenate(gain_shards)[None], "fsdp", axis=0, tiled=True)
    gain_input, gain_query, gain_key, gain_attn, gain_ffin, gain_ffout = [
        gain_rows[:, at : at + width].reshape(-1).astype(jnp.float32)
        for at, width in zip(starts, widths)
    ]
    qkv_mat = gather_rows(jnp.concatenate([w_query, w_key, w_value], axis=1))
    out_mat = gather_rows(w_out)
    gate_up_mat = gather_rows(jnp.concatenate([w_gate, w_up], axis=1))
    down_mat = gather_rows(w_down)
    row_count = tokens.shape[1]
    head_size = gain_query.shape[0]
    query_width = w_query.shape[1]
    head_count = query_width // head_size
    ff_width = w_gate.shape[1]
    total_len = row_count * lax.axis_size("seq")
    segment, position = layout(doc_lengths[0], total_len)
    offset = lax.axis_index("seq") * row_count
    query_seg = lax.dynamic_slice_in_dim(segment, offset, row_count)
    query_pos = lax.dynamic_slice_in_dim(position, offset, row_count)
    places = offset + jnp.arange(row_count, dtype=jnp.int32)
    allowed = (query_seg[:, None] == segment[None, :]) & (
        places[:, None] >= jnp.arange(total_len, dtype=jnp.int32)[None, :]
    )
    angles = query_pos.astype(jnp.float32)[:, None] * frequencies(head_size)[None, :]
    scaling = head_size ** (-0.5)
    inputs = tokens[0].astype(jnp.float32)
    cotangent = d_out[0].astype(jnp.float32)
    input_norm, input_pull = jax.vjp(rms_norm, inputs, gain_input)
    attn_input = input_norm.astype(jnp.bfloat16)
    qkv_proj = matmul(attn_input, qkv_mat)
    q_proj = qkv_proj[:, :query_width]
    k_proj = qkv_proj[:, query_width : query_width + head_size]
    v_proj = qkv_proj[:, query_width + head_size :]

    def query_fn(projected, gain_vec):
        shaped = projected.reshape(projected.shape[0], -1, gain_vec.shape[0])
        return rotate(rms_norm(shaped, gain_vec), angles[:, None, :])

    def key_fn(projected, gain_vec):
        return rotate(rms_norm(projected, gain_vec), angles)

    queries, query_pull = jax.vjp(query_fn, q_proj, gain_query)
    keys_own, key_pull = jax.vjp(key_fn, k_proj, gain_key)
    query_rows = queries.astype(jnp.bfloat16).reshape(row_count * head_count, head_size)
    key_value_rows = lax.all_gather(
        jnp.concatenate([keys_own.astype(jnp.bfloat16), v_proj.astype(jnp.bfloat16)], axis=1),
        "seq",
        axis=0,
        tiled=True,
    )
    key_rows = key_value_rows[:, :head_size]
    value_rows = key_value_rows[:, head_size:]

    def masked_scores():
        raw_scores = times_transpose(query_rows, key_rows).reshape(row_count, head_count, total_len)
        return jnp.where(allowed[:, None, :], raw_scores * scaling, MASKED)

    scores = masked_scores()
    top_score = jnp.max(scores, axis=-1, keepdims=True)
    shifted = jnp.exp(scores - top_score)
    denominator = jnp.sum(shifted, axis=-1, keepdims=True)
    log_total = top_score + jnp.log(denominator)
    probs_low = (
        (shifted / denominator).astype(jnp.bfloat16).reshape(row_count * head_count, total_len)
    )
    mixed_rows = (
        matmul(probs_low, value_rows)
        .reshape(row_count, head_count * head_size)
        .astype(jnp.bfloat16)
    )
    out_proj = matmul(mixed_rows, out_mat)
    attn_norm, attn_pull = jax.vjp(rms_norm, out_proj, gain_attn)
    hidden_one = inputs + attn_norm
    ffin_norm, ffin_pull = jax.vjp(rms_norm, hidden_one, gain_ffin)
    ff_input = ffin_norm.astype(jnp.bfloat16)
    gate_up_proj = matmul(ff_input, gate_up_mat)
    gate_proj = gate_up_proj[:, :ff_width]
    up_proj = gate_up_proj[:, ff_width:]
    activated, gated_pull = jax.vjp(gated, gate_proj, up_proj)
    hidden = activated.astype(jnp.bfloat16)
    down_proj = matmul(hidden, down_mat)
    ffout_norm, ffout_pull = jax.vjp(rms_norm, down_proj, gain_ffout)
    result = hidden_one + ffout_norm
    d_down, grad_gffout = ffout_pull(cotangent)
    d_down_low = d_down.astype(jnp.bfloat16)
    total_down = reduce_rows(transpose_times(hidden, d_down_low))
    d_hidden = times_transpose(d_down_low, down_mat)
    d_gate, d_up = gated_pull(d_hidden)
    d_gate_up_low = jnp.concatenate(
        [d_gate.astype(jnp.bfloat16), d_up.astype(jnp.bfloat16)], axis=1
    )
    total_gate_up = reduce_rows(transpose_times(ff_input, d_gate_up_low))
    d_ffin = times_transpose(d_gate_up_low, gate_up_mat)
    d_hidden_part, grad_gffin = ffin_pull(d_ffin)
    d_hidden_one = cotangent + d_hidden_part
    d_out_proj, grad_gattn = attn_pull(d_hidden_one)
    d_out_low = d_out_proj.astype(jnp.bfloat16)
    total_out = reduce_rows(transpose_times(mixed_rows, d_out_low))
    d_mixed = (
        times_transpose(d_out_low, out_mat)
        .astype(jnp.bfloat16)
        .reshape(row_count * head_count, head_size)
    )
    probs_full = jnp.exp(masked_scores() - log_total)
    d_probs = times_transpose(d_mixed, value_rows).reshape(row_count, head_count, total_len)
    row_dot = jnp.sum(probs_full * d_probs, axis=-1, keepdims=True)
    d_raw = (
        (probs_full * (d_probs - row_dot) * scaling)
        .astype(jnp.bfloat16)
        .reshape(row_count * head_count, total_len)
    )
    grad_rows = jnp.concatenate(
        [
            transpose_times(d_raw, query_rows).astype(jnp.bfloat16),
            transpose_times(probs_low, d_mixed).astype(jnp.bfloat16),
        ],
        axis=1,
    )
    d_queries = matmul(d_raw, key_rows).reshape(row_count, head_count, head_size)
    grad_own = lax.psum_scatter(grad_rows, "seq", scatter_dimension=0, tiled=True).astype(
        jnp.float32
    )
    d_q_proj, grad_gquery = query_pull(d_queries)
    d_k_proj, grad_gkey = key_pull(grad_own[:, :head_size])
    d_qkv_low = jnp.concatenate(
        [
            d_q_proj.astype(jnp.bfloat16),
            d_k_proj.astype(jnp.bfloat16),
            grad_own[:, head_size:].astype(jnp.bfloat16),
        ],
        axis=1,
    )
    grad_qkv = transpose_times(attn_input, d_qkv_low)
    d_attn_input = times_transpose(d_qkv_low, qkv_mat)
    d_inputs_part, grad_ginput = input_pull(d_attn_input)
    d_inputs = d_hidden_one + d_inputs_part
    grad_gains = (grad_ginput, grad_gquery, grad_gkey, grad_gattn, grad_gffin, grad_gffout)
    packed_gains = jnp.concatenate([entry.reshape(shards, -1) for entry in grad_gains], axis=1)
    total_qkv = reduce_rows(grad_qkv)
    total_gains = lax.psum_scatter(
        packed_gains.astype(jnp.bfloat16), "fsdp", scatter_dimension=0, tiled=True
    )
    total_gains = lax.psum(total_gains, ("rep", "seq")).astype(jnp.float32)[0]
    return (
        result.astype(jnp.bfloat16)[None],
        d_inputs.astype(jnp.bfloat16)[None],
        total_qkv[:, :query_width],
        total_qkv[:, query_width : query_width + head_size],
        total_qkv[:, query_width + head_size :],
        total_out,
        total_gate_up[:, :ff_width],
        total_gate_up[:, ff_width:],
        total_down,
    ) + tuple(total_gains[at : at + width] for at, width in zip(starts, widths))


def dot(left_side, right_side):
    return jnp.dot(left_side, right_side, preferred_element_type=F32)


def dot_nt(left_side, right_side):
    return lax.dot_general(
        left_side, right_side, (((1,), (1,)), ((), ())), preferred_element_type=F32
    )


def loop(count, step):
    lax.fori_loop(0, count, lambda i, carry: (step(i), carry)[1], 0)


def at_block(i, size):
    return pl.ds(pl.multiple_of(i * size, size), size)


def inverse_rms(values):
    return lax.rsqrt(jnp.mean(values * values, axis=-1, keepdims=True) + EPS)


def rms_pull(values, gain_row, grad):
    inv = inverse_rms(values)
    scaled = values * inv
    pulled = grad * gain_row
    along = jnp.mean(pulled * scaled, axis=-1, keepdims=True)
    return inv * (pulled - scaled * along), jnp.sum(grad * scaled, axis=0, keepdims=True)


def turn(values, cos_part, sin_part):
    half_width = values.shape[-1] // 2
    front, back = values[:, :half_width], values[:, half_width:]
    return jnp.concatenate(
        [front * cos_part - back * sin_part, back * cos_part + front * sin_part], axis=1
    )


class Plan:
    def __init__(self, rows, width, heads, head, ff):
        self.rows, self.width, self.heads, self.head, self.ff = rows, width, heads, head, ff
        self.half = width // 2
        block = self.half // 4
        sizes = (
            ff * width // (32 * 128),
            self.half * ff // (16 * 128),
            self.half * ff // (16 * 128),
            heads * head * width // (32 * 128),
            block * head // 128,
            block + 16,
        )
        starts = [sum(sizes[:i]) for i in range(len(sizes))]
        self.chunks = tuple(zip(starts, sizes))
        self.block = block
        self.total = sum(sizes)
        self.gains_at = self.total - 16
        self.tiles = width // 128


WEIGHT_AXES = ("y", "z", "z", "y", "z")


def layer_kernel(plan, doc, freq, gain_in, tok, dout, *refs):
    (wq, wk, wv, wo, wg, wu, wd, res_out, dtok_out, flat_out) = refs[:10]
    (qkv_mat, out_mat, gate_mat, up_mat, down_mat, gain_far, attn_in, attn_in_t, qkv_f, queries, kv, keys_t) = refs[10:22]
    (values_t, probs, mixed, out_f, h1, ff_in, ff_in_t, gate_f, up_f, hidden, down_f, d_down, d_h1) = refs[22:35]
    (d_outp, d_mixed, dkv_f, dkv, dkv_c, dkv_y, d_qkv, cos_t, sin_t, scores, d_raw, gain_acc, gain_rows) = refs[35:48]
    (grads, from_c, from_x, from_y, from_z1, from_z2) = refs[48:54]
    (w_local, wx_s, wx_r, wf_s, wf_r, kv_s, kv_r, dk_s, dk_r, gs_, gr_, rs_s, rs_r, fin, free) = refs[54:69]
    rows, width, heads, head, ff = plan.rows, plan.width, plan.heads, plan.head, plan.ff
    half, block = plan.half, plan.block
    rep, x, s = lax.axis_index("rep"), lax.axis_index("fsdp"), lax.axis_index("seq")
    y, c = s // 2, s % 2
    zh, zl = rep // 2, rep % 2
    to = {
        "x": (rep, 1 - x, s),
        "c": (rep, x, y * 2 + 1 - c),
        "y": (rep, x, (1 - y) * 2 + c),
        "z": (zh * 2 + 1 - zl, x, s),
        "zz": ((1 - zh) * 2 + zl, x, s),
    }
    sends = []

    def send(source, target, send_sem, recv_sem, axis):
        copy = pltpu.make_async_remote_copy(
            src_ref=source,
            dst_ref=target,
            send_sem=send_sem,
            recv_sem=recv_sem,
            device_id=to[axis],
            device_id_type=MESH,
        )
        copy.start()
        sends.append(copy)
        return copy

    parts = (
        ((wq, 0), (wk, heads * head), (wv, heads * head + head)),
        ((wo, 0),),
        ((wg, 0),),
        ((wu, 0),),
        ((wd, 0),),
    )
    mats = (qkv_mat, out_mat, gate_mat, up_mat, down_mat)
    locals_of, x_of, f_of = {}, {}, {}
    slot = 0
    slots = []
    for i, (mat, entries) in enumerate(zip(mats, parts)):
        shard_rows = mat.shape[0] // 2
        slots.append(slot)
        locals_of[i] = []
        for ref, col in entries:
            copy = pltpu.make_async_copy(
                ref, mat.at[pl.ds(x * shard_rows, shard_rows), pl.ds(col, ref.shape[1])], w_local.at[slot]
            )
            copy.start()
            locals_of[i].append(copy)
            slot += 1

    barrier = pltpu.get_barrier_semaphore()
    for axis in to:
        pl.semaphore_signal(barrier, inc=1, device_id=to[axis], device_id_type=MESH)
    pl.semaphore_wait(barrier, len(to))

    def quarter_of(i, other):
        bit = y if WEIGHT_AXES[i] == "y" else zl
        return (1 - bit if other else bit) * 2 + c

    def weight_x(i):
        shard_rows = mats[i].shape[0] // 2
        size = shard_rows // 4
        at = quarter_of(i, False) * size
        x_of[i] = []
        for j, (ref, col) in enumerate(parts[i]):
            x_of[i].append(
                send(
                    ref.at[pl.ds(at, size)],
                    mats[i].at[pl.ds(x * shard_rows + at, size), pl.ds(col, ref.shape[1])],
                    wx_s.at[slots[i] + j],
                    wx_r.at[slots[i] + j],
                    "x",
                )
            )

    def weight_forward(i, hop, other, axis):
        shard_rows = mats[i].shape[0] // 2
        size = shard_rows // 4
        where = mats[i].at[pl.ds((1 - x) * shard_rows + quarter_of(i, other) * size, size)]
        f_of[i, hop] = send(where, where, wf_s.at[i, hop], wf_r.at[i, hop], axis)

    def weight_a(i):
        for copy in x_of[i]:
            copy.wait_recv()
        weight_forward(i, 0, False, WEIGHT_AXES[i])
        weight_forward(i, 1, False, "c")

    def weight_b(i):
        f_of[i, 0].wait_recv()
        weight_forward(i, 2, True, "c")

    def weight_done(i):
        f_of[i, 1].wait_recv()
        f_of[i, 2].wait_recv()
        for copy in locals_of[i]:
            copy.wait()

    mine_c, mine_y = c * 8, c * 8 + y * 4
    gathered = from_c.at[1 - x]
    piece_of = lambda high, low: mine_y + 2 * high + low
    hops = {}

    def hop(k, n, source, target, axis):
        hops[k, n] = send(source, target, rs_s.at[k, n], rs_r.at[k, n], axis)

    def span(k):
        return pl.ds(*plan.chunks[k])

    def total_of(k, place, at_y=None, at_z1=None, last=False):
        r = span(k)
        value = grads[x, mine_c + place, r, :].astype(F32) + from_c[x, place, r, :].astype(F32)
        value = value + from_x[place, r, :].astype(F32)
        if at_y is not None:
            value = value + from_y[at_y, r, :].astype(F32)
        if at_z1 is not None:
            value = value + from_z1[at_z1, r, :].astype(F32)
        if last:
            gathered[place, r, :] = (value + from_z2[r, :].astype(F32)).astype(BF)
        else:
            grads[x, mine_c + place, r, :] = value.astype(BF)

    def sum_c(k):
        r = span(k)
        hop(k, 0, grads.at[:, pl.ds((1 - c) * 8, 8), r], from_c.at[:, :, r], "c")

    def sum_x(k):
        r = span(k)
        hops[k, 0].wait_recv()

        def add(i):
            value = grads[1 - x, mine_c + i, r, :].astype(F32) + from_c[1 - x, i, r, :].astype(F32)
            grads[1 - x, mine_c + i, r, :] = value.astype(BF)

        loop(8, add)
        hop(k, 1, grads.at[1 - x, pl.ds(mine_c, 8), r], from_x.at[:, r], "x")

    def sum_y(k):
        r = span(k)
        hops[k, 1].wait_recv()
        hops[k, 0].wait_send()
        pl.semaphore_signal(free.at[k], inc=1, device_id=to["c"], device_id_type=MESH)
        loop(4, lambda i: total_of(k, (1 - y) * 4 + i))
        hop(k, 2, grads.at[x, pl.ds(mine_c + (1 - y) * 4, 4), r], from_y.at[:, r], "y")

    def sum_z1(k):
        r = span(k)
        hops[k, 2].wait_recv()
        loop(2, lambda i: total_of(k, y * 4 + 2 * i + 1 - zl, at_y=2 * i + 1 - zl))
        for i in range(2):
            hop(k, 3 + i, grads.at[x, piece_of(i, 1 - zl), r], from_z1.at[i, r], "z")

    def sum_z2(k):
        r = span(k)
        hops[k, 3].wait_recv()
        hops[k, 4].wait_recv()
        far = 2 * (1 - zh) + zl
        total_of(k, y * 4 + far, at_y=far, at_z1=1 - zh)
        hop(k, 5, grads.at[x, piece_of(1 - zh, zl), r], from_z2.at[r], "zz")

    def back_z2(k):
        r = span(k)
        hops[k, 5].wait_recv()
        near = 2 * zh + zl
        total_of(k, y * 4 + near, at_y=near, at_z1=zh, last=True)
        where = gathered.at[near + y * 4, r]
        hop(k, 6, where, where, "zz")

    def back_z1(k):
        hops[k, 6].wait_recv()
        for i in range(2):
            where = gathered.at[y * 4 + 2 * i + zl, span(k)]
            hop(k, 7 + i, where, where, "z")

    def back_y(k):
        hops[k, 7].wait_recv()
        hops[k, 8].wait_recv()
        where = gathered.at[pl.ds(y * 4, 4), span(k)]
        hop(k, 9, where, where, "y")
        pl.semaphore_wait(free.at[k], 1)
        hop(k, 10, where, grads.at[x, pl.ds(mine_c + y * 4, 4), span(k)], "c")

    def back_c(k):
        hops[k, 9].wait_recv()
        where = gathered.at[pl.ds((1 - y) * 4, 4), span(k)]
        hop(k, 11, where, grads.at[x, pl.ds(mine_c + (1 - y) * 4, 4), span(k)], "c")

    outs = []

    def finish(k):
        hops[k, 10].wait_recv()
        hops[k, 11].wait_recv()
        r = span(k)
        for i, source, first in ((0, gathered, mine_c), (1, grads.at[x, pl.ds((1 - c) * 8, 8)], (1 - c) * 8)):
            copy = pltpu.make_async_copy(source.at[:, r], flat_out.at[pl.ds(first, 8), r], fin.at[k, i])
            copy.start()
            outs.append(copy)

    steps = (sum_c, sum_x, sum_y, sum_z1, sum_z2, back_z2, back_z1, back_y, back_c, finish)
    done = [0] * len(plan.chunks)

    def advance(*pairs):
        for k, upto in pairs:
            while done[k] < upto:
                steps[done[k]](k)
                done[k] += 1

    gain_copy = send(gain_in, gain_far, gs_.at[0], gr_.at[0], "x")
    weight_x(0)
    weight_x(1)
    ends = [doc[0, 0]]
    for i in range(1, doc.shape[1]):
        ends.append(ends[-1] + doc[0, i])

    def start_of(places):
        start = jnp.zeros_like(places)
        for i, end in enumerate(ends):
            start = jnp.where(places >= end, end, start)
        return start

    place_col = s * rows + lax.broadcasted_iota(jnp.int32, (rows, 128), 0)
    angles = (place_col - start_of(place_col)).astype(F32) * freq[...]
    cos_t[...] = jnp.cos(angles)
    sin_t[...] = jnp.sin(angles)
    place_row = s * rows + lax.broadcasted_iota(jnp.int32, (1, rows), 1)
    start_row = start_of(place_row)
    grads_zero = jnp.zeros((16, 128), BF)
    for h in range(2):
        for p in range(2, 16):
            grads[h, p, plan.gains_at : plan.gains_at + 16, :] = grads_zero
    gain_rows[...] = jnp.zeros_like(gain_rows)
    gain_acc[...] = jnp.zeros_like(gain_acc)
    dkv_f[...] = jnp.zeros_like(dkv_f)

    gain_copy.wait_recv()
    gain = lambda i, size: gain_in[i : i + 1, 0:size] + gain_far[i : i + 1, 0:size]

    def by_rows(size, step):
        loop(rows // size, lambda i: step(pl.ds(pl.multiple_of(i * size, size), size)))

    def norm_in(r):
        v = tok[r, :].astype(F32)
        attn_in[r, :] = (v * inverse_rms(v) * gain(0, width)).astype(BF)

    by_rows(64, norm_in)
    attn_in_t[...] = attn_in[...].T
    weight_a(0)
    weight_x(2)
    weight_b(0)
    weight_a(1)
    weight_x(3)
    weight_done(0)

    def project(j):
        qkv_f[j] = dot(attn_in[...], qkv_mat[:, at_block(j, head)])

    project(heads)
    project(heads + 1)
    k_f = qkv_f[heads]
    kv[s, :, 0:head] = turn(k_f * inverse_rms(k_f) * gain(2, head), cos_t[...], sin_t[...]).astype(BF)
    kv[s, :, head : 2 * head] = qkv_f[heads + 1].astype(BF)
    kv_y = send(kv.at[s], kv.at[s], kv_s.at[0], kv_r.at[0], "y")
    kv_c = send(kv.at[s], kv.at[s], kv_s.at[1], kv_r.at[1], "c")
    loop(heads, project)

    def turn_query(h):
        q_f = qkv_f[h]
        queries[h] = turn(q_f * inverse_rms(q_f) * gain(1, head), cos_t[...], sin_t[...]).astype(BF)

    loop(heads, turn_query)
    weight_b(1)
    weight_a(2)
    weight_x(4)
    kv_y.wait_recv()
    far_kv = kv.at[(1 - y) * 2 + c]
    kv_cc = send(far_kv, far_kv, kv_s.at[2], kv_r.at[2], "c")
    kv_c.wait_recv()
    kv_cc.wait_recv()
    blocks = 4
    total_len = blocks * rows

    def transpose_kv(i):
        keys_t[:, at_block(i, rows)] = kv[i, :, 0:head].T
        values_t[:, at_block(i, rows)] = kv[i, :, head : 2 * head].T

    loop(blocks, transpose_kv)
    scaling = head ** (-0.5)

    def attend(h):
        q = queries[h]
        top = jnp.full((1, rows), MASKED, F32)
        for i in range(blocks):
            u = i * rows + lax.broadcasted_iota(jnp.int32, (rows, rows), 0)
            raw = dot_nt(kv[i, :, 0:head], q) * scaling
            raw = jnp.where((u <= place_row) & (u >= start_row), raw, MASKED)
            scores[i] = raw
            top = jnp.maximum(top, jnp.max(raw, axis=0, keepdims=True))
        denominator = jnp.zeros((1, rows), F32)
        for i in range(blocks):
            e = jnp.exp(scores[i] - top)
            scores[i] = e
            denominator = denominator + jnp.sum(e, axis=0, keepdims=True)
        inv = 1.0 / denominator
        for i in range(blocks):
            probs[h, i * rows : (i + 1) * rows, :] = (scores[i] * inv).astype(BF)
        mixed[:, at_block(h, head)] = dot(values_t[...], probs[h]).T.astype(BF)

    loop(heads // 2, attend)
    weight_b(2)
    weight_a(3)
    loop(heads // 2, lambda h: attend(h + heads // 2))
    weight_done(1)
    out_f[...] = dot(mixed[...], out_mat[...])

    def norm_ff(r):
        o = out_f[r, :]
        h = tok[r, :].astype(F32) + o * inverse_rms(o) * gain(3, width)
        h1[r, :] = h
        ff_in[r, :] = (h * inverse_rms(h) * gain(4, width)).astype(BF)

    by_rows(64, norm_ff)
    ff_in_t[...] = ff_in[...].T
    weight_b(3)
    weight_a(4)
    weight_done(2)
    weight_done(3)
    root = 0.7978845608028654

    def feed(j):
        g = dot(ff_in[...], gate_mat[:, at_block(j, head)])
        u = dot(ff_in[...], up_mat[:, at_block(j, head)])
        gate_f[j] = g
        up_f[j] = u
        t = jnp.tanh(root * (g + 0.044715 * (g * g * g)))
        hidden[:, at_block(j, head)] = (0.5 * g * (1.0 + t) * u).astype(BF)

    tiles_ff = ff // head
    loop(tiles_ff, feed)
    weight_b(4)
    weight_done(4)
    down_f[...] = dot(hidden[...], down_mat[...])

    def gain_add(i, size, row):
        gain_acc[i : i + 1, 0:size] = gain_acc[i : i + 1, 0:size] + row

    def norm_out(r):
        d = down_f[r, :]
        res_out[r, :] = (h1[r, :] + d * inverse_rms(d) * gain(5, width)).astype(BF)
        pulled, g_row = rms_pull(d, gain(5, width), dout[r, :].astype(F32))
        d_down[r, :] = pulled.astype(BF)
        gain_add(5, width, g_row)

    by_rows(64, norm_out)
    tiles = plan.tiles
    at_down, at_gate, at_up, at_out, at_q, at_kv = (start for start, _ in plan.chunks)

    def grad_down(j):
        value = dot(hidden[:, at_block(j, head)].T, d_down[...]).astype(BF)
        high, low = j // (tiles_ff // 2), j % (tiles_ff // 2)
        size = ff // 32
        for i in range(head // size):
            for t in range(tiles):
                grads[high, low * (head // size) + i, at_down + size * t : at_down + size * (t + 1), :] = value[
                    size * i : size * (i + 1), 128 * t : 128 * (t + 1)
                ]

    loop(tiles_ff, grad_down)
    advance((0, 1))

    def feed_back(j):
        d_hidden = dot_nt(d_down[...], down_mat[at_block(j, head), :])
        g, u = gate_f[j], up_f[j]
        t = jnp.tanh(root * (g + 0.044715 * (g * g * g)))
        act = 0.5 * g * (1.0 + t)
        slope = 0.5 * (1.0 + t) + 0.5 * g * (1.0 - t * t) * (root * (1.0 + 3 * 0.044715 * (g * g)))
        d_gate = (d_hidden * u * slope).astype(BF)
        d_up = (d_hidden * act).astype(BF)
        for at, value in ((at_gate, d_gate), (at_up, d_up)):
            full = dot(ff_in_t[...], value).astype(BF)
            for h in range(2):
                for t_ in range(2):
                    grads[h, 2 * j + t_, at : at + half, :] = full[half * h : half * (h + 1), 128 * t_ : 128 * (t_ + 1)]
        more = dot_nt(d_gate, gate_mat[:, at_block(j, head)]) + dot_nt(d_up, up_mat[:, at_block(j, head)])
        down_f[...] = down_f[...] + more

    down_f[...] = jnp.zeros_like(down_f)
    loop(tiles_ff // 2, feed_back)
    advance((0, 2))
    loop(tiles_ff // 2, lambda j: feed_back(j + tiles_ff // 2))
    advance((1, 1), (2, 1))

    def norm_mid(r):
        pulled, g_row = rms_pull(h1[r, :], gain(4, width), down_f[r, :])
        gain_add(4, width, g_row)
        d_mid = dout[r, :].astype(F32) + pulled
        d_h1[r, :] = d_mid
        pulled, g_row = rms_pull(out_f[r, :], gain(3, width), d_mid)
        gain_add(3, width, g_row)
        d_outp[r, :] = pulled.astype(BF)

    by_rows(64, norm_mid)

    def grad_out(j):
        value = dot(mixed[:, at_block(j, head)].T, d_outp[...]).astype(BF)
        size = heads * head // 32
        high, low = j // (heads // 2), j % (heads // 2)
        for i in range(head // size):
            for t in range(tiles):
                grads[high, low * (head // size) + i, at_out + size * t : at_out + size * (t + 1), :] = value[
                    size * i : size * (i + 1), 128 * t : 128 * (t + 1)
                ]
        d_mixed[j] = dot_nt(d_outp[...], out_mat[at_block(j, head), :]).astype(BF)

    loop(heads, grad_out)
    advance((1, 2), (2, 2), (3, 1))

    def attend_back(h):
        dm = d_mixed[h]
        along = jnp.zeros((1, rows), F32)
        for i in range(blocks):
            d_probs = dot_nt(kv[i, :, head : 2 * head], dm)
            scores[i] = d_probs
            p = probs[h, i * rows : (i + 1) * rows, :].astype(F32)
            along = along + jnp.sum(p * d_probs, axis=0, keepdims=True)
        for i in range(blocks):
            low = probs[h, i * rows : (i + 1) * rows, :]
            ds = (low.astype(F32) * (scores[i] - along) * scaling).astype(BF)
            d_raw[i * rows : (i + 1) * rows, :] = ds
            r = slice(i * rows, (i + 1) * rows)
            dkv_f[r, 0:head] = dkv_f[r, 0:head] + dot(ds, queries[h])
            dkv_f[r, head : 2 * head] = dkv_f[r, head : 2 * head] + dot(low, dm)
        dq = dot(keys_t[...], d_raw[...]).T
        turned = turn(dq, cos_t[...], -sin_t[...])
        pulled, g_row = rms_pull(qkv_f[h], gain(1, head), turned)
        gain_add(1, head, g_row)
        d_qkv[:, at_block(h, head)] = pulled.astype(BF)

    loop(heads // 2, attend_back)
    advance((3, 2), (0, 3))
    loop(heads // 2, lambda h: attend_back(h + heads // 2))
    for i in range(blocks):
        dkv[i] = dkv_f[i * rows : (i + 1) * rows, :].astype(BF)
    dk_c = [
        send(dkv.at[2 * i + 1 - c], dkv_c.at[i], dk_s.at[i], dk_r.at[i], "c") for i in range(2)
    ]
    advance((0, 4))

    def grad_query(h):
        full = dot(attn_in_t[...], d_qkv[:, at_block(h, head)]).astype(BF)
        for n in range(2):
            for i in range(4):
                for t in range(2):
                    grads[n, 4 * h + i, at_q + block * t : at_q + block * (t + 1), :] = full[
                        half * n + block * i : half * n + block * (i + 1), 128 * t : 128 * (t + 1)
                    ]

    for copy in dk_c:
        copy.wait_recv()
    far = (1 - y) * 2 + c
    dkv[far] = (dkv[far].astype(F32) + dkv_c[1 - y].astype(F32)).astype(BF)
    dk_y = send(dkv.at[far], dkv_y, dk_s.at[2], dk_r.at[2], "y")
    loop(heads, grad_query)
    advance((4, 1), (0, 5), (1, 3), (4, 2), (0, 6))
    dk_y.wait_recv()
    d_own = dkv[s].astype(F32) + dkv_c[y].astype(F32) + dkv_y[...].astype(F32)
    turned = turn(d_own[:, 0:head], cos_t[...], -sin_t[...])
    pulled, g_row = rms_pull(qkv_f[heads], gain(2, head), turned)
    gain_add(2, head, g_row)
    wide = heads * head
    d_qkv[:, wide : wide + head] = pulled.astype(BF)
    d_qkv[:, wide + head : wide + 2 * head] = d_own[:, head : 2 * head].astype(BF)
    full = dot(attn_in_t[...], d_qkv[:, wide : wide + 2 * head]).astype(BF)
    for n in range(2):
        for j in range(4):
            for i in range(4):
                grads[n, 4 * j + i, at_kv : at_kv + block, :] = full[
                    half * n + block * i : half * n + block * (i + 1), 128 * j : 128 * (j + 1)
                ]
    down_f[...] = dot_nt(d_qkv[...], qkv_mat[...])

    def norm_first(r):
        pulled, g_row = rms_pull(tok[r, :].astype(F32), gain(0, width), down_f[r, :])
        gain_add(0, width, g_row)
        dtok_out[r, :] = (d_h1[r, :] + pulled).astype(BF)

    by_rows(64, norm_first)
    for i in range(6):
        for t in range(tiles):
            gain_rows[i * tiles + t : i * tiles + t + 1, :] = gain_acc[i : i + 1, 128 * t : 128 * (t + 1)]
    for p in range(2):
        low = gain_rows[16 * p : 16 * (p + 1), :].astype(BF)
        for h in range(2):
            grads[h, p, plan.gains_at : plan.gains_at + 16, :] = low
    advance((5, 1), (5, 2))
    order = sorted(
        ((k, n) for k in range(6) for n in range(1, 11)), key=lambda e: (2 * e[0] + e[1], e[0])
    )
    advance(*order)
    for copy in sends:
        if not any(copy is hops[k, 0] for k in range(6)):
            copy.wait_send()
    for copy in outs:
        copy.wait()


def spread_kernel(plan, flat, res, dtok, *refs):
    (res_o, dtok_o, q_o, k_o, v_o, o_o, g_o, u_o, d_o, gin, gq, gk, ga, gf, go, rows_f, gains_f) = refs
    p = pl.program_id(0)
    at_down, at_gate, at_up, at_out, at_q, at_kv = (start for start, _ in plan.chunks)
    half, block, head, tiles = plan.half, plan.block, plan.head, plan.tiles
    size = plan.ff // 32
    for t in range(tiles):
        d_o[:, 128 * t : 128 * (t + 1)] = flat[0, at_down + size * t : at_down + size * (t + 1), :].astype(F32)
    g_o[...] = flat[0, at_gate : at_gate + half, :].astype(F32)
    u_o[...] = flat[0, at_up : at_up + half, :].astype(F32)
    size = plan.heads * head // 32
    for t in range(tiles):
        o_o[:, 128 * t : 128 * (t + 1)] = flat[0, at_out + size * t : at_out + size * (t + 1), :].astype(F32)
    for t in range(2):
        q_o[:, 128 * t : 128 * (t + 1)] = flat[0, at_q + block * t : at_q + block * (t + 1), :].astype(F32)
    for j in range(4):
        for i in range(4):

            @pl.when(p == 4 * j + i)
            def _():
                ref = (k_o, v_o)[j // 2]
                ref[block * i : block * (i + 1), 128 * (j % 2) : 128 * (j % 2 + 1)] = flat[
                    0, at_kv : at_kv + block, :
                ].astype(F32)

    @pl.when(p == 0)
    def _():
        res_o[...] = res[...]
        dtok_o[...] = dtok[...]
        rows_f[0:16, :] = flat[0, plan.gains_at : plan.gains_at + 16, :].astype(F32)

    @pl.when(p == 1)
    def _():
        rows_f[16:32, :] = flat[0, plan.gains_at : plan.gains_at + 16, :].astype(F32)
        gains_f[...] = jnp.zeros_like(gains_f)
        for i in range(6):
            for t in range(tiles):
                gains_f[i : i + 1, 128 * t : 128 * (t + 1)] = rows_f[i * tiles + t : i * tiles + t + 1, :]
        first = lax.axis_index("fsdp") == 0
        values = gains_f[...]
        own = jnp.where(first, values, pltpu.roll(values, half, 1))
        for i, ref in ((0, gin), (3, ga), (4, gf), (5, go)):
            ref[...] = own[i : i + 1, 0:half]
        own = jnp.where(first, values[:, 0 : head // 2], values[:, head // 2 : head])
        gq[...] = own[1:2, :]
        gk[...] = own[2:3, :]


def fused(tokens, d_out, doc_lengths, *weights):
    w_query, w_key, w_value, w_out, w_gate, w_up, w_down = weights[:7]
    gains = weights[7:]
    rows, width = tokens.shape[1:]
    head = 2 * weights[8].shape[0]
    heads = w_query.shape[1] // head
    ff = w_gate.shape[1]
    plan = Plan(rows, width, heads, head, ff)
    x = lax.axis_index("fsdp")
    placed = []
    for entry in gains:
        entry = entry.astype(F32)
        none = jnp.zeros_like(entry)
        line = jnp.concatenate([jnp.where(x == 0, entry, none), jnp.where(x == 0, none, entry)])
        placed.append(jnp.pad(line, (0, width - line.shape[0])))
    placed = jnp.stack(placed + [jnp.zeros_like(placed[0])] * 2)
    freq = jnp.asarray(
        np.power(ROPE_BASE, -2.0 * np.arange(head // 2) / head).astype(np.float32)[None]
    )
    vmem, far = pl.BlockSpec(memory_space=pltpu.VMEM), pl.BlockSpec(memory_space=pl.ANY)
    scratch = lambda *shape: pltpu.VMEM(shape, BF)
    scratch32 = lambda *shape: pltpu.VMEM(shape, F32)
    wide = heads * head
    total, chunks = plan.total, len(plan.chunks)
    dma = lambda *shape: pltpu.SemaphoreType.DMA(shape)
    tiles_ff = ff // head
    scratch_shapes = [
        scratch(width, wide + 2 * head),
        scratch(wide, width),
        scratch(width, ff),
        scratch(width, ff),
        scratch(ff, width),
        scratch32(8, width),
        scratch(rows, width),
        scratch(width, rows),
        scratch32(heads + 2, rows, head),
        scratch(heads, rows, head),
        scratch(4, rows, 2 * head),
        scratch(head, 4 * rows),
        scratch(head, 4 * rows),
        scratch(heads, 4 * rows, rows),
        scratch(rows, wide),
        scratch32(rows, width),
        scratch32(rows, width),
        scratch(rows, width),
        scratch(width, rows),
        scratch32(tiles_ff, rows, head),
        scratch32(tiles_ff, rows, head),
        scratch(rows, ff),
        scratch32(rows, width),
        scratch(rows, width),
        scratch32(rows, width),
        scratch(rows, width),
        scratch(heads, rows, head),
        scratch32(4 * rows, 2 * head),
        scratch(4, rows, 2 * head),
        scratch(2, rows, 2 * head),
        scratch(rows, 2 * head),
        scratch(rows, wide + 2 * head),
        scratch32(rows, 128),
        scratch32(rows, 128),
        scratch32(4, rows, rows),
        scratch(4 * rows, rows),
        scratch32(8, width),
        scratch32(32, 128),
        scratch(2, 16, total, 128),
        scratch(2, 8, total, 128),
        scratch(8, total, 128),
        scratch(4, total, 128),
        scratch(2, total, 128),
        scratch(total, 128),
        dma(7),
        dma(7),
        dma(7),
        dma(5, 3),
        dma(5, 3),
        dma(3),
        dma(3),
        dma(3),
        dma(3),
        dma(1),
        dma(1),
        dma(chunks, 12),
        dma(chunks, 12),
        dma(chunks, 2),
        pltpu.SemaphoreType.REGULAR((chunks,)),
    ]
    result, d_tokens, flat = pl.pallas_call(
        functools.partial(layer_kernel, plan),
        out_shape=[
            jax.ShapeDtypeStruct((rows, width), BF),
            jax.ShapeDtypeStruct((rows, width), BF),
            jax.ShapeDtypeStruct((16, total, 128), BF),
        ],
        in_specs=[pl.BlockSpec(memory_space=pltpu.SMEM)] + [vmem] * 4 + [far] * 7,
        out_specs=[vmem, vmem, far],
        scratch_shapes=scratch_shapes,
        compiler_params=pltpu.CompilerParams(
            collective_id=0, has_side_effects=True, vmem_limit_bytes=58 * 2**20
        ),
        name="layer",
    )(doc_lengths, freq, placed, tokens[0], d_out[0], w_query, w_key, w_value, w_out, w_gate, w_up, w_down)
    half, block = plan.half, plan.block
    whole = lambda *shape: pl.BlockSpec(shape, lambda p: (0,) * len(shape))
    shape32 = lambda *shape: jax.ShapeDtypeStruct(shape, F32)
    outs = pl.pallas_call(
        functools.partial(spread_kernel, plan),
        grid=(16,),
        out_shape=[
            jax.ShapeDtypeStruct((rows, width), BF),
            jax.ShapeDtypeStruct((rows, width), BF),
            shape32(half, wide),
            shape32(half, head),
            shape32(half, head),
            shape32(wide // 2, width),
            shape32(half, ff),
            shape32(half, ff),
            shape32(ff // 2, width),
            shape32(1, half),
            shape32(1, head // 2),
            shape32(1, head // 2),
            shape32(1, half),
            shape32(1, half),
            shape32(1, half),
        ],
        in_specs=[
            pl.BlockSpec((1, total, 128), lambda p: (p, 0, 0)),
            whole(rows, width),
            whole(rows, width),
        ],
        out_specs=[
            whole(rows, width),
            whole(rows, width),
            pl.BlockSpec((block, head), lambda p: (p % 4, p // 4)),
            whole(half, head),
            whole(half, head),
            pl.BlockSpec((wide // 32, width), lambda p: (p, 0)),
            pl.BlockSpec((half, 128), lambda p: (0, p)),
            pl.BlockSpec((half, 128), lambda p: (0, p)),
            pl.BlockSpec((ff // 32, width), lambda p: (p, 0)),
            whole(1, half),
            whole(1, head // 2),
            whole(1, head // 2),
            whole(1, half),
            whole(1, half),
            whole(1, half),
        ],
        scratch_shapes=[scratch32(32, 128), scratch32(8, width)],
        name="spread",
    )(flat, result, d_tokens)
    return (outs[0][None], outs[1][None]) + tuple(outs[2:9]) + tuple(o[0] for o in outs[9:])


def solution(mesh):
    whole = mesh.shape
    small = whole["rep"] == 4 and whole["fsdp"] == 2 and whole["seq"] == 4
    body = fused if small else general
    in_specs = (
        P(("rep", "fsdp"), "seq", None),
        P(("rep", "fsdp"), "seq", None),
        P(("rep", "fsdp"), None),
        P("fsdp", None),
        P("fsdp", None),
        P("fsdp", None),
        P("fsdp", None),
        P("fsdp", None),
        P("fsdp", None),
        P("fsdp", None),
        P("fsdp"),
        P("fsdp"),
        P("fsdp"),
        P("fsdp"),
        P("fsdp"),
        P("fsdp"),
    )
    out_specs = (
        P(("rep", "fsdp"), "seq", None),
        P(("rep", "fsdp"), "seq", None),
        P("fsdp", None),
        P("fsdp", None),
        P("fsdp", None),
        P("fsdp", None),
        P("fsdp", None),
        P("fsdp", None),
        P("fsdp", None),
        P("fsdp"),
        P("fsdp"),
        P("fsdp"),
        P("fsdp"),
        P("fsdp"),
        P("fsdp"),
    )
    return jax.shard_map(body, mesh=mesh, in_specs=in_specs, out_specs=out_specs, check_vma=False)
```

```python
import functools

import jax
import jax.numpy as jnp
import numpy as np
from jax import lax
from jax.experimental import pallas as pl
from jax.experimental.pallas import tpu as pltpu
from jax.sharding import PartitionSpec as P

EPS = 1e-06
ROPE_BASE = 1000000.0
MASKED = -1e30
MESH = pl.DeviceIdType.MESH
BF, F32 = jnp.bfloat16, jnp.float32


def rms_norm(values, gain_vec):
    return values * lax.rsqrt(jnp.mean(values * values, axis=-1, keepdims=True) + EPS) * gain_vec


def rotate(values, angles):
    half_width = values.shape[-1] // 2
    front_half = values[..., :half_width]
    back_half = values[..., half_width:]
    cos_part = jnp.cos(angles)
    sin_part = jnp.sin(angles)
    return jnp.concatenate(
        [
            front_half * cos_part - back_half * sin_part,
            back_half * cos_part + front_half * sin_part,
        ],
        axis=-1,
    )


def frequencies(head_size):
    return jnp.power(
        jnp.float32(ROPE_BASE), -2.0 * jnp.arange(head_size // 2, dtype=jnp.float32) / head_size
    )


def layout(lengths_row, total_len):
    count = lengths_row.shape[0]
    before = jnp.arange(count)[None, :] <= jnp.arange(count)[:, None]
    doc_ends = jnp.sum(jnp.where(before, lengths_row[None, :], 0), axis=1)
    starts = doc_ends - lengths_row
    indices = jnp.arange(total_len, dtype=jnp.int32)
    segment = jnp.sum((indices[:, None] >= doc_ends[None, :]).astype(jnp.int32), axis=1)
    onehot = segment[:, None] == jnp.arange(count, dtype=jnp.int32)[None, :]
    doc_begin = jnp.sum(jnp.where(onehot, starts[None, :], 0), axis=1)
    return (segment, indices - doc_begin)


def matmul(left_side, right_side):
    return jnp.dot(left_side, right_side, preferred_element_type=jnp.float32)


def times_transpose(left_side, right_side):
    return lax.dot_general(
        left_side, right_side, (((1,), (1,)), ((), ())), preferred_element_type=jnp.float32
    )


def transpose_times(left_side, right_side):
    return lax.dot_general(
        left_side, right_side, (((0,), (0,)), ((), ())), preferred_element_type=jnp.float32
    )


def gated(gate_proj, up_proj):
    return jax.nn.gelu(gate_proj, approximate=True) * up_proj


def gather_rows(shard):
    return lax.all_gather(shard, "fsdp", axis=0, tiled=True)


def reduce_rows(grad):
    low = grad.astype(jnp.bfloat16)
    own = lax.psum_scatter(low, "fsdp", scatter_dimension=0, tiled=True)
    return lax.psum(own, ("rep", "seq")).astype(jnp.float32)


def general(
    tokens,
    d_out,
    doc_lengths,
    w_query,
    w_key,
    w_value,
    w_out,
    w_gate,
    w_up,
    w_down,
    g_input,
    g_query,
    g_key,
    g_attn,
    g_ffin,
    g_ffout,
):
    shards = lax.axis_size("fsdp")
    gain_shards = (g_input, g_query, g_key, g_attn, g_ffin, g_ffout)
    widths = [entry.shape[0] for entry in gain_shards]
    starts = [sum(widths[:i]) for i in range(len(widths))]
    gain_rows = lax.all_gather(jnp.concatenate(gain_shards)[None], "fsdp", axis=0, tiled=True)
    gain_input, gain_query, gain_key, gain_attn, gain_ffin, gain_ffout = [
        gain_rows[:, at : at + width].reshape(-1).astype(jnp.float32)
        for at, width in zip(starts, widths)
    ]
    qkv_mat = gather_rows(jnp.concatenate([w_query, w_key, w_value], axis=1))
    out_mat = gather_rows(w_out)
    gate_up_mat = gather_rows(jnp.concatenate([w_gate, w_up], axis=1))
    down_mat = gather_rows(w_down)
    row_count = tokens.shape[1]
    head_size = gain_query.shape[0]
    query_width = w_query.shape[1]
    head_count = query_width // head_size
    ff_width = w_gate.shape[1]
    total_len = row_count * lax.axis_size("seq")
    segment, position = layout(doc_lengths[0], total_len)
    offset = lax.axis_index("seq") * row_count
    query_seg = lax.dynamic_slice_in_dim(segment, offset, row_count)
    query_pos = lax.dynamic_slice_in_dim(position, offset, row_count)
    places = offset + jnp.arange(row_count, dtype=jnp.int32)
    allowed = (query_seg[:, None] == segment[None, :]) & (
        places[:, None] >= jnp.arange(total_len, dtype=jnp.int32)[None, :]
    )
    angles = query_pos.astype(jnp.float32)[:, None] * frequencies(head_size)[None, :]
    scaling = head_size ** (-0.5)
    inputs = tokens[0].astype(jnp.float32)
    cotangent = d_out[0].astype(jnp.float32)
    input_norm, input_pull = jax.vjp(rms_norm, inputs, gain_input)
    attn_input = input_norm.astype(jnp.bfloat16)
    qkv_proj = matmul(attn_input, qkv_mat)
    q_proj = qkv_proj[:, :query_width]
    k_proj = qkv_proj[:, query_width : query_width + head_size]
    v_proj = qkv_proj[:, query_width + head_size :]

    def query_fn(projected, gain_vec):
        shaped = projected.reshape(projected.shape[0], -1, gain_vec.shape[0])
        return rotate(rms_norm(shaped, gain_vec), angles[:, None, :])

    def key_fn(projected, gain_vec):
        return rotate(rms_norm(projected, gain_vec), angles)

    queries, query_pull = jax.vjp(query_fn, q_proj, gain_query)
    keys_own, key_pull = jax.vjp(key_fn, k_proj, gain_key)
    query_rows = queries.astype(jnp.bfloat16).reshape(row_count * head_count, head_size)
    key_value_rows = lax.all_gather(
        jnp.concatenate([keys_own.astype(jnp.bfloat16), v_proj.astype(jnp.bfloat16)], axis=1),
        "seq",
        axis=0,
        tiled=True,
    )
    key_rows = key_value_rows[:, :head_size]
    value_rows = key_value_rows[:, head_size:]

    def masked_scores():
        raw_scores = times_transpose(query_rows, key_rows).reshape(row_count, head_count, total_len)
        return jnp.where(allowed[:, None, :], raw_scores * scaling, MASKED)

    scores = masked_scores()
    top_score = jnp.max(scores, axis=-1, keepdims=True)
    shifted = jnp.exp(scores - top_score)
    denominator = jnp.sum(shifted, axis=-1, keepdims=True)
    log_total = top_score + jnp.log(denominator)
    probs_low = (
        (shifted / denominator).astype(jnp.bfloat16).reshape(row_count * head_count, total_len)
    )
    mixed_rows = (
        matmul(probs_low, value_rows)
        .reshape(row_count, head_count * head_size)
        .astype(jnp.bfloat16)
    )
    out_proj = matmul(mixed_rows, out_mat)
    attn_norm, attn_pull = jax.vjp(rms_norm, out_proj, gain_attn)
    hidden_one = inputs + attn_norm
    ffin_norm, ffin_pull = jax.vjp(rms_norm, hidden_one, gain_ffin)
    ff_input = ffin_norm.astype(jnp.bfloat16)
    gate_up_proj = matmul(ff_input, gate_up_mat)
    gate_proj = gate_up_proj[:, :ff_width]
    up_proj = gate_up_proj[:, ff_width:]
    activated, gated_pull = jax.vjp(gated, gate_proj, up_proj)
    hidden = activated.astype(jnp.bfloat16)
    down_proj = matmul(hidden, down_mat)
    ffout_norm, ffout_pull = jax.vjp(rms_norm, down_proj, gain_ffout)
    result = hidden_one + ffout_norm
    d_down, grad_gffout = ffout_pull(cotangent)
    d_down_low = d_down.astype(jnp.bfloat16)
    total_down = reduce_rows(transpose_times(hidden, d_down_low))
    d_hidden = times_transpose(d_down_low, down_mat)
    d_gate, d_up = gated_pull(d_hidden)
    d_gate_up_low = jnp.concatenate(
        [d_gate.astype(jnp.bfloat16), d_up.astype(jnp.bfloat16)], axis=1
    )
    total_gate_up = reduce_rows(transpose_times(ff_input, d_gate_up_low))
    d_ffin = times_transpose(d_gate_up_low, gate_up_mat)
    d_hidden_part, grad_gffin = ffin_pull(d_ffin)
    d_hidden_one = cotangent + d_hidden_part
    d_out_proj, grad_gattn = attn_pull(d_hidden_one)
    d_out_low = d_out_proj.astype(jnp.bfloat16)
    total_out = reduce_rows(transpose_times(mixed_rows, d_out_low))
    d_mixed = (
        times_transpose(d_out_low, out_mat)
        .astype(jnp.bfloat16)
        .reshape(row_count * head_count, head_size)
    )
    probs_full = jnp.exp(masked_scores() - log_total)
    d_probs = times_transpose(d_mixed, value_rows).reshape(row_count, head_count, total_len)
    row_dot = jnp.sum(probs_full * d_probs, axis=-1, keepdims=True)
    d_raw = (
        (probs_full * (d_probs - row_dot) * scaling)
        .astype(jnp.bfloat16)
        .reshape(row_count * head_count, total_len)
    )
    grad_rows = jnp.concatenate(
        [
            transpose_times(d_raw, query_rows).astype(jnp.bfloat16),
            transpose_times(probs_low, d_mixed).astype(jnp.bfloat16),
        ],
        axis=1,
    )
    d_queries = matmul(d_raw, key_rows).reshape(row_count, head_count, head_size)
    grad_own = lax.psum_scatter(grad_rows, "seq", scatter_dimension=0, tiled=True).astype(
        jnp.float32
    )
    d_q_proj, grad_gquery = query_pull(d_queries)
    d_k_proj, grad_gkey = key_pull(grad_own[:, :head_size])
    d_qkv_low = jnp.concatenate(
        [
            d_q_proj.astype(jnp.bfloat16),
            d_k_proj.astype(jnp.bfloat16),
            grad_own[:, head_size:].astype(jnp.bfloat16),
        ],
        axis=1,
    )
    grad_qkv = transpose_times(attn_input, d_qkv_low)
    d_attn_input = times_transpose(d_qkv_low, qkv_mat)
    d_inputs_part, grad_ginput = input_pull(d_attn_input)
    d_inputs = d_hidden_one + d_inputs_part
    grad_gains = (grad_ginput, grad_gquery, grad_gkey, grad_gattn, grad_gffin, grad_gffout)
    packed_gains = jnp.concatenate([entry.reshape(shards, -1) for entry in grad_gains], axis=1)
    total_qkv = reduce_rows(grad_qkv)
    total_gains = lax.psum_scatter(
        packed_gains.astype(jnp.bfloat16), "fsdp", scatter_dimension=0, tiled=True
    )
    total_gains = lax.psum(total_gains, ("rep", "seq")).astype(jnp.float32)[0]
    return (
        result.astype(jnp.bfloat16)[None],
        d_inputs.astype(jnp.bfloat16)[None],
        total_qkv[:, :query_width],
        total_qkv[:, query_width : query_width + head_size],
        total_qkv[:, query_width + head_size :],
        total_out,
        total_gate_up[:, :ff_width],
        total_gate_up[:, ff_width:],
        total_down,
    ) + tuple(total_gains[at : at + width] for at, width in zip(starts, widths))


def dot(left_side, right_side):
    return jnp.dot(left_side, right_side, preferred_element_type=F32)


def dot_nt(left_side, right_side):
    return lax.dot_general(
        left_side, right_side, (((1,), (1,)), ((), ())), preferred_element_type=F32
    )


def loop(count, step):
    lax.fori_loop(0, count, lambda i, carry: (step(i), carry)[1], 0)


def at_block(i, size):
    return pl.ds(pl.multiple_of(i * size, size), size)


def inverse_rms(values):
    return lax.rsqrt(jnp.mean(values * values, axis=-1, keepdims=True) + EPS)


def rms_pull(values, gain_row, grad):
    inv = inverse_rms(values)
    scaled = values * inv
    pulled = grad * gain_row
    along = jnp.mean(pulled * scaled, axis=-1, keepdims=True)
    return inv * (pulled - scaled * along), jnp.sum(grad * scaled, axis=0, keepdims=True)


def turn(values, cos_part, sin_part):
    half_width = values.shape[-1] // 2
    front, back = values[:, :half_width], values[:, half_width:]
    return jnp.concatenate(
        [front * cos_part - back * sin_part, back * cos_part + front * sin_part], axis=1
    )


class Plan:
    def __init__(self, rows, width, heads, head, ff):
        self.rows, self.width, self.heads, self.head, self.ff = rows, width, heads, head, ff
        self.half = width // 2
        block = self.half // 4
        sizes = (
            ff * width // (32 * 128),
            self.half * ff // (16 * 128),
            self.half * ff // (16 * 128),
            heads * head * width // (32 * 128),
            block * head // 128,
            block + 16,
        )
        self.starts = [sum(sizes[:i]) for i in range(len(sizes))]
        self.chunks = tuple(
            (start + size * a // 10, size * (b - a) // 10)
            for start, size, cuts in zip(self.starts, sizes, CUTS)
            for a, b in zip(cuts, cuts[1:])
        )
        self.block = block
        self.total = sum(sizes)
        self.gains_at = self.total - 16
        self.tiles = width // 128


CUTS = ((0, 2, 6, 10), (0, 5, 10), (0, 5, 10), (0, 10), (0, 10), (0, 10))
FIRST = tuple("yyxxxxxxxx")
WEIGHT_WAYS = (("z", None), ("y", "rows"), ("y", "columns"), ("y", "columns"), ("y", None))

SCHEDULE = (
    ("init",), ("wx", 1), ("norm",), ("wx", 2), ("wa", 0), ("wx", 3), ("wa", 1), ("wx", 4), ("wa", 2), ("wb", 1),
    ("wb", 0), ("wa", 3), ("wc", 1), ("kv",), ("q",), ("wb", 2), ("wc", 2), ("wd", 1), ("wb", 3), ("wa", 4),
    ("kvf", 0), ("wc", 3), ("keys",), ("at", 0), ("kvf", 1), ("wd", 2), ("at", 1), ("kvt",), ("outp",), ("wd", 3),
    ("wb", 4), ("ff", 0), ("ff", 1), ("down",), ("nout",), ("gd",), ("sum", 0, 0), ("sum", 1, 0), ("sum", 2, 0),
    ("fb", 0), ("sum", 0, 1), ("fb", 1), ("sum", 1, 1), ("sum", 2, 1), ("fb", 2), ("fb", 3), ("sum", 3, 0),
    ("sum", 4, 0), ("sum", 5, 0), ("sum", 6, 0), ("sum", 0, 2), ("mid",), ("gout",), ("sum", 7, 0), ("sum", 3, 1),
    ("sum", 2, 2), ("sum", 0, 3), ("sum", 1, 2), ("sum", 4, 1), ("ab", 0), ("sum", 5, 1), ("sum", 6, 1),
    ("sum", 0, 4), ("ab", 1), ("sum", 2, 3), ("sum", 7, 1), ("dks",), ("sum", 0, 5), ("gq",), ("sum", 8, 0),
    ("sum", 3, 2), ("dky",), ("sum", 1, 3), ("sum", 0, 6), ("sum", 2, 4), ("sum", 8, 1), ("sum", 0, 7), ("sum", 3, 3),
    ("sum", 1, 4), ("sum", 4, 2), ("sum", 2, 5), ("gkv",), ("last",), ("sum", 9, 0), ("sum", 3, 4), ("sum", 4, 3),
    ("sum", 5, 2), ("sum", 1, 5), ("sum", 9, 1), ("sum", 2, 6), ("sum", 2, 7), ("sum", 3, 5), ("sum", 5, 3),
    ("sum", 6, 2), ("sum", 4, 4), ("sum", 1, 6), ("sum", 1, 7), ("sum", 5, 4), ("sum", 3, 6), ("sum", 3, 7),
    ("sum", 7, 2), ("sum", 4, 5), ("sum", 6, 3), ("sum", 5, 5), ("sum", 7, 3), ("sum", 8, 2), ("sum", 6, 4),
    ("sum", 4, 6), ("sum", 9, 2), ("sum", 4, 7), ("sum", 7, 4), ("sum", 5, 6), ("sum", 5, 7), ("sum", 6, 5),
    ("sum", 8, 3), ("sum", 9, 3), ("sum", 7, 5), ("sum", 6, 6), ("sum", 8, 4), ("sum", 6, 7), ("sum", 9, 4),
    ("sum", 7, 6), ("sum", 7, 7), ("sum", 8, 5), ("sum", 9, 5), ("sum", 8, 6), ("sum", 8, 7), ("sum", 9, 6),
    ("sum", 9, 7),
)


def layer_kernel(plan, doc, freq, *refs):
    shards, refs = refs[:6], refs[6:]
    (tok, dout, wq, wk, wv, wo, wg, wu, wd, res_out, dtok_out, flat_out) = refs[:12]
    refs = refs[2:]
    (qkv_mat, out_mat, gate_mat, up_mat, down_mat, gain_own, gain_far, gain_full, attn_in, attn_in_t, qkv_f, queries, kv, keys_t) = refs[10:24]
    (values_t, probs, mixed, out_f, h1, ff_in, ff_in_t, gate_f, up_f, hidden, down_f, d_down, d_h1) = refs[24:37]
    (d_outp, d_mixed, dkv_f, dkv, dkv_c, dkv_y, d_qkv, cos_t, sin_t, scores, d_raw, gain_acc, gain_rows) = refs[37:50]
    (grads, from_c, from_1, from_2, from_z) = refs[50:55]
    (w_local, wx_s, wx_r, wf_s, wf_r, kv_s, kv_r, dk_s, dk_r, gs_, gr_, rs_s, rs_r, fin, free) = refs[55:70]
    rows, width, heads, head, ff = plan.rows, plan.width, plan.heads, plan.head, plan.ff
    half, block = plan.half, plan.block
    rep, x, s = lax.axis_index("rep"), lax.axis_index("fsdp"), lax.axis_index("seq")
    y, c = s // 2, s % 2
    zh, zl = rep // 2, rep % 2
    to = {
        "x": (rep, 1 - x, s),
        "c": (rep, x, y * 2 + 1 - c),
        "y": (rep, x, (1 - y) * 2 + c),
        "z": (zh * 2 + 1 - zl, x, s),
        "z2": ((1 - zh) * 2 + zl, x, s),
        "z3": ((1 - zh) * 2 + 1 - zl, x, s),
    }
    sends = []

    def send(source, target, send_sem, recv_sem, axis):
        copy = pltpu.make_async_remote_copy(
            src_ref=source,
            dst_ref=target,
            send_sem=send_sem,
            recv_sem=recv_sem,
            device_id=to[axis],
            device_id_type=MESH,
        )
        copy.start()
        sends.append(copy)
        return copy

    parts = (
        ((wq, 0), (wk, heads * head), (wv, heads * head + head)),
        ((wo, 0),),
        ((wg, 0),),
        ((wu, 0),),
        ((wd, 0),),
    )
    mats = (qkv_mat, out_mat, gate_mat, up_mat, down_mat)
    locals_of, x_of, f_of = {}, {}, {}
    slot = 0
    slots = []
    for i, (mat, entries) in enumerate(zip(mats, parts)):
        shard_rows = mat.shape[0] // 2
        slots.append(slot)
        locals_of[i] = []
        for ref, col in entries:
            copy = pltpu.make_async_copy(
                ref, mat.at[pl.ds(x * shard_rows, shard_rows), pl.ds(col, ref.shape[1])], w_local.at[slot]
            )
            copy.start()
            locals_of[i].append(copy)
            slot += 1

    barrier = pltpu.get_barrier_semaphore()
    for axis in to:
        pl.semaphore_signal(barrier, inc=1, device_id=to[axis], device_id_type=MESH)
    pl.semaphore_wait(barrier, len(to))

    def region(i, far_bit, far_z):
        axis, cut = WEIGHT_WAYS[i]
        bit = y if axis == "y" else zl
        quarter = (1 - bit if far_bit else bit) * 2 + c
        low = 1 - zl if far_z else zl
        size, columns = mats[i].shape[0] // 8, mats[i].shape[1]
        if cut == "rows":
            return quarter * size + low * (size // 2), size // 2, None
        if cut == "columns":
            half_columns = columns // 2
            return quarter * size, size, at_block(low, half_columns)
        return quarter * size, size, None

    def weight_x(i):
        shard_rows = mats[i].shape[0] // 2
        at, size, columns = region(i, False, False)
        x_of[i] = []
        for j, (ref, col) in enumerate(parts[i]):
            here = pl.ds(0, ref.shape[1]) if columns is None else columns
            there = pl.ds(col, ref.shape[1]) if columns is None else columns
            x_of[i].append(
                send(
                    ref.at[pl.ds(at, size), here],
                    mats[i].at[pl.ds(x * shard_rows + at, size), there],
                    wx_s.at[slots[i] + j],
                    wx_r.at[slots[i] + j],
                    "x",
                )
            )

    def weight_forward(i, n, axis, far_bit, far_z=False):
        shard_rows = mats[i].shape[0] // 2
        at, size, columns = region(i, far_bit, far_z)
        where = mats[i].at[pl.ds((1 - x) * shard_rows + at, size)]
        if columns is not None:
            where = mats[i].at[pl.ds((1 - x) * shard_rows + at, size), columns]
        f_of[i, n] = send(where, where, wf_s.at[i, n], wf_r.at[i, n], axis)

    def weight_a(i):
        for copy in x_of[i]:
            copy.wait_recv()
        weight_forward(i, 0, WEIGHT_WAYS[i][0], False)
        if WEIGHT_WAYS[i][1]:
            weight_forward(i, 3, "z", False)
        weight_forward(i, 1, "c", False)

    def weight_b(i):
        f_of[i, 0].wait_recv()
        if WEIGHT_WAYS[i][1]:
            weight_forward(i, 4, "z", True)
        weight_forward(i, 2, "c", True)

    def weight_c(i):
        f_of[i, 3].wait_recv()
        weight_forward(i, 5, "c", False, True)

    def weight_d(i):
        f_of[i, 4].wait_recv()
        weight_forward(i, 6, "c", True, True)

    def weight_done(i):
        for n in (1, 2, 5, 6) if WEIGHT_WAYS[i][1] else (1, 2):
            f_of[i, n].wait_recv()
        for copy in locals_of[i]:
            copy.wait()

    mine_c, mine_y = c * 8, c * 8 + y * 4
    gathered = from_c.at[1 - x]
    piece_of = lambda high, low: mine_y + 2 * high + low
    hops = {}

    def hop(k, n, source, target, axis):
        hops[k, n] = send(source, target, rs_s.at[k, n], rs_r.at[k, n], axis)

    def span(k):
        return pl.ds(*plan.chunks[k])

    def total_of(k, m, last=False):
        r = span(k)
        place = y * 4 + m
        value = grads[x, mine_c + place, r, :].astype(F32) + from_c[x, place, r, :].astype(F32)
        first = place if FIRST[k] == "x" else 4 * x + m
        value = value + from_1[first, r, :].astype(F32) + from_2[m, r, :].astype(F32)
        if last:
            for i in range(3):
                value = value + from_z[i, r, :].astype(F32)
            gathered[place, r, :] = value.astype(BF)
        else:
            grads[x, mine_c + place, r, :] = value.astype(BF)

    def add_core(k, h, place, first=None):
        r = span(k)
        value = grads[h, mine_c + place, r, :].astype(F32) + from_c[h, place, r, :].astype(F32)
        if first is not None:
            value = value + from_1[first, r, :].astype(F32)
        grads[h, mine_c + place, r, :] = value.astype(BF)

    z_ways = (("z", zh, 1 - zl), ("z2", 1 - zh, zl), ("z3", 1 - zh, 1 - zl))

    def sum_c(k):
        r = span(k)
        hop(k, 0, grads.at[:, pl.ds((1 - c) * 8, 8), r], from_c.at[:, :, r], "c")

    def sum_1(k):
        r = span(k)
        hops[k, 0].wait_recv()
        if FIRST[k] == "x":
            loop(8, lambda i: add_core(k, 1 - x, i))
            for i in range(2):
                hop(k, (1, 12)[i], grads.at[1 - x, pl.ds(mine_c + 4 * i, 4), r], from_1.at[pl.ds(4 * i, 4), r], "x")
        else:
            far = (1 - y) * 4
            for h in range(2):
                loop(4, lambda i: add_core(k, h, far + i))
                hop(k, (1, 12)[h], grads.at[h, pl.ds(mine_c + far, 4), r], from_1.at[pl.ds(4 * h, 4), r], "y")

    def sum_2(k):
        r = span(k)
        hops[k, 1].wait_recv()
        hops[k, 12].wait_recv()
        hops[k, 0].wait_send()
        pl.semaphore_signal(free.at[k], inc=1, device_id=to["c"], device_id_type=MESH)
        if FIRST[k] == "x":
            far = (1 - y) * 4
            loop(4, lambda i: add_core(k, x, far + i, far + i))
            hop(k, 2, grads.at[x, pl.ds(mine_c + far, 4), r], from_2.at[:, r], "y")
        else:
            loop(4, lambda i: add_core(k, 1 - x, y * 4 + i, 4 * (1 - x) + i))
            hop(k, 2, grads.at[1 - x, pl.ds(mine_y, 4), r], from_2.at[:, r], "x")

    def sum_z(k):
        r = span(k)
        hops[k, 2].wait_recv()
        for i, (axis, high, low) in enumerate(z_ways):
            total_of(k, 2 * high + low)
            hop(k, 3 + i, grads.at[x, piece_of(high, low), r], from_z.at[i, r], axis)

    def back_z(k):
        r = span(k)
        for i in range(3):
            hops[k, 3 + i].wait_recv()
        near = 2 * zh + zl
        total_of(k, near, last=True)
        where = gathered.at[near + y * 4, r]
        for i, (axis, _, _) in enumerate(z_ways):
            hop(k, 6 + i, where, where, axis)

    def back_y(k):
        for i in range(3):
            hops[k, 6 + i].wait_recv()
        where = gathered.at[pl.ds(y * 4, 4), span(k)]
        hop(k, 9, where, where, "y")
        pl.semaphore_wait(free.at[k], 1)
        hop(k, 10, where, grads.at[x, pl.ds(mine_c + y * 4, 4), span(k)], "c")

    def back_c(k):
        hops[k, 9].wait_recv()
        where = gathered.at[pl.ds((1 - y) * 4, 4), span(k)]
        hop(k, 11, where, grads.at[x, pl.ds(mine_c + (1 - y) * 4, 4), span(k)], "c")

    outs = []

    def finish(k):
        hops[k, 10].wait_recv()
        hops[k, 11].wait_recv()
        r = span(k)
        for i, source, first in ((0, gathered, mine_c), (1, grads.at[x, pl.ds((1 - c) * 8, 8)], (1 - c) * 8)):
            copy = pltpu.make_async_copy(source.at[:, r], flat_out.at[pl.ds(first, 8), r], fin.at[k, i])
            copy.start()
            outs.append(copy)

    steps = (sum_c, sum_1, sum_2, sum_z, back_z, back_y, back_c, finish)

    ends = [doc[0, 0]]
    for i in range(1, doc.shape[1]):
        ends.append(ends[-1] + doc[0, i])

    def start_of(places):
        start = jnp.zeros_like(places)
        for i, end in enumerate(ends):
            start = jnp.where(places >= end, end, start)
        return start

    gain_own[...] = jnp.zeros_like(gain_own)
    for i, ref in enumerate(shards):
        gain_own[i : i + 1, 0 : ref.shape[0]] = ref[...].astype(F32).reshape(1, ref.shape[0])
    gain_copy = send(gain_own, gain_far, gs_.at[0], gr_.at[0], "x")
    weight_x(0)
    place_row = s * rows + lax.broadcasted_iota(jnp.int32, (1, rows), 1)
    start_row = start_of(place_row)
    gain = lambda i, size: gain_full[i : i + 1, 0:size]
    scaling = head ** (-0.5)
    blocks = 4
    root = 0.7978845608028654
    tiles_ff = ff // head
    tiles = plan.tiles
    wide = heads * head
    at_down, at_gate, at_up, at_out, at_q, at_kv = plan.starts
    held = {}

    def by_rows(size, step):
        loop(rows // size, lambda i: step(pl.ds(pl.multiple_of(i * size, size), size)))

    def task_init():
        place_col = s * rows + lax.broadcasted_iota(jnp.int32, (rows, 128), 0)
        angles = (place_col - start_of(place_col)).astype(F32) * freq[...]
        cos_t[...] = jnp.cos(angles)
        sin_t[...] = jnp.sin(angles)
        none = jnp.zeros((16, 128), BF)
        for h in range(2):
            for p in range(2, 16):
                grads[h, p, plan.gains_at : plan.gains_at + 16, :] = none
        gain_rows[...] = jnp.zeros_like(gain_rows)
        gain_acc[...] = jnp.zeros_like(gain_acc)
        dkv_f[...] = jnp.zeros_like(dkv_f)

    def norm_in(r):
        v = tok[r, :].astype(F32)
        attn_in[r, :] = (v * inverse_rms(v) * gain(0, width)).astype(BF)

    def task_norm():
        gain_copy.wait_recv()
        own, far = gain_own[...], gain_far[...]
        first, second = jnp.where(x == 0, own, far), jnp.where(x == 0, far, own)
        line = lax.broadcasted_iota(jnp.int32, own.shape, 0)
        short = (line == 1) | (line == 2)
        moved = jnp.where(short, pltpu.roll(second, head // 2, 1), pltpu.roll(second, half, 1))
        gain_full[...] = first + moved
        by_rows(64, norm_in)
        attn_in_t[...] = attn_in[...].T

    def project(j):
        qkv_f[j] = dot(attn_in[...], qkv_mat[:, at_block(j, head)])

    def task_kv():
        weight_done(0)
        project(heads)
        project(heads + 1)
        k_f = qkv_f[heads]
        kv[s, :, 0:head] = turn(k_f * inverse_rms(k_f) * gain(2, head), cos_t[...], sin_t[...]).astype(BF)
        kv[s, :, head : 2 * head] = qkv_f[heads + 1].astype(BF)
        for n in range(2):
            where = kv.at[s, :, n * head : (n + 1) * head]
            held["y", n] = send(where, where, kv_s.at[n], kv_r.at[n], "y")
            held["c", n] = send(where, where, kv_s.at[2 + n], kv_r.at[2 + n], "c")

    def turn_query(h):
        project(h)
        q_f = qkv_f[h]
        queries[h] = turn(q_f * inverse_rms(q_f) * gain(1, head), cos_t[...], sin_t[...]).astype(BF)

    def task_q():
        loop(heads, turn_query)

    def task_kvf(n):
        held["y", n].wait_recv()
        where = kv.at[(1 - y) * 2 + c, :, n * head : (n + 1) * head]
        held["cc", n] = send(where, where, kv_s.at[4 + n], kv_r.at[4 + n], "c")

    def transpose_keys(i):
        keys_t[:, at_block(i, rows)] = kv[i, :, 0:head].T

    def transpose_values(i):
        values_t[:, at_block(i, rows)] = kv[i, :, head : 2 * head].T

    def task_keys():
        held["c", 0].wait_recv()
        held["cc", 0].wait_recv()

    def task_kvt():
        held["c", 1].wait_recv()
        held["cc", 1].wait_recv()
        loop(blocks, transpose_values)

    def attend(h):
        q = queries[h]
        top = jnp.full((1, rows), MASKED, F32)
        for i in range(blocks):
            u = i * rows + lax.broadcasted_iota(jnp.int32, (rows, rows), 0)
            raw = dot_nt(kv[i, :, 0:head], q) * scaling
            raw = jnp.where((u <= place_row) & (u >= start_row), raw, MASKED)
            scores[i] = raw
            top = jnp.maximum(top, jnp.max(raw, axis=0, keepdims=True))
        denominator = jnp.zeros((1, rows), F32)
        for i in range(blocks):
            e = jnp.exp(scores[i] - top)
            scores[i] = e
            denominator = denominator + jnp.sum(e, axis=0, keepdims=True)
        inv = 1.0 / denominator
        for i in range(blocks):
            probs[h, i * rows : (i + 1) * rows, :] = (scores[i] * inv).astype(BF)

    def mix(h):
        mixed[:, at_block(h, head)] = dot(values_t[...], probs[h]).T.astype(BF)

    def task_at(n):
        loop(2, lambda i: attend(2 * n + i))

    def norm_ff(r):
        o = out_f[r, :]
        h = tok[r, :].astype(F32) + o * inverse_rms(o) * gain(3, width)
        h1[r, :] = h
        ff_in[r, :] = (h * inverse_rms(h) * gain(4, width)).astype(BF)

    def task_outp():
        loop(heads, mix)
        weight_done(1)
        out_f[...] = dot(mixed[...], out_mat[...])
        by_rows(64, norm_ff)
        ff_in_t[...] = ff_in[...].T

    def feed(j):
        g = dot(ff_in[...], gate_mat[:, at_block(j, head)])
        u = dot(ff_in[...], up_mat[:, at_block(j, head)])
        gate_f[j] = g
        up_f[j] = u
        t = jnp.tanh(root * (g + 0.044715 * (g * g * g)))
        hidden[:, at_block(j, head)] = (0.5 * g * (1.0 + t) * u).astype(BF)

    def task_ff(n):
        if n == 0:
            weight_done(2)
            weight_done(3)
        loop(tiles_ff // 2, lambda j: feed(j + n * (tiles_ff // 2)))

    def task_down():
        weight_done(4)
        down_f[...] = dot(hidden[...], down_mat[...])

    def gain_add(i, size, row):
        gain_acc[i : i + 1, 0:size] = gain_acc[i : i + 1, 0:size] + row

    def norm_out(r):
        d = down_f[r, :]
        res_out[r, :] = (h1[r, :] + d * inverse_rms(d) * gain(5, width)).astype(BF)
        pulled, g_row = rms_pull(d, gain(5, width), dout[r, :].astype(F32))
        d_down[r, :] = pulled.astype(BF)
        gain_add(5, width, g_row)

    def task_nout():
        by_rows(64, norm_out)

    def grad_down(j):
        value = dot(hidden[:, at_block(j, head)].T, d_down[...]).astype(BF)
        high, low = j // (tiles_ff // 2), j % (tiles_ff // 2)
        size = ff // 32
        for i in range(head // size):
            for t in range(tiles):
                grads[high, low * (head // size) + i, at_down + size * t : at_down + size * (t + 1), :] = value[
                    size * i : size * (i + 1), 128 * t : 128 * (t + 1)
                ]

    def task_gd():
        loop(tiles_ff, grad_down)

    def feed_back(j):
        d_hidden = dot_nt(d_down[...], down_mat[at_block(j, head), :])
        g, u = gate_f[j], up_f[j]
        t = jnp.tanh(root * (g + 0.044715 * (g * g * g)))
        act = 0.5 * g * (1.0 + t)
        slope = 0.5 * (1.0 + t) + 0.5 * g * (1.0 - t * t) * (root * (1.0 + 3 * 0.044715 * (g * g)))
        d_gate = (d_hidden * u * slope).astype(BF)
        d_up = (d_hidden * act).astype(BF)
        for at, value in ((at_gate, d_gate), (at_up, d_up)):
            full = dot(ff_in_t[...], value).astype(BF)
            for h in range(2):
                for t_ in range(2):
                    grads[h, 2 * j + t_, at : at + half, :] = full[half * h : half * (h + 1), 128 * t_ : 128 * (t_ + 1)]
        more = dot_nt(d_gate, gate_mat[:, at_block(j, head)]) + dot_nt(d_up, up_mat[:, at_block(j, head)])
        down_f[...] = down_f[...] + more

    def task_fb(n):
        if n == 0:
            down_f[...] = jnp.zeros_like(down_f)
        loop(tiles_ff // 4, lambda j: feed_back(j + n * (tiles_ff // 4)))

    def norm_mid(r):
        pulled, g_row = rms_pull(h1[r, :], gain(4, width), down_f[r, :])
        gain_add(4, width, g_row)
        d_mid = dout[r, :].astype(F32) + pulled
        d_h1[r, :] = d_mid
        pulled, g_row = rms_pull(out_f[r, :], gain(3, width), d_mid)
        gain_add(3, width, g_row)
        d_outp[r, :] = pulled.astype(BF)

    def task_mid():
        by_rows(64, norm_mid)

    def grad_out(j):
        value = dot(mixed[:, at_block(j, head)].T, d_outp[...]).astype(BF)
        size = heads * head // 32
        high, low = j // (heads // 2), j % (heads // 2)
        for i in range(head // size):
            for t in range(tiles):
                grads[high, low * (head // size) + i, at_out + size * t : at_out + size * (t + 1), :] = value[
                    size * i : size * (i + 1), 128 * t : 128 * (t + 1)
                ]
        d_mixed[j] = dot_nt(d_outp[...], out_mat[at_block(j, head), :]).astype(BF)

    def task_gout():
        loop(blocks, transpose_keys)
        loop(heads, grad_out)

    def attend_back(h):
        dm = d_mixed[h]
        along = jnp.zeros((1, rows), F32)
        for i in range(blocks):
            d_probs = dot_nt(kv[i, :, head : 2 * head], dm)
            scores[i] = d_probs
            p = probs[h, i * rows : (i + 1) * rows, :].astype(F32)
            along = along + jnp.sum(p * d_probs, axis=0, keepdims=True)
        for i in range(blocks):
            low = probs[h, i * rows : (i + 1) * rows, :]
            ds = (low.astype(F32) * (scores[i] - along) * scaling).astype(BF)
            d_raw[i * rows : (i + 1) * rows, :] = ds
            r = slice(i * rows, (i + 1) * rows)
            dkv_f[r, 0:head] = dkv_f[r, 0:head] + dot(ds, queries[h])
            dkv_f[r, head : 2 * head] = dkv_f[r, head : 2 * head] + dot(low, dm)
        dq = dot(keys_t[...], d_raw[...]).T
        turned = turn(dq, cos_t[...], -sin_t[...])
        pulled, g_row = rms_pull(qkv_f[h], gain(1, head), turned)
        gain_add(1, head, g_row)
        d_qkv[:, at_block(h, head)] = pulled.astype(BF)

    def task_ab(n):
        loop(2, lambda i: attend_back(2 * n + i))

    def task_dks():
        for i in range(blocks):
            dkv[i] = dkv_f[i * rows : (i + 1) * rows, :].astype(BF)
        held["dk_c"] = [
            send(dkv.at[2 * i + 1 - c], dkv_c.at[i], dk_s.at[i], dk_r.at[i], "c") for i in range(2)
        ]

    def grad_query(h):
        full = dot(attn_in_t[...], d_qkv[:, at_block(h, head)]).astype(BF)
        for n in range(2):
            for i in range(4):
                for t in range(2):
                    grads[n, 4 * h + i, at_q + block * t : at_q + block * (t + 1), :] = full[
                        half * n + block * i : half * n + block * (i + 1), 128 * t : 128 * (t + 1)
                    ]

    def task_dky():
        for copy in held["dk_c"]:
            copy.wait_recv()
        far = (1 - y) * 2 + c
        dkv[far] = (dkv[far].astype(F32) + dkv_c[1 - y].astype(F32)).astype(BF)
        held["dk_y"] = send(dkv.at[far], dkv_y, dk_s.at[2], dk_r.at[2], "y")

    def task_gq():
        loop(heads, grad_query)

    def task_gkv():
        held["dk_y"].wait_recv()
        d_own = dkv[s].astype(F32) + dkv_c[y].astype(F32) + dkv_y[...].astype(F32)
        turned = turn(d_own[:, 0:head], cos_t[...], -sin_t[...])
        pulled, g_row = rms_pull(qkv_f[heads], gain(2, head), turned)
        gain_add(2, head, g_row)
        d_qkv[:, wide : wide + head] = pulled.astype(BF)
        d_qkv[:, wide + head : wide + 2 * head] = d_own[:, head : 2 * head].astype(BF)
        full = dot(attn_in_t[...], d_qkv[:, wide : wide + 2 * head]).astype(BF)
        for n in range(2):
            for j in range(4):
                for i in range(4):
                    grads[n, 4 * j + i, at_kv : at_kv + block, :] = full[
                        half * n + block * i : half * n + block * (i + 1), 128 * j : 128 * (j + 1)
                    ]
        down_f[...] = dot_nt(d_qkv[...], qkv_mat[...])


    def norm_first(r):
        pulled, g_row = rms_pull(tok[r, :].astype(F32), gain(0, width), down_f[r, :])
        gain_add(0, width, g_row)
        dtok_out[r, :] = (d_h1[r, :] + pulled).astype(BF)

    def task_last():
        by_rows(64, norm_first)
        for i in range(6):
            for t in range(tiles):
                gain_rows[i * tiles + t : i * tiles + t + 1, :] = gain_acc[i : i + 1, 128 * t : 128 * (t + 1)]
        for p in range(2):
            low = gain_rows[16 * p : 16 * (p + 1), :].astype(BF)
            for h in range(2):
                grads[h, p, plan.gains_at : plan.gains_at + 16, :] = low

    def task_w(way, i):
        {"x": weight_x, "a": weight_a, "b": weight_b, "c": weight_c, "d": weight_d}[way](i)

    named = {
        "init": task_init, "norm": task_norm, "kv": task_kv, "q": task_q, "kvf": task_kvf, "keys": task_keys, "kvt": task_kvt, "at": task_at,
        "outp": task_outp, "ff": task_ff, "down": task_down, "nout": task_nout, "gd": task_gd, "fb": task_fb,
        "mid": task_mid, "gout": task_gout, "ab": task_ab, "dks": task_dks, "dky": task_dky, "gq": task_gq,
        "gkv": task_gkv, "last": task_last,
    }
    for entry in SCHEDULE:
        name, *rest = entry
        if name == "sum":
            steps[rest[1]](rest[0])
        elif name[0] == "w":
            task_w(name[1], *rest)
        else:
            named[name](*rest)
    freed = [hops[k, 0] for k in range(len(plan.chunks))]
    for copy in sends:
        if not any(copy is other for other in freed):
            copy.wait_send()
    for copy in outs:
        copy.wait()


def spread_kernel(plan, flat, res, dtok, *refs):
    (res_o, dtok_o, q_o, k_o, v_o, o_o, g_o, u_o, d_o, gin, gq, gk, ga, gf, go, gains_f) = refs
    step = pl.program_id(0)
    at_down, at_gate, at_up, at_out, at_q, at_kv = plan.starts
    half, block, head, tiles = plan.half, plan.block, plan.head, plan.tiles

    def put(ref, rows, size, col, i, at):
        ref[rows : rows + size, col : col + 128] = flat[i, at : at + size, :].astype(F32)

    for i in range(4):
        for at, ref, size in ((at_down, d_o, plan.ff // 32), (at_out, o_o, plan.heads * head // 32)):
            for t in range(tiles):
                put(ref, size * i, size, 128 * t, i, at + size * t)
        put(g_o, 0, half, 128 * i, i, at_gate)
        put(u_o, 0, half, 128 * i, i, at_up)
        for t in range(2):
            put(q_o, block * i, block, 128 * t, i, at_q + block * t)

    @pl.when(step < 2)
    def _():
        for i in range(4):
            put(k_o, block * i, block, 0, i, at_kv)

    @pl.when(step >= 2)
    def _():
        for i in range(4):
            put(v_o, block * i, block, 0, i, at_kv)

    @pl.when(step == 0)
    def _():
        res_o[...] = res[...]
        dtok_o[...] = dtok[...]
        gains_f[...] = jnp.zeros_like(gains_f)
        for p in range(2):
            lines = flat[p, plan.gains_at : plan.gains_at + 16, :].astype(F32)
            for n in range(16):
                i, t = (16 * p + n) // tiles, (16 * p + n) % tiles
                if i < 6:
                    gains_f[i : i + 1, 128 * t : 128 * (t + 1)] = lines[n : n + 1, :]
        first = lax.axis_index("fsdp") == 0
        values = gains_f[...]
        own = jnp.where(first, values, pltpu.roll(values, half, 1))
        for i, ref in ((0, gin), (3, ga), (4, gf), (5, go)):
            ref[...] = own[i, 0:half]
        own = jnp.where(first, values[:, 0 : head // 2], values[:, head // 2 : head])
        gq[...] = own[1, :]
        gk[...] = own[2, :]


def fused(tokens, d_out, doc_lengths, *weights):
    w_query, w_key, w_value, w_out, w_gate, w_up, w_down = weights[:7]
    gains = weights[7:]
    rows, width = tokens.shape[1:]
    head = 2 * weights[8].shape[0]
    heads = w_query.shape[1] // head
    ff = w_gate.shape[1]
    plan = Plan(rows, width, heads, head, ff)
    freq = jnp.asarray(
        np.power(ROPE_BASE, -2.0 * np.arange(head // 2) / head).astype(np.float32)[None]
    )
    vmem, far = pl.BlockSpec(memory_space=pltpu.VMEM), pl.BlockSpec(memory_space=pl.ANY)
    scratch = lambda *shape: pltpu.VMEM(shape, BF)
    scratch32 = lambda *shape: pltpu.VMEM(shape, F32)
    wide = heads * head
    total, chunks = plan.total, len(plan.chunks)
    dma = lambda *shape: pltpu.SemaphoreType.DMA(shape)
    tiles_ff = ff // head
    scratch_shapes = [
        scratch(width, wide + 2 * head),
        scratch(wide, width),
        scratch(width, ff),
        scratch(width, ff),
        scratch(ff, width),
        scratch32(8, width),
        scratch32(8, width),
        scratch32(8, width),
        scratch(rows, width),
        scratch(width, rows),
        scratch32(heads + 2, rows, head),
        scratch(heads, rows, head),
        scratch(4, rows, 2 * head),
        scratch(head, 4 * rows),
        scratch(head, 4 * rows),
        scratch(heads, 4 * rows, rows),
        scratch(rows, wide),
        scratch32(rows, width),
        scratch32(rows, width),
        scratch(rows, width),
        scratch(width, rows),
        scratch32(tiles_ff, rows, head),
        scratch32(tiles_ff, rows, head),
        scratch(rows, ff),
        scratch32(rows, width),
        scratch(rows, width),
        scratch32(rows, width),
        scratch(rows, width),
        scratch(heads, rows, head),
        scratch32(4 * rows, 2 * head),
        scratch(4, rows, 2 * head),
        scratch(2, rows, 2 * head),
        scratch(rows, 2 * head),
        scratch(rows, wide + 2 * head),
        scratch32(rows, 128),
        scratch32(rows, 128),
        scratch32(4, rows, rows),
        scratch(4 * rows, rows),
        scratch32(8, width),
        scratch32(32, 128),
        scratch(2, 16, total, 128),
        scratch(2, 8, total, 128),
        scratch(8, total, 128),
        scratch(4, total, 128),
        scratch(3, total, 128),
        dma(7),
        dma(7),
        dma(7),
        dma(5, 7),
        dma(5, 7),
        dma(6),
        dma(6),
        dma(3),
        dma(3),
        dma(1),
        dma(1),
        dma(chunks, 13),
        dma(chunks, 13),
        dma(chunks, 2),
        pltpu.SemaphoreType.REGULAR((chunks,)),
    ]
    result, d_tokens, flat = pl.pallas_call(
        functools.partial(layer_kernel, plan),
        out_shape=[
            jax.ShapeDtypeStruct((rows, width), BF),
            jax.ShapeDtypeStruct((rows, width), BF),
            jax.ShapeDtypeStruct((16, total, 128), BF),
        ],
        in_specs=[pl.BlockSpec(memory_space=pltpu.SMEM)] + [vmem] * 9 + [far] * 7,
        out_specs=[vmem, vmem, far],
        scratch_shapes=scratch_shapes,
        compiler_params=pltpu.CompilerParams(
            collective_id=0, has_side_effects=True, vmem_limit_bytes=58 * 2**20
        ),
        name="layer",
    )(doc_lengths, freq, *gains, tokens[0], d_out[0], w_query, w_key, w_value, w_out, w_gate, w_up, w_down)
    half, block = plan.half, plan.block
    whole = lambda *shape: pl.BlockSpec(shape, lambda p: (0,) * len(shape))
    shape32 = lambda *shape: jax.ShapeDtypeStruct(shape, F32)
    outs = pl.pallas_call(
        functools.partial(spread_kernel, plan),
        grid=(4,),
        out_shape=[
            jax.ShapeDtypeStruct((rows, width), BF),
            jax.ShapeDtypeStruct((rows, width), BF),
            shape32(half, wide),
            shape32(half, head),
            shape32(half, head),
            shape32(wide // 2, width),
            shape32(half, ff),
            shape32(half, ff),
            shape32(ff // 2, width),
            shape32(half),
            shape32(head // 2),
            shape32(head // 2),
            shape32(half),
            shape32(half),
            shape32(half),
        ],
        in_specs=[
            pl.BlockSpec((4, total, 128), lambda p: (p, 0, 0)),
            whole(rows, width),
            whole(rows, width),
        ],
        out_specs=[
            whole(rows, width),
            whole(rows, width),
            pl.BlockSpec((half, head), lambda p: (0, p)),
            pl.BlockSpec((half, 128), lambda p: (0, jnp.minimum(p, 1))),
            pl.BlockSpec((half, 128), lambda p: (0, jnp.maximum(p, 2) - 2)),
            pl.BlockSpec((wide // 8, width), lambda p: (p, 0)),
            pl.BlockSpec((half, ff // 4), lambda p: (0, p)),
            pl.BlockSpec((half, ff // 4), lambda p: (0, p)),
            pl.BlockSpec((ff // 8, width), lambda p: (p, 0)),
            whole(half),
            whole(head // 2),
            whole(head // 2),
            whole(half),
            whole(half),
            whole(half),
        ],
        scratch_shapes=[scratch32(8, width)],
        compiler_params=pltpu.CompilerParams(vmem_limit_bytes=40 * 2**20),
        name="spread",
    )(flat, result, d_tokens)
    return (outs[0][None], outs[1][None]) + tuple(outs[2:])


def solution(mesh):
    whole = mesh.shape
    small = whole["rep"] == 4 and whole["fsdp"] == 2 and whole["seq"] == 4
    body = fused if small else general
    in_specs = (
        P(("rep", "fsdp"), "seq", None),
        P(("rep", "fsdp"), "seq", None),
        P(("rep", "fsdp"), None),
        P("fsdp", None),
        P("fsdp", None),
        P("fsdp", None),
        P("fsdp", None),
        P("fsdp", None),
        P("fsdp", None),
        P("fsdp", None),
        P("fsdp"),
        P("fsdp"),
        P("fsdp"),
        P("fsdp"),
        P("fsdp"),
        P("fsdp"),
    )
    out_specs = (
        P(("rep", "fsdp"), "seq", None),
        P(("rep", "fsdp"), "seq", None),
        P("fsdp", None),
        P("fsdp", None),
        P("fsdp", None),
        P("fsdp", None),
        P("fsdp", None),
        P("fsdp", None),
        P("fsdp", None),
        P("fsdp"),
        P("fsdp"),
        P("fsdp"),
        P("fsdp"),
        P("fsdp"),
        P("fsdp"),
    )
    return jax.shard_map(body, mesh=mesh, in_specs=in_specs, out_specs=out_specs, check_vma=False)
```

```python
import functools

import jax
import jax.numpy as jnp
import numpy as np
from jax import lax
from jax.experimental import pallas as pl
from jax.experimental.pallas import tpu as pltpu
from jax.sharding import PartitionSpec as P

EPS = 1e-06
ROPE_BASE = 1000000.0
MASKED = -1e30
MESH = pl.DeviceIdType.MESH
BF, F32 = jnp.bfloat16, jnp.float32


def rms_norm(values, gain_vec):
    return values * lax.rsqrt(jnp.mean(values * values, axis=-1, keepdims=True) + EPS) * gain_vec


def rotate(values, angles):
    half_width = values.shape[-1] // 2
    front_half = values[..., :half_width]
    back_half = values[..., half_width:]
    cos_part = jnp.cos(angles)
    sin_part = jnp.sin(angles)
    return jnp.concatenate(
        [
            front_half * cos_part - back_half * sin_part,
            back_half * cos_part + front_half * sin_part,
        ],
        axis=-1,
    )


def frequencies(head_size):
    return jnp.power(
        jnp.float32(ROPE_BASE), -2.0 * jnp.arange(head_size // 2, dtype=jnp.float32) / head_size
    )


def layout(lengths_row, total_len):
    count = lengths_row.shape[0]
    before = jnp.arange(count)[None, :] <= jnp.arange(count)[:, None]
    doc_ends = jnp.sum(jnp.where(before, lengths_row[None, :], 0), axis=1)
    starts = doc_ends - lengths_row
    indices = jnp.arange(total_len, dtype=jnp.int32)
    segment = jnp.sum((indices[:, None] >= doc_ends[None, :]).astype(jnp.int32), axis=1)
    onehot = segment[:, None] == jnp.arange(count, dtype=jnp.int32)[None, :]
    doc_begin = jnp.sum(jnp.where(onehot, starts[None, :], 0), axis=1)
    return (segment, indices - doc_begin)


def matmul(left_side, right_side):
    return jnp.dot(left_side, right_side, preferred_element_type=jnp.float32)


def times_transpose(left_side, right_side):
    return lax.dot_general(
        left_side, right_side, (((1,), (1,)), ((), ())), preferred_element_type=jnp.float32
    )


def transpose_times(left_side, right_side):
    return lax.dot_general(
        left_side, right_side, (((0,), (0,)), ((), ())), preferred_element_type=jnp.float32
    )


def gated(gate_proj, up_proj):
    return jax.nn.gelu(gate_proj, approximate=True) * up_proj


def gather_rows(shard):
    return lax.all_gather(shard, "fsdp", axis=0, tiled=True)


def reduce_rows(grad):
    low = grad.astype(jnp.bfloat16)
    own = lax.psum_scatter(low, "fsdp", scatter_dimension=0, tiled=True)
    return lax.psum(own, ("rep", "seq")).astype(jnp.float32)


def general(
    tokens,
    d_out,
    doc_lengths,
    w_query,
    w_key,
    w_value,
    w_out,
    w_gate,
    w_up,
    w_down,
    g_input,
    g_query,
    g_key,
    g_attn,
    g_ffin,
    g_ffout,
):
    shards = lax.axis_size("fsdp")
    gain_shards = (g_input, g_query, g_key, g_attn, g_ffin, g_ffout)
    widths = [entry.shape[0] for entry in gain_shards]
    starts = [sum(widths[:i]) for i in range(len(widths))]
    gain_rows = lax.all_gather(jnp.concatenate(gain_shards)[None], "fsdp", axis=0, tiled=True)
    gain_input, gain_query, gain_key, gain_attn, gain_ffin, gain_ffout = [
        gain_rows[:, at : at + width].reshape(-1).astype(jnp.float32)
        for at, width in zip(starts, widths)
    ]
    qkv_mat = gather_rows(jnp.concatenate([w_query, w_key, w_value], axis=1))
    out_mat = gather_rows(w_out)
    gate_up_mat = gather_rows(jnp.concatenate([w_gate, w_up], axis=1))
    down_mat = gather_rows(w_down)
    row_count = tokens.shape[1]
    head_size = gain_query.shape[0]
    query_width = w_query.shape[1]
    head_count = query_width // head_size
    ff_width = w_gate.shape[1]
    total_len = row_count * lax.axis_size("seq")
    segment, position = layout(doc_lengths[0], total_len)
    offset = lax.axis_index("seq") * row_count
    query_seg = lax.dynamic_slice_in_dim(segment, offset, row_count)
    query_pos = lax.dynamic_slice_in_dim(position, offset, row_count)
    places = offset + jnp.arange(row_count, dtype=jnp.int32)
    allowed = (query_seg[:, None] == segment[None, :]) & (
        places[:, None] >= jnp.arange(total_len, dtype=jnp.int32)[None, :]
    )
    angles = query_pos.astype(jnp.float32)[:, None] * frequencies(head_size)[None, :]
    scaling = head_size ** (-0.5)
    inputs = tokens[0].astype(jnp.float32)
    cotangent = d_out[0].astype(jnp.float32)
    input_norm, input_pull = jax.vjp(rms_norm, inputs, gain_input)
    attn_input = input_norm.astype(jnp.bfloat16)
    qkv_proj = matmul(attn_input, qkv_mat)
    q_proj = qkv_proj[:, :query_width]
    k_proj = qkv_proj[:, query_width : query_width + head_size]
    v_proj = qkv_proj[:, query_width + head_size :]

    def query_fn(projected, gain_vec):
        shaped = projected.reshape(projected.shape[0], -1, gain_vec.shape[0])
        return rotate(rms_norm(shaped, gain_vec), angles[:, None, :])

    def key_fn(projected, gain_vec):
        return rotate(rms_norm(projected, gain_vec), angles)

    queries, query_pull = jax.vjp(query_fn, q_proj, gain_query)
    keys_own, key_pull = jax.vjp(key_fn, k_proj, gain_key)
    query_rows = queries.astype(jnp.bfloat16).reshape(row_count * head_count, head_size)
    key_value_rows = lax.all_gather(
        jnp.concatenate([keys_own.astype(jnp.bfloat16), v_proj.astype(jnp.bfloat16)], axis=1),
        "seq",
        axis=0,
        tiled=True,
    )
    key_rows = key_value_rows[:, :head_size]
    value_rows = key_value_rows[:, head_size:]

    def masked_scores():
        raw_scores = times_transpose(query_rows, key_rows).reshape(row_count, head_count, total_len)
        return jnp.where(allowed[:, None, :], raw_scores * scaling, MASKED)

    scores = masked_scores()
    top_score = jnp.max(scores, axis=-1, keepdims=True)
    shifted = jnp.exp(scores - top_score)
    denominator = jnp.sum(shifted, axis=-1, keepdims=True)
    log_total = top_score + jnp.log(denominator)
    probs_low = (
        (shifted / denominator).astype(jnp.bfloat16).reshape(row_count * head_count, total_len)
    )
    mixed_rows = (
        matmul(probs_low, value_rows)
        .reshape(row_count, head_count * head_size)
        .astype(jnp.bfloat16)
    )
    out_proj = matmul(mixed_rows, out_mat)
    attn_norm, attn_pull = jax.vjp(rms_norm, out_proj, gain_attn)
    hidden_one = inputs + attn_norm
    ffin_norm, ffin_pull = jax.vjp(rms_norm, hidden_one, gain_ffin)
    ff_input = ffin_norm.astype(jnp.bfloat16)
    gate_up_proj = matmul(ff_input, gate_up_mat)
    gate_proj = gate_up_proj[:, :ff_width]
    up_proj = gate_up_proj[:, ff_width:]
    activated, gated_pull = jax.vjp(gated, gate_proj, up_proj)
    hidden = activated.astype(jnp.bfloat16)
    down_proj = matmul(hidden, down_mat)
    ffout_norm, ffout_pull = jax.vjp(rms_norm, down_proj, gain_ffout)
    result = hidden_one + ffout_norm
    d_down, grad_gffout = ffout_pull(cotangent)
    d_down_low = d_down.astype(jnp.bfloat16)
    total_down = reduce_rows(transpose_times(hidden, d_down_low))
    d_hidden = times_transpose(d_down_low, down_mat)
    d_gate, d_up = gated_pull(d_hidden)
    d_gate_up_low = jnp.concatenate(
        [d_gate.astype(jnp.bfloat16), d_up.astype(jnp.bfloat16)], axis=1
    )
    total_gate_up = reduce_rows(transpose_times(ff_input, d_gate_up_low))
    d_ffin = times_transpose(d_gate_up_low, gate_up_mat)
    d_hidden_part, grad_gffin = ffin_pull(d_ffin)
    d_hidden_one = cotangent + d_hidden_part
    d_out_proj, grad_gattn = attn_pull(d_hidden_one)
    d_out_low = d_out_proj.astype(jnp.bfloat16)
    total_out = reduce_rows(transpose_times(mixed_rows, d_out_low))
    d_mixed = (
        times_transpose(d_out_low, out_mat)
        .astype(jnp.bfloat16)
        .reshape(row_count * head_count, head_size)
    )
    probs_full = jnp.exp(masked_scores() - log_total)
    d_probs = times_transpose(d_mixed, value_rows).reshape(row_count, head_count, total_len)
    row_dot = jnp.sum(probs_full * d_probs, axis=-1, keepdims=True)
    d_raw = (
        (probs_full * (d_probs - row_dot) * scaling)
        .astype(jnp.bfloat16)
        .reshape(row_count * head_count, total_len)
    )
    grad_rows = jnp.concatenate(
        [
            transpose_times(d_raw, query_rows).astype(jnp.bfloat16),
            transpose_times(probs_low, d_mixed).astype(jnp.bfloat16),
        ],
        axis=1,
    )
    d_queries = matmul(d_raw, key_rows).reshape(row_count, head_count, head_size)
    grad_own = lax.psum_scatter(grad_rows, "seq", scatter_dimension=0, tiled=True).astype(
        jnp.float32
    )
    d_q_proj, grad_gquery = query_pull(d_queries)
    d_k_proj, grad_gkey = key_pull(grad_own[:, :head_size])
    d_qkv_low = jnp.concatenate(
        [
            d_q_proj.astype(jnp.bfloat16),
            d_k_proj.astype(jnp.bfloat16),
            grad_own[:, head_size:].astype(jnp.bfloat16),
        ],
        axis=1,
    )
    grad_qkv = transpose_times(attn_input, d_qkv_low)
    d_attn_input = times_transpose(d_qkv_low, qkv_mat)
    d_inputs_part, grad_ginput = input_pull(d_attn_input)
    d_inputs = d_hidden_one + d_inputs_part
    grad_gains = (grad_ginput, grad_gquery, grad_gkey, grad_gattn, grad_gffin, grad_gffout)
    packed_gains = jnp.concatenate([entry.reshape(shards, -1) for entry in grad_gains], axis=1)
    total_qkv = reduce_rows(grad_qkv)
    total_gains = lax.psum_scatter(
        packed_gains.astype(jnp.bfloat16), "fsdp", scatter_dimension=0, tiled=True
    )
    total_gains = lax.psum(total_gains, ("rep", "seq")).astype(jnp.float32)[0]
    return (
        result.astype(jnp.bfloat16)[None],
        d_inputs.astype(jnp.bfloat16)[None],
        total_qkv[:, :query_width],
        total_qkv[:, query_width : query_width + head_size],
        total_qkv[:, query_width + head_size :],
        total_out,
        total_gate_up[:, :ff_width],
        total_gate_up[:, ff_width:],
        total_down,
    ) + tuple(total_gains[at : at + width] for at, width in zip(starts, widths))


def dot(left_side, right_side):
    return jnp.dot(left_side, right_side, preferred_element_type=F32)


def dot_nt(left_side, right_side):
    return lax.dot_general(
        left_side, right_side, (((1,), (1,)), ((), ())), preferred_element_type=F32
    )


def loop(count, step):
    lax.fori_loop(0, count, lambda i, carry: (step(i), carry)[1], 0)


def at_block(i, size):
    return pl.ds(pl.multiple_of(i * size, size), size)


def inverse_rms(values):
    return lax.rsqrt(jnp.mean(values * values, axis=-1, keepdims=True) + EPS)


def rms_pull(values, gain_row, grad):
    inv = inverse_rms(values)
    scaled = values * inv
    pulled = grad * gain_row
    along = jnp.mean(pulled * scaled, axis=-1, keepdims=True)
    return inv * (pulled - scaled * along), jnp.sum(grad * scaled, axis=0, keepdims=True)


def turn(values, cos_part, sin_part):
    half_width = values.shape[-1] // 2
    front, back = values[:, :half_width], values[:, half_width:]
    return jnp.concatenate(
        [front * cos_part - back * sin_part, back * cos_part + front * sin_part], axis=1
    )


class Plan:
    def __init__(self, rows, width, heads, head, ff):
        self.rows, self.width, self.heads, self.head, self.ff = rows, width, heads, head, ff
        self.half = width // 2
        block = self.half // 4
        sizes = (
            ff * width // (32 * 128),
            self.half * ff // (16 * 128),
            self.half * ff // (16 * 128),
            heads * head * width // (32 * 128),
            block * head // 128,
            block + 16,
        )
        self.starts = [sum(sizes[:i]) for i in range(len(sizes))]
        self.chunks = tuple(
            (start + size * a // 10, size * (b - a) // 10)
            for start, size, cuts in zip(self.starts, sizes, CUTS)
            for a, b in zip(cuts, cuts[1:])
        )
        self.block = block
        self.total = sum(sizes)
        self.gains_at = self.total - 16
        self.token_rows = rows * width // (16 * 128)
        self.tiles = width // 128


CUTS = ((0, 2, 6, 10), (0, 5, 10), (0, 5, 10), (0, 10), (0, 10), (0, 10))
FIRST = tuple("xxyyxyxxxx")
DIRECT = tuple("tttdttuttu")
WEIGHTS = ((0, 0, 3, "z", None), (0, 3, None, "y", None), (1, 0, None, "y", "rows"), (2, 0, None, "y", "columns"), (3, 0, None, "z", "columns"), (4, 0, None, "z", None))

SCHEDULE = (
    ("init",), ("wx", 1), ("norm",), ("wx", 2), ("wa", 0), ("wx", 3), ("wa", 1), ("wx", 4), ("wa", 2), ("wb", 0),
    ("wb", 1), ("wx", 5), ("wa", 3), ("kv",), ("wb", 2), ("wc", 2), ("q",), ("wa", 4), ("wb", 3), ("wc", 3),
    ("wd", 2), ("kvf", 0), ("wa", 5), ("keys",), ("at", 0), ("wb", 4), ("kvf", 1), ("at", 1), ("kvt",), ("wd", 3),
    ("outp",), ("wc", 4), ("wd", 4), ("ff", 0), ("wb", 5), ("ff", 1), ("down",), ("nout",), ("gd",), ("sum", 0, 0),
    ("sum", 1, 0), ("sum", 2, 0), ("fb", 0), ("sum", 0, 1), ("fb", 1), ("sum", 1, 1), ("sum", 2, 1), ("fb", 2),
    ("fb", 3), ("sum", 3, 0), ("sum", 4, 0), ("sum", 5, 0), ("sum", 6, 0), ("sum", 0, 2), ("mid",), ("gout",),
    ("sum", 3, 1), ("sum", 4, 1), ("sum", 7, 0), ("sum", 2, 2), ("sum", 1, 2), ("sum", 5, 1), ("sum", 0, 3),
    ("ab", 0), ("sum", 6, 1), ("sum", 7, 1), ("sum", 0, 4), ("ab", 1), ("dks",), ("sum", 0, 5), ("gq",),
    ("sum", 8, 0), ("sum", 3, 2), ("sum", 4, 2), ("dky",), ("sum", 1, 3), ("sum", 0, 6), ("sum", 2, 3), ("sum", 8, 1),
    ("sum", 1, 4), ("sum", 0, 7), ("sum", 2, 4), ("sum", 5, 2), ("sum", 6, 2), ("sum", 1, 5), ("sum", 2, 5),
    ("sum", 4, 3), ("sum", 1, 6), ("sum", 2, 6), ("sum", 7, 2), ("sum", 4, 4), ("sum", 1, 7), ("gkv",), ("sum", 0, 8),
    ("sum", 3, 3), ("sum", 2, 7), ("last",), ("sum", 9, 0), ("sum", 4, 5), ("sum", 0, 9), ("sum", 6, 3),
    ("sum", 9, 1), ("sum", 3, 4), ("sum", 7, 3), ("sum", 8, 2), ("sum", 4, 6), ("sum", 6, 4), ("sum", 1, 8),
    ("sum", 5, 3), ("sum", 1, 9), ("sum", 3, 5), ("sum", 2, 8), ("sum", 7, 4), ("sum", 2, 9), ("sum", 9, 2),
    ("sum", 4, 7), ("sum", 8, 3), ("sum", 6, 5), ("sum", 5, 4), ("sum", 7, 5), ("sum", 3, 6), ("sum", 8, 4),
    ("sum", 3, 7), ("sum", 9, 3), ("sum", 5, 5), ("sum", 7, 6), ("sum", 4, 8), ("sum", 8, 5), ("sum", 9, 4),
    ("sum", 6, 6), ("sum", 4, 9), ("sum", 5, 6), ("sum", 7, 7), ("sum", 8, 6), ("sum", 9, 5), ("sum", 7, 8),
    ("sum", 5, 7), ("sum", 9, 6), ("sum", 6, 7), ("sum", 7, 9), ("sum", 8, 7), ("sum", 9, 7), ("sum", 5, 8),
    ("sum", 6, 8), ("sum", 5, 9), ("sum", 9, 8), ("sum", 8, 8), ("sum", 6, 9), ("sum", 9, 9), ("sum", 8, 9),
)


SECOND = {"y": "z", "z": "y"}


def layer_kernel(plan, doc, freq, *refs):
    shards, refs = refs[:6], refs[6:]
    (tok, dout, wq, wk, wv, wo, wg, wu, wd, flat_out) = refs[:10]
    (qkv_mat, out_mat, gate_mat, up_mat, down_mat, gain_own, gain_far, gain_full, attn_in, attn_in_t, qkv_f, queries, kv, keys_t) = refs[10:24]
    (values_t, probs, mixed, out_f, h1, ff_in, ff_in_t, gate_f, up_f, hidden, down_f, d_down, d_h1) = refs[24:37]
    scores = gate_f
    (d_outp, d_mixed, dkv, dkv_c, dkv_y, d_qkv, cos_t, sin_t, d_raw, gain_acc, gain_rows) = refs[37:48]
    (grads, from_c, from_1, from_2, from_z) = refs[48:53]
    (w_local, wx_s, wx_r, wf_s, wf_r, kv_s, kv_r, dk_s, dk_r, gs_, gr_, rs_s, rs_r, fin, free, packed, out_sem) = refs[53:70]
    rows, width, heads, head, ff = plan.rows, plan.width, plan.heads, plan.head, plan.ff
    half, block = plan.half, plan.block
    rep, x, s = lax.axis_index("rep"), lax.axis_index("fsdp"), lax.axis_index("seq")
    y, c = s // 2, s % 2
    zh, zl = rep // 2, rep % 2
    to = {
        "x": (rep, 1 - x, s),
        "c": (rep, x, y * 2 + 1 - c),
        "y": (rep, x, (1 - y) * 2 + c),
        "z": (zh * 2 + 1 - zl, x, s),
        "z2": ((1 - zh) * 2 + zl, x, s),
        "z3": ((1 - zh) * 2 + 1 - zl, x, s),
    }
    sends = []

    def send(source, target, send_sem, recv_sem, axis):
        copy = pltpu.make_async_remote_copy(
            src_ref=source,
            dst_ref=target,
            send_sem=send_sem,
            recv_sem=recv_sem,
            device_id=to[axis],
            device_id_type=MESH,
        )
        copy.start()
        sends.append(copy)
        return copy

    parts = (
        ((wq, 0), (wk, heads * head), (wv, heads * head + head)),
        ((wo, 0),),
        ((wg, 0),),
        ((wu, 0),),
        ((wd, 0),),
    )
    mats = (qkv_mat, out_mat, gate_mat, up_mat, down_mat)
    locals_of, x_of, f_of = {}, {}, {}
    slot = 0
    slots = []
    for i, (mat, entries) in enumerate(zip(mats, parts)):
        shard_rows = mat.shape[0] // 2
        locals_of[i] = []
        for ref, col in entries:
            copy = pltpu.make_async_copy(
                ref, mat.at[pl.ds(x * shard_rows, shard_rows), pl.ds(col, ref.shape[1])], w_local.at[slot]
            )
            copy.start()
            locals_of[i].append(copy)
            slot += 1

    barrier = pltpu.get_barrier_semaphore()
    for axis in to:
        pl.semaphore_signal(barrier, inc=1, device_id=to[axis], device_id_type=MESH)
    pl.semaphore_wait(barrier, len(to))

    for m, *_ in WEIGHTS:
        slots.append(sum(len(parts[n]) for n, *_ in WEIGHTS[: len(slots)]))

    def region(i, far_bit, far_z):
        m, first, last, axis, cut = WEIGHTS[i]
        bit = y if axis == "y" else zl
        quarter = (1 - bit if far_bit else bit) * 2 + c
        low = zl if axis == "y" else y
        low = 1 - low if far_z else low
        size, columns = mats[m].shape[0] // 8, mats[m].shape[1]
        skip, size, at = 16 * first, (size if last is None else 16 * last) - 16 * first, quarter * size
        if cut == "rows":
            return at + low * (size // 2), size // 2, None
        if cut == "columns":
            return at + skip, size, at_block(low, columns // 2)
        return at + skip, size, None

    def weight_x(i):
        shard_rows = mats[WEIGHTS[i][0]].shape[0] // 2
        at, size, columns = region(i, False, False)
        x_of[i] = []
        for j, (ref, col) in enumerate(parts[WEIGHTS[i][0]]):
            here = pl.ds(0, ref.shape[1]) if columns is None else columns
            there = pl.ds(col, ref.shape[1]) if columns is None else columns
            x_of[i].append(
                send(
                    ref.at[pl.ds(at, size), here],
                    mats[WEIGHTS[i][0]].at[pl.ds(x * shard_rows + at, size), there],
                    wx_s.at[slots[i] + j],
                    wx_r.at[slots[i] + j],
                    "x",
                )
            )

    def weight_forward(i, n, axis, far_bit, far_z=False):
        shard_rows = mats[WEIGHTS[i][0]].shape[0] // 2
        at, size, columns = region(i, far_bit, far_z)
        where = mats[WEIGHTS[i][0]].at[pl.ds((1 - x) * shard_rows + at, size)]
        if columns is not None:
            where = mats[WEIGHTS[i][0]].at[pl.ds((1 - x) * shard_rows + at, size), columns]
        f_of[i, n] = send(where, where, wf_s.at[i, n], wf_r.at[i, n], axis)

    def weight_a(i):
        for copy in x_of[i]:
            copy.wait_recv()
        weight_forward(i, 0, WEIGHTS[i][3], False)
        if WEIGHTS[i][4]:
            weight_forward(i, 3, SECOND[WEIGHTS[i][3]], False)
        weight_forward(i, 1, "c", False)

    def weight_b(i):
        f_of[i, 0].wait_recv()
        if WEIGHTS[i][4]:
            weight_forward(i, 4, SECOND[WEIGHTS[i][3]], True)
        weight_forward(i, 2, "c", True)

    def weight_c(i):
        f_of[i, 3].wait_recv()
        weight_forward(i, 5, "c", False, True)

    def weight_d(i):
        f_of[i, 4].wait_recv()
        weight_forward(i, 6, "c", True, True)

    def weight_done(m):
        for i in range(len(WEIGHTS)):
            if WEIGHTS[i][0] == m:
                for n in (1, 2, 5, 6) if WEIGHTS[i][4] else (1, 2):
                    f_of[i, n].wait_recv()
        for copy in locals_of[m]:
            copy.wait()

    mine_c, mine_y = c * 8, c * 8 + y * 4
    gathered = from_c.at[1 - x]
    piece_of = lambda high, low: mine_y + 2 * high + low
    hops = {}

    def hop(k, n, source, target, axis):
        hops[k, n] = send(source, target, rs_s.at[k, n], rs_r.at[k, n], axis)

    def span(k):
        return pl.ds(*plan.chunks[k])

    def total_of(k, m, last=False, z=()):
        r = span(k)
        place = y * 4 + m
        value = grads[x, mine_c + place, r, :].astype(F32) + from_c[x, place, r, :].astype(F32)
        first = place if FIRST[k] == "x" else 4 * x + m
        value = value + from_1[first, r, :].astype(F32) + from_2[m, r, :].astype(F32)
        for i in z:
            value = value + from_z[i, r, :].astype(F32)
        if last:
            gathered[place, r, :] = value.astype(BF)
        else:
            grads[x, mine_c + place, r, :] = value.astype(BF)

    def add_core(k, h, place, first=None):
        r = span(k)
        value = grads[h, mine_c + place, r, :].astype(F32) + from_c[h, place, r, :].astype(F32)
        if first is not None:
            value = value + from_1[first, r, :].astype(F32)
        grads[h, mine_c + place, r, :] = value.astype(BF)

    z_ways = (("z", zh, 1 - zl), ("z2", 1 - zh, zl), ("z3", 1 - zh, 1 - zl))

    def sum_c(k):
        r = span(k)
        hop(k, 0, grads.at[:, pl.ds((1 - c) * 8, 8), r], from_c.at[:, :, r], "c")

    def sum_1(k):
        r = span(k)
        hops[k, 0].wait_recv()
        if FIRST[k] == "x":
            loop(8, lambda i: add_core(k, 1 - x, i))
            for i in range(2):
                hop(k, (1, 12)[i], grads.at[1 - x, pl.ds(mine_c + 4 * i, 4), r], from_1.at[pl.ds(4 * i, 4), r], "x")
        else:
            far = (1 - y) * 4
            for h in range(2):
                loop(4, lambda i: add_core(k, h, far + i))
                hop(k, (1, 12)[h], grads.at[h, pl.ds(mine_c + far, 4), r], from_1.at[pl.ds(4 * h, 4), r], "y")

    def sum_2(k):
        r = span(k)
        hops[k, 1].wait_recv()
        hops[k, 12].wait_recv()
        hops[k, 0].wait_send()
        pl.semaphore_signal(free.at[k], inc=1, device_id=to["c"], device_id_type=MESH)
        if FIRST[k] == "x":
            far = (1 - y) * 4
            loop(4, lambda i: add_core(k, x, far + i, far + i))
            hop(k, 2, grads.at[x, pl.ds(mine_c + far, 4), r], from_2.at[:, r], "y")
        else:
            loop(4, lambda i: add_core(k, 1 - x, y * 4 + i, 4 * (1 - x) + i))
            hop(k, 2, grads.at[1 - x, pl.ds(mine_y, 4), r], from_2.at[:, r], "x")

    def sum_z(k):
        r = span(k)
        hops[k, 2].wait_recv()
        for i, (axis, high, low) in enumerate(z_ways):
            total_of(k, 2 * high + low)
            hop(k, 3 + i, grads.at[x, piece_of(high, low), r], from_z.at[i, r], axis)

    def sum_z1(k):
        r = span(k)
        hops[k, 2].wait_recv()
        for i in range(2):
            total_of(k, 2 * i + 1 - zl)
            hop(k, 3 + i, grads.at[x, piece_of(i, 1 - zl), r], from_z.at[i, r], "z")

    def sum_z2(k):
        r = span(k)
        hops[k, 3].wait_recv()
        hops[k, 4].wait_recv()
        total_of(k, 2 * (1 - zh) + zl, z=(1 - zh,))
        hop(k, 5, grads.at[x, piece_of(1 - zh, zl), r], from_z.at[2, r], "z2")

    def back_z2(k):
        hops[k, 5].wait_recv()
        near = 2 * zh + zl
        total_of(k, near, last=True, z=(zh, 2))
        where = gathered.at[near + y * 4, span(k)]
        hop(k, 6, where, where, "z2")

    def back_z1(k):
        hops[k, 6].wait_recv()
        for i in range(2):
            where = gathered.at[y * 4 + 2 * i + zl, span(k)]
            hop(k, 7 + i, where, where, "z")

    def back_z(k):
        r = span(k)
        for i in range(3):
            hops[k, 3 + i].wait_recv()
        near = 2 * zh + zl
        total_of(k, near, last=True, z=(0, 1, 2))
        where = gathered.at[near + y * 4, r]
        for i, (axis, _, _) in enumerate(z_ways):
            hop(k, 6 + i, where, where, axis)

    def back_y(k):
        for i in range(3) if DIRECT[k] == "d" else (1, 2):
            hops[k, 6 + i].wait_recv()
        where = gathered.at[pl.ds(y * 4, 4), span(k)]
        hop(k, 9, where, where, "y")
        pl.semaphore_wait(free.at[k], 1)
        hop(k, 10, where, grads.at[x, pl.ds(mine_c + y * 4, 4), span(k)], "c")

    def back_c(k):
        hops[k, 9].wait_recv()
        where = gathered.at[pl.ds((1 - y) * 4, 4), span(k)]
        hop(k, 11, where, grads.at[x, pl.ds(mine_c + (1 - y) * 4, 4), span(k)], "c")

    outs = []

    def finish(k):
        hops[k, 10].wait_recv()
        if (k, 11) in hops:
            hops[k, 11].wait_recv()
        r = span(k)
        for i, source, first in ((0, gathered, mine_c), (1, grads.at[x, pl.ds((1 - c) * 8, 8)], (1 - c) * 8)):
            copy = pltpu.make_async_copy(source.at[:, r], flat_out.at[pl.ds(first, 8), r], fin.at[k, i])
            copy.start()
            outs.append(copy)

    def home_y(k):
        for i in range(3, 6) if DIRECT[k] == "v" else (5,):
            hops[k, i].wait_recv()
        near = 2 * zh + zl
        total_of(k, near, last=True, z=(0, 1, 2) if DIRECT[k] == "v" else (zh, 2))
        where = gathered.at[near + y * 4, span(k)]
        hop(k, 9, where, where, "y")

    def home_z2(k):
        hops[k, 9].wait_recv()
        for i in range(2):
            where = gathered.at[4 * i + 2 * zh + zl, span(k)]
            hop(k, 6 + i, where, where, "z2")

    def home_z1(k):
        hops[k, 6].wait_recv()
        hops[k, 7].wait_recv()
        for i, n in enumerate((8, 13, 14, 15)):
            where = gathered.at[2 * i + zl, span(k)]
            hop(k, n, where, where, "z")

    def home_c(k):
        for n in (8, 13, 14, 15):
            hops[k, n].wait_recv()
        pl.semaphore_wait(free.at[k], 1)
        hop(k, 10, gathered.at[:, span(k)], grads.at[x, pl.ds(mine_c, 8), span(k)], "c")

    ends_with = (back_y, back_c, finish)
    home = (home_y, home_z2, home_z1, home_c, finish)
    steps_of = {
        "d": (sum_c, sum_1, sum_2, sum_z, back_z) + ends_with,
        "t": (sum_c, sum_1, sum_2, sum_z1, sum_z2, back_z2, back_z1) + ends_with,
        "u": (sum_c, sum_1, sum_2, sum_z1, sum_z2) + home,
        "v": (sum_c, sum_1, sum_2, sum_z) + home,
    }

    ends = [doc[0, 0]]
    for i in range(1, doc.shape[1]):
        ends.append(ends[-1] + doc[0, i])

    def start_of(places):
        start = jnp.zeros_like(places)
        for i, end in enumerate(ends):
            start = jnp.where(places >= end, end, start)
        return start

    gain_own[...] = jnp.zeros_like(gain_own)
    for i, ref in enumerate(shards):
        gain_own[i : i + 1, 0 : ref.shape[0]] = ref[...].astype(F32).reshape(1, ref.shape[0])
    gain_copy = send(gain_own, gain_far, gs_.at[0], gr_.at[0], "x")
    weight_x(0)
    place_row = s * rows + lax.broadcasted_iota(jnp.int32, (1, rows), 1)
    start_row = start_of(place_row)
    gain = lambda i, size: gain_full[i : i + 1, 0:size]
    scaling = head ** (-0.5)
    blocks = 4
    root = 0.7978845608028654
    tiles_ff = ff // head
    tiles = plan.tiles
    wide = heads * head
    at_down, at_gate, at_up, at_out, at_q, at_kv = plan.starts
    held = {}

    def pack(n, r0, size, value):
        value = value.astype(BF)
        for i in range(size // 16):
            for t in range(tiles):
                at = n * plan.token_rows + 16 * t
                packed[r0 // 16 + i, at : at + 16, :] = value[16 * i : 16 * (i + 1), 128 * t : 128 * (t + 1)]

    def by_number(size, step):
        loop(rows // size, lambda i: step(i * size, pl.ds(pl.multiple_of(i * size, size), size)))

    def by_rows(size, step):
        loop(rows // size, lambda i: step(pl.ds(pl.multiple_of(i * size, size), size)))

    def task_init():
        place_col = s * rows + lax.broadcasted_iota(jnp.int32, (rows, 128), 0)
        angles = (place_col - start_of(place_col)).astype(F32) * freq[...]
        cos_t[...] = jnp.cos(angles)
        sin_t[...] = jnp.sin(angles)
        none = jnp.zeros((16, 128), BF)
        for h in range(2):
            for p in range(2, 16):
                grads[h, p, plan.gains_at : plan.gains_at + 16, :] = none
        gain_rows[...] = jnp.zeros_like(gain_rows)
        gain_acc[...] = jnp.zeros_like(gain_acc)

    def norm_in(r):
        v = tok[r, :].astype(F32)
        attn_in[r, :] = (v * inverse_rms(v) * gain(0, width)).astype(BF)

    def task_norm():
        gain_copy.wait_recv()
        own, far = gain_own[...], gain_far[...]
        first, second = jnp.where(x == 0, own, far), jnp.where(x == 0, far, own)
        line = lax.broadcasted_iota(jnp.int32, own.shape, 0)
        short = (line == 1) | (line == 2)
        moved = jnp.where(short, pltpu.roll(second, head // 2, 1), pltpu.roll(second, half, 1))
        gain_full[...] = first + moved
        by_rows(64, norm_in)
        attn_in_t[...] = attn_in[...].T

    def project(j):
        qkv_f[j] = dot(attn_in[...], qkv_mat[:, at_block(j, head)])

    def task_kv():
        weight_done(0)
        project(heads)
        project(heads + 1)
        k_f = qkv_f[heads]
        kv[s, :, 0:head] = turn(k_f * inverse_rms(k_f) * gain(2, head), cos_t[...], sin_t[...]).astype(BF)
        kv[s, :, head : 2 * head] = qkv_f[heads + 1].astype(BF)
        for n in range(2):
            where = kv.at[s, :, n * head : (n + 1) * head]
            held["y", n] = send(where, where, kv_s.at[n], kv_r.at[n], "y")
            held["c", n] = send(where, where, kv_s.at[2 + n], kv_r.at[2 + n], "c")

    def turn_query(h):
        project(h)
        q_f = qkv_f[h]
        queries[h] = turn(q_f * inverse_rms(q_f) * gain(1, head), cos_t[...], sin_t[...]).astype(BF)

    def task_q():
        loop(heads, turn_query)

    def task_kvf(n):
        held["y", n].wait_recv()
        where = kv.at[(1 - y) * 2 + c, :, n * head : (n + 1) * head]
        held["cc", n] = send(where, where, kv_s.at[4 + n], kv_r.at[4 + n], "c")

    def transpose_keys(i):
        keys_t[:, at_block(i, rows)] = kv[i, :, 0:head].T

    def transpose_values(i):
        values_t[:, at_block(i, rows)] = kv[i, :, head : 2 * head].T

    def task_keys():
        held["c", 0].wait_recv()
        held["cc", 0].wait_recv()

    def task_kvt():
        held["c", 1].wait_recv()
        held["cc", 1].wait_recv()
        loop(blocks, transpose_values)

    def attend(h):
        q = queries[h]
        top = jnp.full((1, rows), MASKED, F32)
        for i in range(blocks):
            u = i * rows + lax.broadcasted_iota(jnp.int32, (rows, rows), 0)
            raw = dot_nt(kv[i, :, 0:head], q) * scaling
            raw = jnp.where((u <= place_row) & (u >= start_row), raw, MASKED)
            scores[i] = raw
            top = jnp.maximum(top, jnp.max(raw, axis=0, keepdims=True))
        denominator = jnp.zeros((1, rows), F32)
        for i in range(blocks):
            e = jnp.exp(scores[i] - top)
            scores[i] = e
            denominator = denominator + jnp.sum(e, axis=0, keepdims=True)
        inv = 1.0 / denominator
        for i in range(blocks):
            probs[h, i * rows : (i + 1) * rows, :] = (scores[i] * inv).astype(BF)

    def mix(h):
        mixed[:, at_block(h, head)] = dot(values_t[...], probs[h]).T.astype(BF)

    def task_at(n):
        loop(2, lambda i: attend(2 * n + i))

    def norm_ff(r):
        o = out_f[r, :]
        h = tok[r, :].astype(F32) + o * inverse_rms(o) * gain(3, width)
        h1[r, :] = h
        ff_in[r, :] = (h * inverse_rms(h) * gain(4, width)).astype(BF)

    def task_outp():
        loop(heads, mix)
        weight_done(1)
        out_f[...] = dot(mixed[...], out_mat[...])
        by_rows(64, norm_ff)
        ff_in_t[...] = ff_in[...].T

    def feed(j):
        g = dot(ff_in[...], gate_mat[:, at_block(j, head)])
        u = dot(ff_in[...], up_mat[:, at_block(j, head)])
        gate_f[j] = g
        up_f[j] = u
        t = jnp.tanh(root * (g + 0.044715 * (g * g * g)))
        hidden[:, at_block(j, head)] = (0.5 * g * (1.0 + t) * u).astype(BF)

    def task_ff(n):
        if n == 0:
            weight_done(2)
            weight_done(3)
        loop(tiles_ff // 2, lambda j: feed(j + n * (tiles_ff // 2)))

    def task_down():
        weight_done(4)
        down_f[...] = dot(hidden[...], down_mat[...])

    def gain_add(i, size, row):
        gain_acc[i : i + 1, 0:size] = gain_acc[i : i + 1, 0:size] + row

    def norm_out(r0, r):
        d = down_f[r, :]
        pack(0, r0, 64, h1[r, :] + d * inverse_rms(d) * gain(5, width))
        pulled, g_row = rms_pull(d, gain(5, width), dout[r, :].astype(F32))
        d_down[r, :] = pulled.astype(BF)
        gain_add(5, width, g_row)

    def task_nout():
        by_number(64, norm_out)

    def grad_down(j):
        value = dot(hidden[:, at_block(j, head)].T, d_down[...]).astype(BF)
        high, low = j // (tiles_ff // 2), j % (tiles_ff // 2)
        size = ff // 32
        for i in range(head // size):
            for t in range(tiles):
                grads[high, low * (head // size) + i, at_down + size * t : at_down + size * (t + 1), :] = value[
                    size * i : size * (i + 1), 128 * t : 128 * (t + 1)
                ]

    def task_gd():
        loop(tiles_ff, grad_down)

    def feed_back(j):
        d_hidden = dot_nt(d_down[...], down_mat[at_block(j, head), :])
        g, u = gate_f[j], up_f[j]
        t = jnp.tanh(root * (g + 0.044715 * (g * g * g)))
        act = 0.5 * g * (1.0 + t)
        slope = 0.5 * (1.0 + t) + 0.5 * g * (1.0 - t * t) * (root * (1.0 + 3 * 0.044715 * (g * g)))
        d_gate = (d_hidden * u * slope).astype(BF)
        d_up = (d_hidden * act).astype(BF)
        for at, value in ((at_gate, d_gate), (at_up, d_up)):
            full = dot(ff_in_t[...], value).astype(BF)
            for h in range(2):
                for t_ in range(2):
                    grads[h, 2 * j + t_, at : at + half, :] = full[half * h : half * (h + 1), 128 * t_ : 128 * (t_ + 1)]
        more = dot_nt(d_gate, gate_mat[:, at_block(j, head)]) + dot_nt(d_up, up_mat[:, at_block(j, head)])
        down_f[...] = down_f[...] + more

    def task_fb(n):
        if n == 0:
            down_f[...] = jnp.zeros_like(down_f)
        loop(tiles_ff // 4, lambda j: feed_back(j + n * (tiles_ff // 4)))

    def norm_mid(r):
        pulled, g_row = rms_pull(h1[r, :], gain(4, width), down_f[r, :])
        gain_add(4, width, g_row)
        d_mid = dout[r, :].astype(F32) + pulled
        d_h1[r, :] = d_mid
        pulled, g_row = rms_pull(out_f[r, :], gain(3, width), d_mid)
        gain_add(3, width, g_row)
        d_outp[r, :] = pulled.astype(BF)

    def task_mid():
        by_rows(64, norm_mid)

    def grad_out(j):
        value = dot(mixed[:, at_block(j, head)].T, d_outp[...]).astype(BF)
        size = heads * head // 32
        high, low = j // (heads // 2), j % (heads // 2)
        for i in range(head // size):
            for t in range(tiles):
                grads[high, low * (head // size) + i, at_out + size * t : at_out + size * (t + 1), :] = value[
                    size * i : size * (i + 1), 128 * t : 128 * (t + 1)
                ]
        d_mixed[j] = dot_nt(d_outp[...], out_mat[at_block(j, head), :]).astype(BF)

    def task_gout():
        loop(blocks, transpose_keys)
        loop(heads, grad_out)

    def attend_back(h):
        dm = d_mixed[h]
        along = jnp.zeros((1, rows), F32)
        for i in range(blocks):
            d_probs = dot_nt(kv[i, :, head : 2 * head], dm)
            scores[i] = d_probs
            p = probs[h, i * rows : (i + 1) * rows, :].astype(F32)
            along = along + jnp.sum(p * d_probs, axis=0, keepdims=True)
        for i in range(blocks):
            low = probs[h, i * rows : (i + 1) * rows, :]
            ds = (low.astype(F32) * (scores[i] - along) * scaling).astype(BF)
            d_raw[i * rows : (i + 1) * rows, :] = ds
            up_f[i] = up_f[i] + dot(ds, queries[h])
            up_f[blocks + i] = up_f[blocks + i] + dot(low, dm)
        dq = dot(keys_t[...], d_raw[...]).T
        turned = turn(dq, cos_t[...], -sin_t[...])
        pulled, g_row = rms_pull(qkv_f[h], gain(1, head), turned)
        gain_add(1, head, g_row)
        d_qkv[:, at_block(h, head)] = pulled.astype(BF)

    def task_ab(n):
        if n == 0:
            up_f[...] = jnp.zeros_like(up_f)
        loop(2, lambda i: attend_back(2 * n + i))

    def task_dks():
        for i in range(blocks):
            dkv[i, :, 0:head] = up_f[i].astype(BF)
            dkv[i, :, head : 2 * head] = up_f[blocks + i].astype(BF)
        held["dk_c"] = [
            send(dkv.at[2 * i + 1 - c], dkv_c.at[i], dk_s.at[i], dk_r.at[i], "c") for i in range(2)
        ]

    def grad_query(h):
        full = dot(attn_in_t[...], d_qkv[:, at_block(h, head)]).astype(BF)
        for n in range(2):
            for i in range(4):
                for t in range(2):
                    grads[n, 4 * h + i, at_q + block * t : at_q + block * (t + 1), :] = full[
                        half * n + block * i : half * n + block * (i + 1), 128 * t : 128 * (t + 1)
                    ]

    def task_dky():
        for copy in held["dk_c"]:
            copy.wait_recv()
        far = (1 - y) * 2 + c
        dkv[far] = (dkv[far].astype(F32) + dkv_c[1 - y].astype(F32)).astype(BF)
        held["dk_y"] = send(dkv.at[far], dkv_y, dk_s.at[2], dk_r.at[2], "y")

    def task_gq():
        loop(heads, grad_query)

    def task_gkv():
        held["dk_y"].wait_recv()
        d_own = dkv[s].astype(F32) + dkv_c[y].astype(F32) + dkv_y[...].astype(F32)
        turned = turn(d_own[:, 0:head], cos_t[...], -sin_t[...])
        pulled, g_row = rms_pull(qkv_f[heads], gain(2, head), turned)
        gain_add(2, head, g_row)
        d_qkv[:, wide : wide + head] = pulled.astype(BF)
        d_qkv[:, wide + head : wide + 2 * head] = d_own[:, head : 2 * head].astype(BF)
        full = dot(attn_in_t[...], d_qkv[:, wide : wide + 2 * head]).astype(BF)
        for n in range(2):
            for j in range(4):
                for i in range(4):
                    grads[n, 4 * j + i, at_kv : at_kv + block, :] = full[
                        half * n + block * i : half * n + block * (i + 1), 128 * j : 128 * (j + 1)
                    ]
        down_f[...] = dot_nt(d_qkv[...], qkv_mat[...])


    def norm_first(r0, r):
        pulled, g_row = rms_pull(tok[r, :].astype(F32), gain(0, width), down_f[r, :])
        gain_add(0, width, g_row)
        pack(1, r0, 64, d_h1[r, :] + pulled)

    def task_last():
        by_number(64, norm_first)
        copy = pltpu.make_async_copy(packed, flat_out.at[:, pl.ds(plan.total, 2 * plan.token_rows)], out_sem.at[0])
        copy.start()
        outs.append(copy)
        for i in range(6):
            for t in range(tiles):
                gain_rows[i * tiles + t : i * tiles + t + 1, :] = gain_acc[i : i + 1, 128 * t : 128 * (t + 1)]
        for p in range(2):
            low = gain_rows[16 * p : 16 * (p + 1), :].astype(BF)
            for h in range(2):
                grads[h, p, plan.gains_at : plan.gains_at + 16, :] = low

    def task_w(way, i):
        {"x": weight_x, "a": weight_a, "b": weight_b, "c": weight_c, "d": weight_d}[way](i)

    named = {
        "init": task_init, "norm": task_norm, "kv": task_kv, "q": task_q, "kvf": task_kvf, "keys": task_keys, "kvt": task_kvt, "at": task_at,
        "outp": task_outp, "ff": task_ff, "down": task_down, "nout": task_nout, "gd": task_gd, "fb": task_fb,
        "mid": task_mid, "gout": task_gout, "ab": task_ab, "dks": task_dks, "dky": task_dky, "gq": task_gq,
        "gkv": task_gkv, "last": task_last,
    }
    for entry in SCHEDULE:
        name, *rest = entry
        if name == "sum":
            steps_of[DIRECT[rest[0]]][rest[1]](rest[0])
        elif name[0] == "w":
            task_w(name[1], *rest)
        else:
            named[name](*rest)
    freed = [hops[k, 0] for k in range(len(plan.chunks))]
    for copy in sends:
        if not any(copy is other for other in freed):
            copy.wait_send()
    for copy in outs:
        copy.wait()


def spread_kernel(plan, flat, *refs):
    (res_o, dtok_o, q_o, k_o, v_o, o_o, g_o, u_o, d_o, gin, gq, gk, ga, gf, go, gains_f) = refs
    step = pl.program_id(0)
    at_down, at_gate, at_up, at_out, at_q, at_kv = plan.starts
    half, block, head, tiles = plan.half, plan.block, plan.head, plan.tiles

    def put(ref, rows, size, col, i, at):
        ref[rows : rows + size, col : col + 128] = flat[i, at : at + size, :].astype(F32)

    for i in range(4):
        for n, ref in enumerate((res_o, dtok_o)):
            for t in range(tiles):
                at = plan.total + n * plan.token_rows + 16 * t
                ref[16 * i : 16 * (i + 1), 128 * t : 128 * (t + 1)] = flat[i, at : at + 16, :]
        for at, ref, size in ((at_down, d_o, plan.ff // 32), (at_out, o_o, plan.heads * head // 32)):
            for t in range(tiles):
                put(ref, size * i, size, 128 * t, i, at + size * t)
        put(g_o, 0, half, 128 * i, i, at_gate)
        put(u_o, 0, half, 128 * i, i, at_up)
        for t in range(2):
            put(q_o, block * i, block, 128 * t, i, at_q + block * t)

    @pl.when(step < 2)
    def _():
        for i in range(4):
            put(k_o, block * i, block, 0, i, at_kv)

    @pl.when(step >= 2)
    def _():
        for i in range(4):
            put(v_o, block * i, block, 0, i, at_kv)

    @pl.when(step == 0)
    def _():
        gains_f[...] = jnp.zeros_like(gains_f)
        for p in range(2):
            lines = flat[p, plan.gains_at : plan.gains_at + 16, :].astype(F32)
            for n in range(16):
                i, t = (16 * p + n) // tiles, (16 * p + n) % tiles
                if i < 6:
                    gains_f[i : i + 1, 128 * t : 128 * (t + 1)] = lines[n : n + 1, :]
        first = lax.axis_index("fsdp") == 0
        values = gains_f[...]
        own = jnp.where(first, values, pltpu.roll(values, half, 1))
        for i, ref in ((0, gin), (3, ga), (4, gf), (5, go)):
            ref[...] = own[i, 0:half]
        own = jnp.where(first, values[:, 0 : head // 2], values[:, head // 2 : head])
        gq[...] = own[1, :]
        gk[...] = own[2, :]


def fused(tokens, d_out, doc_lengths, *weights):
    w_query, w_key, w_value, w_out, w_gate, w_up, w_down = weights[:7]
    gains = weights[7:]
    rows, width = tokens.shape[1:]
    head = 2 * weights[8].shape[0]
    heads = w_query.shape[1] // head
    ff = w_gate.shape[1]
    plan = Plan(rows, width, heads, head, ff)
    freq = jnp.asarray(
        np.power(ROPE_BASE, -2.0 * np.arange(head // 2) / head).astype(np.float32)[None]
    )
    vmem, far = pl.BlockSpec(memory_space=pltpu.VMEM), pl.BlockSpec(memory_space=pl.ANY)
    scratch = lambda *shape: pltpu.VMEM(shape, BF)
    scratch32 = lambda *shape: pltpu.VMEM(shape, F32)
    wide = heads * head
    total, chunks = plan.total, len(plan.chunks)
    dma = lambda *shape: pltpu.SemaphoreType.DMA(shape)
    tiles_ff = ff // head
    scratch_shapes = [
        scratch(width, wide + 2 * head),
        scratch(wide, width),
        scratch(width, ff),
        scratch(width, ff),
        scratch(ff, width),
        scratch32(8, width),
        scratch32(8, width),
        scratch32(8, width),
        scratch(rows, width),
        scratch(width, rows),
        scratch32(heads + 2, rows, head),
        scratch(heads, rows, head),
        scratch(4, rows, 2 * head),
        scratch(head, 4 * rows),
        scratch(head, 4 * rows),
        scratch(heads, 4 * rows, rows),
        scratch(rows, wide),
        scratch32(rows, width),
        scratch32(rows, width),
        scratch(rows, width),
        scratch(width, rows),
        scratch32(tiles_ff, rows, head),
        scratch32(tiles_ff, rows, head),
        scratch(rows, ff),
        scratch32(rows, width),
        scratch(rows, width),
        scratch32(rows, width),
        scratch(rows, width),
        scratch(heads, rows, head),
        scratch(4, rows, 2 * head),
        scratch(2, rows, 2 * head),
        scratch(rows, 2 * head),
        scratch(rows, wide + 2 * head),
        scratch32(rows, 128),
        scratch32(rows, 128),
        scratch(4 * rows, rows),
        scratch32(8, width),
        scratch32(32, 128),
        scratch(2, 16, total, 128),
        scratch(2, 8, total, 128),
        scratch(8, total, 128),
        scratch(4, total, 128),
        scratch(3, total, 128),
        dma(7),
        dma(3 * len(WEIGHTS)),
        dma(3 * len(WEIGHTS)),
        dma(len(WEIGHTS), 7),
        dma(len(WEIGHTS), 7),
        dma(6),
        dma(6),
        dma(3),
        dma(3),
        dma(1),
        dma(1),
        dma(chunks, 16),
        dma(chunks, 16),
        dma(chunks, 2),
        pltpu.SemaphoreType.REGULAR((chunks,)),
        scratch(16, 2 * plan.token_rows, 128),
        dma(1),
    ]
    flat = pl.pallas_call(
        functools.partial(layer_kernel, plan),
        out_shape=jax.ShapeDtypeStruct((16, total + 2 * plan.token_rows, 128), BF),
        in_specs=[pl.BlockSpec(memory_space=pltpu.SMEM)] + [vmem] * 9 + [far] * 7,
        out_specs=far,
        scratch_shapes=scratch_shapes,
        compiler_params=pltpu.CompilerParams(
            collective_id=0, has_side_effects=True, vmem_limit_bytes=55 * 2**20
        ),
        name="layer",
    )(doc_lengths, freq, *gains, tokens[0], d_out[0], w_query, w_key, w_value, w_out, w_gate, w_up, w_down)
    half, block = plan.half, plan.block
    whole = lambda *shape: pl.BlockSpec(shape, lambda p: (0,) * len(shape))
    shape32 = lambda *shape: jax.ShapeDtypeStruct(shape, F32)
    outs = pl.pallas_call(
        functools.partial(spread_kernel, plan),
        grid=(4,),
        out_shape=[
            jax.ShapeDtypeStruct((rows, width), BF),
            jax.ShapeDtypeStruct((rows, width), BF),
            shape32(half, wide),
            shape32(half, head),
            shape32(half, head),
            shape32(wide // 2, width),
            shape32(half, ff),
            shape32(half, ff),
            shape32(ff // 2, width),
            shape32(half),
            shape32(head // 2),
            shape32(head // 2),
            shape32(half),
            shape32(half),
            shape32(half),
        ],
        in_specs=[
            pl.BlockSpec((4, total + 2 * plan.token_rows, 128), lambda p: (p, 0, 0)),
        ],
        out_specs=[
            pl.BlockSpec((rows // 4, width), lambda p: (p, 0)),
            pl.BlockSpec((rows // 4, width), lambda p: (p, 0)),
            pl.BlockSpec((half, head), lambda p: (0, p)),
            pl.BlockSpec((half, 128), lambda p: (0, jnp.minimum(p, 1))),
            pl.BlockSpec((half, 128), lambda p: (0, jnp.maximum(p, 2) - 2)),
            pl.BlockSpec((wide // 8, width), lambda p: (p, 0)),
            pl.BlockSpec((half, ff // 4), lambda p: (0, p)),
            pl.BlockSpec((half, ff // 4), lambda p: (0, p)),
            pl.BlockSpec((ff // 8, width), lambda p: (p, 0)),
            whole(half),
            whole(head // 2),
            whole(head // 2),
            whole(half),
            whole(half),
            whole(half),
        ],
        scratch_shapes=[scratch32(8, width)],
        compiler_params=pltpu.CompilerParams(vmem_limit_bytes=24 * 2**20),
        name="spread",
    )(flat)
    return (outs[0][None], outs[1][None]) + tuple(outs[2:])


def solution(mesh):
    whole = mesh.shape
    small = whole["rep"] == 4 and whole["fsdp"] == 2 and whole["seq"] == 4
    body = fused if small else general
    in_specs = (
        P(("rep", "fsdp"), "seq", None),
        P(("rep", "fsdp"), "seq", None),
        P(("rep", "fsdp"), None),
        P("fsdp", None),
        P("fsdp", None),
        P("fsdp", None),
        P("fsdp", None),
        P("fsdp", None),
        P("fsdp", None),
        P("fsdp", None),
        P("fsdp"),
        P("fsdp"),
        P("fsdp"),
        P("fsdp"),
        P("fsdp"),
        P("fsdp"),
    )
    out_specs = (
        P(("rep", "fsdp"), "seq", None),
        P(("rep", "fsdp"), "seq", None),
        P("fsdp", None),
        P("fsdp", None),
        P("fsdp", None),
        P("fsdp", None),
        P("fsdp", None),
        P("fsdp", None),
        P("fsdp", None),
        P("fsdp"),
        P("fsdp"),
        P("fsdp"),
        P("fsdp"),
        P("fsdp"),
        P("fsdp"),
    )
    return jax.shard_map(body, mesh=mesh, in_specs=in_specs, out_specs=out_specs, check_vma=False)
```

```python
import functools

import jax
import jax.numpy as jnp
import numpy as np
from jax import lax
from jax.experimental import pallas as pl
from jax.experimental.pallas import tpu as pltpu
from jax.sharding import PartitionSpec as P

EPS = 1e-06
ROPE_BASE = 1000000.0
MASKED = -1e30
MESH = pl.DeviceIdType.MESH
BF, F32 = jnp.bfloat16, jnp.float32


def rms_norm(values, gain_vec):
    return values * lax.rsqrt(jnp.mean(values * values, axis=-1, keepdims=True) + EPS) * gain_vec


def rotate(values, angles):
    half_width = values.shape[-1] // 2
    front_half = values[..., :half_width]
    back_half = values[..., half_width:]
    cos_part = jnp.cos(angles)
    sin_part = jnp.sin(angles)
    return jnp.concatenate(
        [
            front_half * cos_part - back_half * sin_part,
            back_half * cos_part + front_half * sin_part,
        ],
        axis=-1,
    )


def frequencies(head_size):
    return jnp.power(
        jnp.float32(ROPE_BASE), -2.0 * jnp.arange(head_size // 2, dtype=jnp.float32) / head_size
    )


def layout(lengths_row, total_len):
    count = lengths_row.shape[0]
    before = jnp.arange(count)[None, :] <= jnp.arange(count)[:, None]
    doc_ends = jnp.sum(jnp.where(before, lengths_row[None, :], 0), axis=1)
    starts = doc_ends - lengths_row
    indices = jnp.arange(total_len, dtype=jnp.int32)
    segment = jnp.sum((indices[:, None] >= doc_ends[None, :]).astype(jnp.int32), axis=1)
    onehot = segment[:, None] == jnp.arange(count, dtype=jnp.int32)[None, :]
    doc_begin = jnp.sum(jnp.where(onehot, starts[None, :], 0), axis=1)
    return (segment, indices - doc_begin)


def matmul(left_side, right_side):
    return jnp.dot(left_side, right_side, preferred_element_type=jnp.float32)


def times_transpose(left_side, right_side):
    return lax.dot_general(
        left_side, right_side, (((1,), (1,)), ((), ())), preferred_element_type=jnp.float32
    )


def transpose_times(left_side, right_side):
    return lax.dot_general(
        left_side, right_side, (((0,), (0,)), ((), ())), preferred_element_type=jnp.float32
    )


def gated(gate_proj, up_proj):
    return jax.nn.gelu(gate_proj, approximate=True) * up_proj


def gather_rows(shard):
    return lax.all_gather(shard, "fsdp", axis=0, tiled=True)


def reduce_rows(grad):
    low = grad.astype(jnp.bfloat16)
    own = lax.psum_scatter(low, "fsdp", scatter_dimension=0, tiled=True)
    return lax.psum(own, ("rep", "seq")).astype(jnp.float32)


def general(
    tokens,
    d_out,
    doc_lengths,
    w_query,
    w_key,
    w_value,
    w_out,
    w_gate,
    w_up,
    w_down,
    g_input,
    g_query,
    g_key,
    g_attn,
    g_ffin,
    g_ffout,
):
    shards = lax.axis_size("fsdp")
    gain_shards = (g_input, g_query, g_key, g_attn, g_ffin, g_ffout)
    widths = [entry.shape[0] for entry in gain_shards]
    starts = [sum(widths[:i]) for i in range(len(widths))]
    gain_rows = lax.all_gather(jnp.concatenate(gain_shards)[None], "fsdp", axis=0, tiled=True)
    gain_input, gain_query, gain_key, gain_attn, gain_ffin, gain_ffout = [
        gain_rows[:, at : at + width].reshape(-1).astype(jnp.float32)
        for at, width in zip(starts, widths)
    ]
    qkv_mat = gather_rows(jnp.concatenate([w_query, w_key, w_value], axis=1))
    out_mat = gather_rows(w_out)
    gate_up_mat = gather_rows(jnp.concatenate([w_gate, w_up], axis=1))
    down_mat = gather_rows(w_down)
    row_count = tokens.shape[1]
    head_size = gain_query.shape[0]
    query_width = w_query.shape[1]
    head_count = query_width // head_size
    ff_width = w_gate.shape[1]
    total_len = row_count * lax.axis_size("seq")
    segment, position = layout(doc_lengths[0], total_len)
    offset = lax.axis_index("seq") * row_count
    query_seg = lax.dynamic_slice_in_dim(segment, offset, row_count)
    query_pos = lax.dynamic_slice_in_dim(position, offset, row_count)
    places = offset + jnp.arange(row_count, dtype=jnp.int32)
    allowed = (query_seg[:, None] == segment[None, :]) & (
        places[:, None] >= jnp.arange(total_len, dtype=jnp.int32)[None, :]
    )
    angles = query_pos.astype(jnp.float32)[:, None] * frequencies(head_size)[None, :]
    scaling = head_size ** (-0.5)
    inputs = tokens[0].astype(jnp.float32)
    cotangent = d_out[0].astype(jnp.float32)
    input_norm, input_pull = jax.vjp(rms_norm, inputs, gain_input)
    attn_input = input_norm.astype(jnp.bfloat16)
    qkv_proj = matmul(attn_input, qkv_mat)
    q_proj = qkv_proj[:, :query_width]
    k_proj = qkv_proj[:, query_width : query_width + head_size]
    v_proj = qkv_proj[:, query_width + head_size :]

    def query_fn(projected, gain_vec):
        shaped = projected.reshape(projected.shape[0], -1, gain_vec.shape[0])
        return rotate(rms_norm(shaped, gain_vec), angles[:, None, :])

    def key_fn(projected, gain_vec):
        return rotate(rms_norm(projected, gain_vec), angles)

    queries, query_pull = jax.vjp(query_fn, q_proj, gain_query)
    keys_own, key_pull = jax.vjp(key_fn, k_proj, gain_key)
    query_rows = queries.astype(jnp.bfloat16).reshape(row_count * head_count, head_size)
    key_value_rows = lax.all_gather(
        jnp.concatenate([keys_own.astype(jnp.bfloat16), v_proj.astype(jnp.bfloat16)], axis=1),
        "seq",
        axis=0,
        tiled=True,
    )
    key_rows = key_value_rows[:, :head_size]
    value_rows = key_value_rows[:, head_size:]

    def masked_scores():
        raw_scores = times_transpose(query_rows, key_rows).reshape(row_count, head_count, total_len)
        return jnp.where(allowed[:, None, :], raw_scores * scaling, MASKED)

    scores = masked_scores()
    top_score = jnp.max(scores, axis=-1, keepdims=True)
    shifted = jnp.exp(scores - top_score)
    denominator = jnp.sum(shifted, axis=-1, keepdims=True)
    log_total = top_score + jnp.log(denominator)
    probs_low = (
        (shifted / denominator).astype(jnp.bfloat16).reshape(row_count * head_count, total_len)
    )
    mixed_rows = (
        matmul(probs_low, value_rows)
        .reshape(row_count, head_count * head_size)
        .astype(jnp.bfloat16)
    )
    out_proj = matmul(mixed_rows, out_mat)
    attn_norm, attn_pull = jax.vjp(rms_norm, out_proj, gain_attn)
    hidden_one = inputs + attn_norm
    ffin_norm, ffin_pull = jax.vjp(rms_norm, hidden_one, gain_ffin)
    ff_input = ffin_norm.astype(jnp.bfloat16)
    gate_up_proj = matmul(ff_input, gate_up_mat)
    gate_proj = gate_up_proj[:, :ff_width]
    up_proj = gate_up_proj[:, ff_width:]
    activated, gated_pull = jax.vjp(gated, gate_proj, up_proj)
    hidden = activated.astype(jnp.bfloat16)
    down_proj = matmul(hidden, down_mat)
    ffout_norm, ffout_pull = jax.vjp(rms_norm, down_proj, gain_ffout)
    result = hidden_one + ffout_norm
    d_down, grad_gffout = ffout_pull(cotangent)
    d_down_low = d_down.astype(jnp.bfloat16)
    total_down = reduce_rows(transpose_times(hidden, d_down_low))
    d_hidden = times_transpose(d_down_low, down_mat)
    d_gate, d_up = gated_pull(d_hidden)
    d_gate_up_low = jnp.concatenate(
        [d_gate.astype(jnp.bfloat16), d_up.astype(jnp.bfloat16)], axis=1
    )
    total_gate_up = reduce_rows(transpose_times(ff_input, d_gate_up_low))
    d_ffin = times_transpose(d_gate_up_low, gate_up_mat)
    d_hidden_part, grad_gffin = ffin_pull(d_ffin)
    d_hidden_one = cotangent + d_hidden_part
    d_out_proj, grad_gattn = attn_pull(d_hidden_one)
    d_out_low = d_out_proj.astype(jnp.bfloat16)
    total_out = reduce_rows(transpose_times(mixed_rows, d_out_low))
    d_mixed = (
        times_transpose(d_out_low, out_mat)
        .astype(jnp.bfloat16)
        .reshape(row_count * head_count, head_size)
    )
    probs_full = jnp.exp(masked_scores() - log_total)
    d_probs = times_transpose(d_mixed, value_rows).reshape(row_count, head_count, total_len)
    row_dot = jnp.sum(probs_full * d_probs, axis=-1, keepdims=True)
    d_raw = (
        (probs_full * (d_probs - row_dot) * scaling)
        .astype(jnp.bfloat16)
        .reshape(row_count * head_count, total_len)
    )
    grad_rows = jnp.concatenate(
        [
            transpose_times(d_raw, query_rows).astype(jnp.bfloat16),
            transpose_times(probs_low, d_mixed).astype(jnp.bfloat16),
        ],
        axis=1,
    )
    d_queries = matmul(d_raw, key_rows).reshape(row_count, head_count, head_size)
    grad_own = lax.psum_scatter(grad_rows, "seq", scatter_dimension=0, tiled=True).astype(
        jnp.float32
    )
    d_q_proj, grad_gquery = query_pull(d_queries)
    d_k_proj, grad_gkey = key_pull(grad_own[:, :head_size])
    d_qkv_low = jnp.concatenate(
        [
            d_q_proj.astype(jnp.bfloat16),
            d_k_proj.astype(jnp.bfloat16),
            grad_own[:, head_size:].astype(jnp.bfloat16),
        ],
        axis=1,
    )
    grad_qkv = transpose_times(attn_input, d_qkv_low)
    d_attn_input = times_transpose(d_qkv_low, qkv_mat)
    d_inputs_part, grad_ginput = input_pull(d_attn_input)
    d_inputs = d_hidden_one + d_inputs_part
    grad_gains = (grad_ginput, grad_gquery, grad_gkey, grad_gattn, grad_gffin, grad_gffout)
    packed_gains = jnp.concatenate([entry.reshape(shards, -1) for entry in grad_gains], axis=1)
    total_qkv = reduce_rows(grad_qkv)
    total_gains = lax.psum_scatter(
        packed_gains.astype(jnp.bfloat16), "fsdp", scatter_dimension=0, tiled=True
    )
    total_gains = lax.psum(total_gains, ("rep", "seq")).astype(jnp.float32)[0]
    return (
        result.astype(jnp.bfloat16)[None],
        d_inputs.astype(jnp.bfloat16)[None],
        total_qkv[:, :query_width],
        total_qkv[:, query_width : query_width + head_size],
        total_qkv[:, query_width + head_size :],
        total_out,
        total_gate_up[:, :ff_width],
        total_gate_up[:, ff_width:],
        total_down,
    ) + tuple(total_gains[at : at + width] for at, width in zip(starts, widths))


def dot(left_side, right_side):
    return jnp.dot(left_side, right_side, preferred_element_type=F32)


def dot_nt(left_side, right_side):
    return lax.dot_general(
        left_side, right_side, (((1,), (1,)), ((), ())), preferred_element_type=F32
    )


def loop(count, step):
    lax.fori_loop(0, count, lambda i, carry: (step(i), carry)[1], 0)


def at_block(i, size):
    return pl.ds(pl.multiple_of(i * size, size), size)


def inverse_rms(values):
    return lax.rsqrt(jnp.mean(values * values, axis=-1, keepdims=True) + EPS)


def rms_pull(values, gain_row, grad):
    inv = inverse_rms(values)
    scaled = values * inv
    pulled = grad * gain_row
    along = jnp.mean(pulled * scaled, axis=-1, keepdims=True)
    return inv * (pulled - scaled * along), jnp.sum(grad * scaled, axis=0, keepdims=True)


def turn(values, cos_part, sin_part):
    half_width = values.shape[-1] // 2
    front, back = values[:, :half_width], values[:, half_width:]
    return jnp.concatenate(
        [front * cos_part - back * sin_part, back * cos_part + front * sin_part], axis=1
    )


class Plan:
    def __init__(self, rows, width, heads, head, ff):
        self.rows, self.width, self.heads, self.head, self.ff = rows, width, heads, head, ff
        self.half = width // 2
        block = self.half // 4
        sizes = (
            ff * width // (32 * 128),
            self.half * ff // (16 * 128),
            self.half * ff // (16 * 128),
            heads * head * width // (32 * 128),
            block * head // 128,
            block + 16,
        )
        self.starts = [sum(sizes[:i]) for i in range(len(sizes))]
        self.chunks = tuple(
            (start + size * a // 10, size * (b - a) // 10)
            for start, size, cuts in zip(self.starts, sizes, CUTS)
            for a, b in zip(cuts, cuts[1:])
        )
        self.block = block
        self.total = sum(sizes)
        self.gains_at = self.total - 16
        self.token_rows = rows * width // (16 * 128)
        self.tiles = width // 128


CUTS = ((0, 2, 6, 10), (0, 5, 10), (0, 5, 10), (0, 5, 10), (0, 10), (0, 10))
FIRST = tuple("yxyxxxxxyxx")
DIRECT = tuple("vddddtdutdd")
WEIGHTS = ((0, 0, 3, "z", None), (0, 3, None, "y", None), (1, 0, None, "y", "rows"), (2, 0, None, "y", "columns"), (3, 0, None, "z", "columns"), (4, 0, None, "z", None))

SCHEDULE = (
    ("init",), ("wx", 1), ("norm",), ("wx", 2), ("wa", 0), ("wx", 3), ("wa", 1), ("wx", 4), ("wa", 2), ("wb", 0),
    ("wb", 1), ("wx", 5), ("wa", 3), ("kv",), ("wb", 2), ("wc", 2), ("q",), ("wa", 4), ("wb", 3), ("wc", 3),
    ("wd", 2), ("kvf", 0), ("wa", 5), ("keys",), ("at", 0), ("wb", 4), ("kvf", 1), ("at", 1), ("kvt",), ("wd", 3),
    ("outp",), ("wc", 4), ("wd", 4), ("ff", 0), ("wb", 5), ("ff", 1), ("down",), ("nout",), ("gd",), ("sum", 0, 0),
    ("sum", 1, 0), ("sum", 2, 0), ("fb", 0), ("sum", 0, 1), ("fb", 1), ("sum", 1, 1), ("sum", 2, 1), ("fb", 2),
    ("fb", 3), ("sum", 3, 0), ("sum", 4, 0), ("sum", 5, 0), ("sum", 6, 0), ("sum", 0, 2), ("mid",), ("gout",),
    ("sum", 3, 1), ("sum", 4, 1), ("sum", 7, 0), ("sum", 8, 0), ("sum", 1, 2), ("sum", 2, 2), ("sum", 5, 1),
    ("sum", 0, 3), ("ab", 0), ("sum", 6, 1), ("sum", 7, 1), ("sum", 8, 1), ("sum", 0, 4), ("sum", 1, 3), ("ab", 1),
    ("sum", 3, 2), ("dks",), ("gq",), ("sum", 9, 0), ("sum", 1, 4), ("sum", 8, 2), ("sum", 0, 5), ("dky",),
    ("sum", 9, 1), ("sum", 3, 3), ("sum", 4, 2), ("sum", 1, 5), ("sum", 0, 6), ("sum", 2, 3), ("gkv",), ("sum", 3, 4),
    ("sum", 0, 7), ("last",), ("sum", 10, 0), ("sum", 0, 8), ("sum", 4, 3), ("sum", 2, 4), ("sum", 5, 2),
    ("sum", 10, 1), ("sum", 1, 6), ("sum", 3, 5), ("sum", 1, 7), ("sum", 5, 3), ("sum", 4, 4), ("sum", 6, 2),
    ("sum", 2, 5), ("sum", 3, 6), ("sum", 5, 4), ("sum", 7, 2), ("sum", 3, 7), ("sum", 8, 3), ("sum", 6, 3),
    ("sum", 4, 5), ("sum", 5, 5), ("sum", 8, 4), ("sum", 2, 6), ("sum", 7, 3), ("sum", 2, 7), ("sum", 6, 4),
    ("sum", 9, 2), ("sum", 5, 6), ("sum", 4, 6), ("sum", 8, 5), ("sum", 7, 4), ("sum", 4, 7), ("sum", 10, 2),
    ("sum", 9, 3), ("sum", 6, 5), ("sum", 5, 7), ("sum", 8, 6), ("sum", 10, 3), ("sum", 7, 5), ("sum", 6, 6),
    ("sum", 9, 4), ("sum", 8, 7), ("sum", 6, 7), ("sum", 10, 4), ("sum", 5, 8), ("sum", 7, 6), ("sum", 5, 9),
    ("sum", 8, 8), ("sum", 9, 5), ("sum", 8, 9), ("sum", 10, 5), ("sum", 7, 7), ("sum", 9, 6), ("sum", 9, 7),
    ("sum", 7, 8), ("sum", 10, 6), ("sum", 7, 9), ("sum", 10, 7),
)


SECOND = {"y": "z", "z": "y"}


def layer_kernel(plan, doc, freq, *refs):
    shards, refs = refs[:6], refs[6:]
    (tok, dout, wq, wk, wv, wo, wg, wu, wd, flat_out) = refs[:10]
    (qkv_mat, out_mat, gate_mat, up_mat, down_mat, gain_own, gain_far, gain_full, attn_in, attn_in_t, qkv_f, queries, kv, keys_t) = refs[10:24]
    (values_t, probs, mixed, out_f, h1, ff_in, ff_in_t, gate_f, up_f, hidden, down_f, d_down, d_h1) = refs[24:37]
    scores = gate_f
    (d_outp, d_mixed, dkv, dkv_c, dkv_y, d_qkv, cos_t, sin_t, d_raw, gain_acc, gain_rows) = refs[37:48]
    (grads, from_c, from_1, from_2, from_z) = refs[48:53]
    (w_local, wx_s, wx_r, wf_s, wf_r, kv_s, kv_r, dk_s, dk_r, gs_, gr_, rs_s, rs_r, fin, free, packed, out_sem) = refs[53:70]
    rows, width, heads, head, ff = plan.rows, plan.width, plan.heads, plan.head, plan.ff
    half, block = plan.half, plan.block
    rep, x, s = lax.axis_index("rep"), lax.axis_index("fsdp"), lax.axis_index("seq")
    y, c = s // 2, s % 2
    zh, zl = rep // 2, rep % 2
    to = {
        "x": (rep, 1 - x, s),
        "c": (rep, x, y * 2 + 1 - c),
        "y": (rep, x, (1 - y) * 2 + c),
        "z": (zh * 2 + 1 - zl, x, s),
        "z2": ((1 - zh) * 2 + zl, x, s),
        "z3": ((1 - zh) * 2 + 1 - zl, x, s),
    }
    sends = []

    def send(source, target, send_sem, recv_sem, axis):
        copy = pltpu.make_async_remote_copy(
            src_ref=source,
            dst_ref=target,
            send_sem=send_sem,
            recv_sem=recv_sem,
            device_id=to[axis],
            device_id_type=MESH,
        )
        copy.start()
        sends.append(copy)
        return copy

    parts = (
        ((wq, 0), (wk, heads * head), (wv, heads * head + head)),
        ((wo, 0),),
        ((wg, 0),),
        ((wu, 0),),
        ((wd, 0),),
    )
    mats = (qkv_mat, out_mat, gate_mat, up_mat, down_mat)
    locals_of, x_of, f_of = {}, {}, {}
    slot = 0
    slots = []
    for i, (mat, entries) in enumerate(zip(mats, parts)):
        shard_rows = mat.shape[0] // 2
        locals_of[i] = []
        for ref, col in entries:
            copy = pltpu.make_async_copy(
                ref, mat.at[pl.ds(x * shard_rows, shard_rows), pl.ds(col, ref.shape[1])], w_local.at[slot]
            )
            copy.start()
            locals_of[i].append(copy)
            slot += 1

    barrier = pltpu.get_barrier_semaphore()
    for axis in to:
        pl.semaphore_signal(barrier, inc=1, device_id=to[axis], device_id_type=MESH)
    pl.semaphore_wait(barrier, len(to))

    for m, *_ in WEIGHTS:
        slots.append(sum(len(parts[n]) for n, *_ in WEIGHTS[: len(slots)]))

    def region(i, far_bit, far_z):
        m, first, last, axis, cut = WEIGHTS[i]
        bit = y if axis == "y" else zl
        quarter = (1 - bit if far_bit else bit) * 2 + c
        low = zl if axis == "y" else y
        low = 1 - low if far_z else low
        size, columns = mats[m].shape[0] // 8, mats[m].shape[1]
        skip, size, at = 16 * first, (size if last is None else 16 * last) - 16 * first, quarter * size
        if cut == "rows":
            return at + low * (size // 2), size // 2, None
        if cut == "columns":
            return at + skip, size, at_block(low, columns // 2)
        return at + skip, size, None

    def weight_x(i):
        shard_rows = mats[WEIGHTS[i][0]].shape[0] // 2
        at, size, columns = region(i, False, False)
        x_of[i] = []
        for j, (ref, col) in enumerate(parts[WEIGHTS[i][0]]):
            here = pl.ds(0, ref.shape[1]) if columns is None else columns
            there = pl.ds(col, ref.shape[1]) if columns is None else columns
            x_of[i].append(
                send(
                    ref.at[pl.ds(at, size), here],
                    mats[WEIGHTS[i][0]].at[pl.ds(x * shard_rows + at, size), there],
                    wx_s.at[slots[i] + j],
                    wx_r.at[slots[i] + j],
                    "x",
                )
            )

    def weight_forward(i, n, axis, far_bit, far_z=False):
        shard_rows = mats[WEIGHTS[i][0]].shape[0] // 2
        at, size, columns = region(i, far_bit, far_z)
        where = mats[WEIGHTS[i][0]].at[pl.ds((1 - x) * shard_rows + at, size)]
        if columns is not None:
            where = mats[WEIGHTS[i][0]].at[pl.ds((1 - x) * shard_rows + at, size), columns]
        f_of[i, n] = send(where, where, wf_s.at[i, n], wf_r.at[i, n], axis)

    def weight_a(i):
        for copy in x_of[i]:
            copy.wait_recv()
        weight_forward(i, 0, WEIGHTS[i][3], False)
        if WEIGHTS[i][4]:
            weight_forward(i, 3, SECOND[WEIGHTS[i][3]], False)
        weight_forward(i, 1, "c", False)

    def weight_b(i):
        f_of[i, 0].wait_recv()
        if WEIGHTS[i][4]:
            weight_forward(i, 4, SECOND[WEIGHTS[i][3]], True)
        weight_forward(i, 2, "c", True)

    def weight_c(i):
        f_of[i, 3].wait_recv()
        weight_forward(i, 5, "c", False, True)

    def weight_d(i):
        f_of[i, 4].wait_recv()
        weight_forward(i, 6, "c", True, True)

    def weight_done(m):
        for i in range(len(WEIGHTS)):
            if WEIGHTS[i][0] == m:
                for n in (1, 2, 5, 6) if WEIGHTS[i][4] else (1, 2):
                    f_of[i, n].wait_recv()
        for copy in locals_of[m]:
            copy.wait()

    mine_c, mine_y = c * 8, c * 8 + y * 4
    gathered = from_c.at[1 - x]
    piece_of = lambda high, low: mine_y + 2 * high + low
    hops = {}

    def hop(k, n, source, target, axis):
        hops[k, n] = send(source, target, rs_s.at[k, n], rs_r.at[k, n], axis)

    def span(k):
        return pl.ds(*plan.chunks[k])

    def total_of(k, m, last=False, z=()):
        r = span(k)
        place = y * 4 + m
        value = grads[x, mine_c + place, r, :].astype(F32) + from_c[x, place, r, :].astype(F32)
        first = place if FIRST[k] == "x" else 4 * x + m
        value = value + from_1[first, r, :].astype(F32) + from_2[m, r, :].astype(F32)
        for i in z:
            value = value + from_z[i, r, :].astype(F32)
        if last:
            gathered[place, r, :] = value.astype(BF)
        else:
            grads[x, mine_c + place, r, :] = value.astype(BF)

    def add_core(k, h, place, first=None):
        r = span(k)
        value = grads[h, mine_c + place, r, :].astype(F32) + from_c[h, place, r, :].astype(F32)
        if first is not None:
            value = value + from_1[first, r, :].astype(F32)
        grads[h, mine_c + place, r, :] = value.astype(BF)

    z_ways = (("z", zh, 1 - zl), ("z2", 1 - zh, zl), ("z3", 1 - zh, 1 - zl))

    def sum_c(k):
        r = span(k)
        hop(k, 0, grads.at[:, pl.ds((1 - c) * 8, 8), r], from_c.at[:, :, r], "c")

    def sum_1(k):
        r = span(k)
        hops[k, 0].wait_recv()
        if FIRST[k] == "x":
            loop(8, lambda i: add_core(k, 1 - x, i))
            for i in range(2):
                hop(k, (1, 12)[i], grads.at[1 - x, pl.ds(mine_c + 4 * i, 4), r], from_1.at[pl.ds(4 * i, 4), r], "x")
        else:
            far = (1 - y) * 4
            for h in range(2):
                loop(4, lambda i: add_core(k, h, far + i))
                hop(k, (1, 12)[h], grads.at[h, pl.ds(mine_c + far, 4), r], from_1.at[pl.ds(4 * h, 4), r], "y")

    def sum_2(k):
        r = span(k)
        hops[k, 1].wait_recv()
        hops[k, 12].wait_recv()
        hops[k, 0].wait_send()
        pl.semaphore_signal(free.at[k], inc=1, device_id=to["c"], device_id_type=MESH)
        if FIRST[k] == "x":
            far = (1 - y) * 4
            loop(4, lambda i: add_core(k, x, far + i, far + i))
            hop(k, 2, grads.at[x, pl.ds(mine_c + far, 4), r], from_2.at[:, r], "y")
        else:
            loop(4, lambda i: add_core(k, 1 - x, y * 4 + i, 4 * (1 - x) + i))
            hop(k, 2, grads.at[1 - x, pl.ds(mine_y, 4), r], from_2.at[:, r], "x")

    def sum_z(k):
        r = span(k)
        hops[k, 2].wait_recv()
        for i, (axis, high, low) in enumerate(z_ways):
            total_of(k, 2 * high + low)
            hop(k, 3 + i, grads.at[x, piece_of(high, low), r], from_z.at[i, r], axis)

    def sum_z1(k):
        r = span(k)
        hops[k, 2].wait_recv()
        for i in range(2):
            total_of(k, 2 * i + 1 - zl)
            hop(k, 3 + i, grads.at[x, piece_of(i, 1 - zl), r], from_z.at[i, r], "z")

    def sum_z2(k):
        r = span(k)
        hops[k, 3].wait_recv()
        hops[k, 4].wait_recv()
        total_of(k, 2 * (1 - zh) + zl, z=(1 - zh,))
        hop(k, 5, grads.at[x, piece_of(1 - zh, zl), r], from_z.at[2, r], "z2")

    def back_z2(k):
        hops[k, 5].wait_recv()
        near = 2 * zh + zl
        total_of(k, near, last=True, z=(zh, 2))
        where = gathered.at[near + y * 4, span(k)]
        hop(k, 6, where, where, "z2")

    def back_z1(k):
        hops[k, 6].wait_recv()
        for i in range(2):
            where = gathered.at[y * 4 + 2 * i + zl, span(k)]
            hop(k, 7 + i, where, where, "z")

    def back_z(k):
        r = span(k)
        for i in range(3):
            hops[k, 3 + i].wait_recv()
        near = 2 * zh + zl
        total_of(k, near, last=True, z=(0, 1, 2))
        where = gathered.at[near + y * 4, r]
        for i, (axis, _, _) in enumerate(z_ways):
            hop(k, 6 + i, where, where, axis)

    def back_y(k):
        for i in range(3) if DIRECT[k] == "d" else (1, 2):
            hops[k, 6 + i].wait_recv()
        where = gathered.at[pl.ds(y * 4, 4), span(k)]
        hop(k, 9, where, where, "y")
        pl.semaphore_wait(free.at[k], 1)
        hop(k, 10, where, grads.at[x, pl.ds(mine_c + y * 4, 4), span(k)], "c")

    def back_c(k):
        hops[k, 9].wait_recv()
        where = gathered.at[pl.ds((1 - y) * 4, 4), span(k)]
        hop(k, 11, where, grads.at[x, pl.ds(mine_c + (1 - y) * 4, 4), span(k)], "c")

    outs = []

    def finish(k):
        hops[k, 10].wait_recv()
        if (k, 11) in hops:
            hops[k, 11].wait_recv()
        r = span(k)
        for i, source, first in ((0, gathered, mine_c), (1, grads.at[x, pl.ds((1 - c) * 8, 8)], (1 - c) * 8)):
            copy = pltpu.make_async_copy(source.at[:, r], flat_out.at[pl.ds(first, 8), r], fin.at[k, i])
            copy.start()
            outs.append(copy)

    def home_y(k):
        for i in range(3, 6) if DIRECT[k] == "v" else (5,):
            hops[k, i].wait_recv()
        near = 2 * zh + zl
        total_of(k, near, last=True, z=(0, 1, 2) if DIRECT[k] == "v" else (zh, 2))
        where = gathered.at[near + y * 4, span(k)]
        hop(k, 9, where, where, "y")

    def home_z2(k):
        hops[k, 9].wait_recv()
        for i in range(2):
            where = gathered.at[4 * i + 2 * zh + zl, span(k)]
            hop(k, 6 + i, where, where, "z2")

    def home_z1(k):
        hops[k, 6].wait_recv()
        hops[k, 7].wait_recv()
        for i, n in enumerate((8, 13, 14, 15)):
            where = gathered.at[2 * i + zl, span(k)]
            hop(k, n, where, where, "z")

    def home_c(k):
        for n in (8, 13, 14, 15):
            hops[k, n].wait_recv()
        pl.semaphore_wait(free.at[k], 1)
        hop(k, 10, gathered.at[:, span(k)], grads.at[x, pl.ds(mine_c, 8), span(k)], "c")

    ends_with = (back_y, back_c, finish)
    home = (home_y, home_z2, home_z1, home_c, finish)
    steps_of = {
        "d": (sum_c, sum_1, sum_2, sum_z, back_z) + ends_with,
        "t": (sum_c, sum_1, sum_2, sum_z1, sum_z2, back_z2, back_z1) + ends_with,
        "u": (sum_c, sum_1, sum_2, sum_z1, sum_z2) + home,
        "v": (sum_c, sum_1, sum_2, sum_z) + home,
    }

    ends = [doc[0, 0]]
    for i in range(1, doc.shape[1]):
        ends.append(ends[-1] + doc[0, i])

    def start_of(places):
        start = jnp.zeros_like(places)
        for i, end in enumerate(ends):
            start = jnp.where(places >= end, end, start)
        return start

    gain_own[...] = jnp.zeros_like(gain_own)
    for i, ref in enumerate(shards):
        gain_own[i : i + 1, 0 : ref.shape[0]] = ref[...].astype(F32).reshape(1, ref.shape[0])
    gain_copy = send(gain_own, gain_far, gs_.at[0], gr_.at[0], "x")
    weight_x(0)
    place_row = s * rows + lax.broadcasted_iota(jnp.int32, (1, rows), 1)
    start_row = start_of(place_row)
    gain = lambda i, size: gain_full[i : i + 1, 0:size]
    scaling = head ** (-0.5)
    blocks = 4
    root = 0.7978845608028654
    tiles_ff = ff // head
    tiles = plan.tiles
    wide = heads * head
    at_down, at_gate, at_up, at_out, at_q, at_kv = plan.starts
    held = {}

    def pack(n, r0, size, value):
        value = value.astype(BF)
        for i in range(size // 16):
            for t in range(tiles):
                at = n * plan.token_rows + 16 * t
                packed[r0 // 16 + i, at : at + 16, :] = value[16 * i : 16 * (i + 1), 128 * t : 128 * (t + 1)]

    def by_number(size, step):
        loop(rows // size, lambda i: step(i * size, pl.ds(pl.multiple_of(i * size, size), size)))

    def by_rows(size, step):
        loop(rows // size, lambda i: step(pl.ds(pl.multiple_of(i * size, size), size)))

    def task_init():
        place_col = s * rows + lax.broadcasted_iota(jnp.int32, (rows, 128), 0)
        angles = (place_col - start_of(place_col)).astype(F32) * freq[...]
        cos_t[...] = jnp.cos(angles)
        sin_t[...] = jnp.sin(angles)
        none = jnp.zeros((16, 128), BF)
        for h in range(2):
            for p in range(2, 16):
                grads[h, p, plan.gains_at : plan.gains_at + 16, :] = none
        gain_rows[...] = jnp.zeros_like(gain_rows)
        gain_acc[...] = jnp.zeros_like(gain_acc)

    def norm_in(r):
        v = tok[r, :].astype(F32)
        attn_in[r, :] = (v * inverse_rms(v) * gain(0, width)).astype(BF)

    def task_norm():
        gain_copy.wait_recv()
        own, far = gain_own[...], gain_far[...]
        first, second = jnp.where(x == 0, own, far), jnp.where(x == 0, far, own)
        line = lax.broadcasted_iota(jnp.int32, own.shape, 0)
        short = (line == 1) | (line == 2)
        moved = jnp.where(short, pltpu.roll(second, head // 2, 1), pltpu.roll(second, half, 1))
        gain_full[...] = first + moved
        by_rows(64, norm_in)
        attn_in_t[...] = attn_in[...].T

    def project(j):
        qkv_f[j] = dot(attn_in[...], qkv_mat[:, at_block(j, head)])

    def task_kv():
        weight_done(0)
        project(heads)
        project(heads + 1)
        k_f = qkv_f[heads]
        kv[s, :, 0:head] = turn(k_f * inverse_rms(k_f) * gain(2, head), cos_t[...], sin_t[...]).astype(BF)
        kv[s, :, head : 2 * head] = qkv_f[heads + 1].astype(BF)
        for n in range(2):
            where = kv.at[s, :, n * head : (n + 1) * head]
            held["y", n] = send(where, where, kv_s.at[n], kv_r.at[n], "y")
            held["c", n] = send(where, where, kv_s.at[2 + n], kv_r.at[2 + n], "c")

    def turn_query(h):
        project(h)
        q_f = qkv_f[h]
        queries[h] = turn(q_f * inverse_rms(q_f) * gain(1, head), cos_t[...], sin_t[...]).astype(BF)

    def task_q():
        loop(heads, turn_query)

    def task_kvf(n):
        held["y", n].wait_recv()
        where = kv.at[(1 - y) * 2 + c, :, n * head : (n + 1) * head]
        held["cc", n] = send(where, where, kv_s.at[4 + n], kv_r.at[4 + n], "c")

    def transpose_keys(i):
        keys_t[:, at_block(i, rows)] = kv[i, :, 0:head].T

    def transpose_values(i):
        values_t[:, at_block(i, rows)] = kv[i, :, head : 2 * head].T

    def task_keys():
        held["c", 0].wait_recv()
        held["cc", 0].wait_recv()

    def task_kvt():
        held["c", 1].wait_recv()
        held["cc", 1].wait_recv()
        loop(blocks, transpose_values)

    def attend(h):
        q = queries[h]
        top = jnp.full((1, rows), MASKED, F32)
        for i in range(blocks):
            u = i * rows + lax.broadcasted_iota(jnp.int32, (rows, rows), 0)
            raw = dot_nt(kv[i, :, 0:head], q) * scaling
            raw = jnp.where((u <= place_row) & (u >= start_row), raw, MASKED)
            scores[i] = raw
            top = jnp.maximum(top, jnp.max(raw, axis=0, keepdims=True))
        denominator = jnp.zeros((1, rows), F32)
        for i in range(blocks):
            e = jnp.exp(scores[i] - top)
            scores[i] = e
            denominator = denominator + jnp.sum(e, axis=0, keepdims=True)
        inv = 1.0 / denominator
        for i in range(blocks):
            probs[h, i * rows : (i + 1) * rows, :] = (scores[i] * inv).astype(BF)

    def mix(h):
        mixed[:, at_block(h, head)] = dot(values_t[...], probs[h]).T.astype(BF)

    def task_at(n):
        loop(2, lambda i: attend(2 * n + i))

    def norm_ff(r):
        o = out_f[r, :]
        h = tok[r, :].astype(F32) + o * inverse_rms(o) * gain(3, width)
        h1[r, :] = h
        ff_in[r, :] = (h * inverse_rms(h) * gain(4, width)).astype(BF)

    def task_outp():
        loop(heads, mix)
        weight_done(1)
        out_f[...] = dot(mixed[...], out_mat[...])
        by_rows(64, norm_ff)
        ff_in_t[...] = ff_in[...].T

    def feed(j):
        g = dot(ff_in[...], gate_mat[:, at_block(j, head)])
        u = dot(ff_in[...], up_mat[:, at_block(j, head)])
        gate_f[j] = g
        up_f[j] = u
        t = jnp.tanh(root * (g + 0.044715 * (g * g * g)))
        hidden[:, at_block(j, head)] = (0.5 * g * (1.0 + t) * u).astype(BF)

    def task_ff(n):
        if n == 0:
            weight_done(2)
            weight_done(3)
        loop(tiles_ff // 2, lambda j: feed(j + n * (tiles_ff // 2)))

    def task_down():
        weight_done(4)
        down_f[...] = dot(hidden[...], down_mat[...])

    def gain_add(i, size, row):
        gain_acc[i : i + 1, 0:size] = gain_acc[i : i + 1, 0:size] + row

    def norm_out(r0, r):
        d = down_f[r, :]
        pack(0, r0, 64, h1[r, :] + d * inverse_rms(d) * gain(5, width))
        pulled, g_row = rms_pull(d, gain(5, width), dout[r, :].astype(F32))
        d_down[r, :] = pulled.astype(BF)
        gain_add(5, width, g_row)

    def task_nout():
        by_number(64, norm_out)

    def grad_down(j):
        value = dot(hidden[:, at_block(j, head)].T, d_down[...]).astype(BF)
        high, low = j // (tiles_ff // 2), j % (tiles_ff // 2)
        size = ff // 32
        for i in range(head // size):
            for t in range(tiles):
                grads[high, low * (head // size) + i, at_down + size * t : at_down + size * (t + 1), :] = value[
                    size * i : size * (i + 1), 128 * t : 128 * (t + 1)
                ]

    def task_gd():
        loop(tiles_ff, grad_down)

    def feed_back(j):
        d_hidden = dot_nt(d_down[...], down_mat[at_block(j, head), :])
        g, u = gate_f[j], up_f[j]
        t = jnp.tanh(root * (g + 0.044715 * (g * g * g)))
        act = 0.5 * g * (1.0 + t)
        slope = 0.5 * (1.0 + t) + 0.5 * g * (1.0 - t * t) * (root * (1.0 + 3 * 0.044715 * (g * g)))
        d_gate = (d_hidden * u * slope).astype(BF)
        d_up = (d_hidden * act).astype(BF)
        for at, value in ((at_gate, d_gate), (at_up, d_up)):
            full = dot(ff_in_t[...], value).astype(BF)
            for h in range(2):
                for t_ in range(2):
                    grads[h, 2 * j + t_, at : at + half, :] = full[half * h : half * (h + 1), 128 * t_ : 128 * (t_ + 1)]
        more = dot_nt(d_gate, gate_mat[:, at_block(j, head)]) + dot_nt(d_up, up_mat[:, at_block(j, head)])
        down_f[...] = down_f[...] + more

    def task_fb(n):
        if n == 0:
            down_f[...] = jnp.zeros_like(down_f)
        loop(tiles_ff // 4, lambda j: feed_back(j + n * (tiles_ff // 4)))

    def norm_mid(r):
        pulled, g_row = rms_pull(h1[r, :], gain(4, width), down_f[r, :])
        gain_add(4, width, g_row)
        d_mid = dout[r, :].astype(F32) + pulled
        d_h1[r, :] = d_mid
        pulled, g_row = rms_pull(out_f[r, :], gain(3, width), d_mid)
        gain_add(3, width, g_row)
        d_outp[r, :] = pulled.astype(BF)

    def task_mid():
        by_rows(64, norm_mid)

    def grad_out(j):
        value = dot(mixed[:, at_block(j, head)].T, d_outp[...]).astype(BF)
        size = heads * head // 32
        high, low = j // (heads // 2), j % (heads // 2)
        for i in range(head // size):
            for t in range(tiles):
                grads[high, low * (head // size) + i, at_out + size * t : at_out + size * (t + 1), :] = value[
                    size * i : size * (i + 1), 128 * t : 128 * (t + 1)
                ]
        d_mixed[j] = dot_nt(d_outp[...], out_mat[at_block(j, head), :]).astype(BF)

    def task_gout():
        loop(blocks, transpose_keys)
        loop(heads, grad_out)

    def attend_back(h):
        dm = d_mixed[h]
        along = jnp.zeros((1, rows), F32)
        for i in range(blocks):
            d_probs = dot_nt(kv[i, :, head : 2 * head], dm)
            scores[i] = d_probs
            p = probs[h, i * rows : (i + 1) * rows, :].astype(F32)
            along = along + jnp.sum(p * d_probs, axis=0, keepdims=True)
        for i in range(blocks):
            low = probs[h, i * rows : (i + 1) * rows, :]
            ds = (low.astype(F32) * (scores[i] - along) * scaling).astype(BF)
            d_raw[i * rows : (i + 1) * rows, :] = ds
            up_f[i] = up_f[i] + dot(ds, queries[h])
            up_f[blocks + i] = up_f[blocks + i] + dot(low, dm)
        dq = dot(keys_t[...], d_raw[...]).T
        turned = turn(dq, cos_t[...], -sin_t[...])
        pulled, g_row = rms_pull(qkv_f[h], gain(1, head), turned)
        gain_add(1, head, g_row)
        d_qkv[:, at_block(h, head)] = pulled.astype(BF)

    def task_ab(n):
        if n == 0:
            up_f[...] = jnp.zeros_like(up_f)
        loop(2, lambda i: attend_back(2 * n + i))

    def task_dks():
        for i in range(blocks):
            dkv[i, :, 0:head] = up_f[i].astype(BF)
            dkv[i, :, head : 2 * head] = up_f[blocks + i].astype(BF)
        held["dk_c"] = [
            send(dkv.at[2 * i + 1 - c], dkv_c.at[i], dk_s.at[i], dk_r.at[i], "c") for i in range(2)
        ]

    def grad_query(h):
        full = dot(attn_in_t[...], d_qkv[:, at_block(h, head)]).astype(BF)
        for n in range(2):
            for i in range(4):
                for t in range(2):
                    grads[n, 4 * h + i, at_q + block * t : at_q + block * (t + 1), :] = full[
                        half * n + block * i : half * n + block * (i + 1), 128 * t : 128 * (t + 1)
                    ]

    def task_dky():
        for copy in held["dk_c"]:
            copy.wait_recv()
        far = (1 - y) * 2 + c
        dkv[far] = (dkv[far].astype(F32) + dkv_c[1 - y].astype(F32)).astype(BF)
        held["dk_y"] = send(dkv.at[far], dkv_y, dk_s.at[2], dk_r.at[2], "y")

    def task_gq():
        loop(heads, grad_query)

    def task_gkv():
        held["dk_y"].wait_recv()
        d_own = dkv[s].astype(F32) + dkv_c[y].astype(F32) + dkv_y[...].astype(F32)
        turned = turn(d_own[:, 0:head], cos_t[...], -sin_t[...])
        pulled, g_row = rms_pull(qkv_f[heads], gain(2, head), turned)
        gain_add(2, head, g_row)
        d_qkv[:, wide : wide + head] = pulled.astype(BF)
        d_qkv[:, wide + head : wide + 2 * head] = d_own[:, head : 2 * head].astype(BF)
        full = dot(attn_in_t[...], d_qkv[:, wide : wide + 2 * head]).astype(BF)
        for n in range(2):
            for j in range(4):
                for i in range(4):
                    grads[n, 4 * j + i, at_kv : at_kv + block, :] = full[
                        half * n + block * i : half * n + block * (i + 1), 128 * j : 128 * (j + 1)
                    ]
        down_f[...] = dot_nt(d_qkv[...], qkv_mat[...])


    def norm_first(r0, r):
        pulled, g_row = rms_pull(tok[r, :].astype(F32), gain(0, width), down_f[r, :])
        gain_add(0, width, g_row)
        pack(1, r0, 64, d_h1[r, :] + pulled)

    def task_last():
        by_number(64, norm_first)
        copy = pltpu.make_async_copy(packed, flat_out.at[:, pl.ds(plan.total, 2 * plan.token_rows)], out_sem.at[0])
        copy.start()
        outs.append(copy)
        for i in range(6):
            for t in range(tiles):
                gain_rows[i * tiles + t : i * tiles + t + 1, :] = gain_acc[i : i + 1, 128 * t : 128 * (t + 1)]
        for p in range(2):
            low = gain_rows[16 * p : 16 * (p + 1), :].astype(BF)
            for h in range(2):
                grads[h, p, plan.gains_at : plan.gains_at + 16, :] = low

    def task_w(way, i):
        {"x": weight_x, "a": weight_a, "b": weight_b, "c": weight_c, "d": weight_d}[way](i)

    named = {
        "init": task_init, "norm": task_norm, "kv": task_kv, "q": task_q, "kvf": task_kvf, "keys": task_keys, "kvt": task_kvt, "at": task_at,
        "outp": task_outp, "ff": task_ff, "down": task_down, "nout": task_nout, "gd": task_gd, "fb": task_fb,
        "mid": task_mid, "gout": task_gout, "ab": task_ab, "dks": task_dks, "dky": task_dky, "gq": task_gq,
        "gkv": task_gkv, "last": task_last,
    }
    for entry in SCHEDULE:
        name, *rest = entry
        if name == "sum":
            steps_of[DIRECT[rest[0]]][rest[1]](rest[0])
        elif name[0] == "w":
            task_w(name[1], *rest)
        else:
            named[name](*rest)
    freed = [hops[k, 0] for k in range(len(plan.chunks))]
    for copy in sends:
        if not any(copy is other for other in freed):
            copy.wait_send()
    for copy in outs:
        copy.wait()


def spread_kernel(plan, flat, *refs):
    (res_o, dtok_o, q_o, k_o, v_o, o_o, g_o, u_o, d_o, gin, gq, gk, ga, gf, go, gains_f) = refs
    step = pl.program_id(0)
    at_down, at_gate, at_up, at_out, at_q, at_kv = plan.starts
    half, block, head, tiles = plan.half, plan.block, plan.head, plan.tiles

    def put(ref, rows, size, col, i, at):
        ref[rows : rows + size, col : col + 128] = flat[i, at : at + size, :].astype(F32)

    for i in range(4):
        for n, ref in enumerate((res_o, dtok_o)):
            for t in range(tiles):
                at = plan.total + n * plan.token_rows + 16 * t
                ref[16 * i : 16 * (i + 1), 128 * t : 128 * (t + 1)] = flat[i, at : at + 16, :]
        for at, ref, size in ((at_down, d_o, plan.ff // 32), (at_out, o_o, plan.heads * head // 32)):
            for t in range(tiles):
                put(ref, size * i, size, 128 * t, i, at + size * t)
        put(g_o, 0, half, 128 * i, i, at_gate)
        put(u_o, 0, half, 128 * i, i, at_up)
        for t in range(2):
            put(q_o, block * i, block, 128 * t, i, at_q + block * t)

    @pl.when(step < 2)
    def _():
        for i in range(4):
            put(k_o, block * i, block, 0, i, at_kv)

    @pl.when(step >= 2)
    def _():
        for i in range(4):
            put(v_o, block * i, block, 0, i, at_kv)

    @pl.when(step == 0)
    def _():
        gains_f[...] = jnp.zeros_like(gains_f)
        for p in range(2):
            lines = flat[p, plan.gains_at : plan.gains_at + 16, :].astype(F32)
            for n in range(16):
                i, t = (16 * p + n) // tiles, (16 * p + n) % tiles
                if i < 6:
                    gains_f[i : i + 1, 128 * t : 128 * (t + 1)] = lines[n : n + 1, :]
        first = lax.axis_index("fsdp") == 0
        values = gains_f[...]
        own = jnp.where(first, values, pltpu.roll(values, half, 1))
        for i, ref in ((0, gin), (3, ga), (4, gf), (5, go)):
            ref[...] = own[i, 0:half]
        own = jnp.where(first, values[:, 0 : head // 2], values[:, head // 2 : head])
        gq[...] = own[1, :]
        gk[...] = own[2, :]


def fused(tokens, d_out, doc_lengths, *weights):
    w_query, w_key, w_value, w_out, w_gate, w_up, w_down = weights[:7]
    gains = weights[7:]
    rows, width = tokens.shape[1:]
    head = 2 * weights[8].shape[0]
    heads = w_query.shape[1] // head
    ff = w_gate.shape[1]
    plan = Plan(rows, width, heads, head, ff)
    freq = jnp.asarray(
        np.power(ROPE_BASE, -2.0 * np.arange(head // 2) / head).astype(np.float32)[None]
    )
    vmem, far = pl.BlockSpec(memory_space=pltpu.VMEM), pl.BlockSpec(memory_space=pl.ANY)
    scratch = lambda *shape: pltpu.VMEM(shape, BF)
    scratch32 = lambda *shape: pltpu.VMEM(shape, F32)
    wide = heads * head
    total, chunks = plan.total, len(plan.chunks)
    dma = lambda *shape: pltpu.SemaphoreType.DMA(shape)
    tiles_ff = ff // head
    scratch_shapes = [
        scratch(width, wide + 2 * head),
        scratch(wide, width),
        scratch(width, ff),
        scratch(width, ff),
        scratch(ff, width),
        scratch32(8, width),
        scratch32(8, width),
        scratch32(8, width),
        scratch(rows, width),
        scratch(width, rows),
        scratch32(heads + 2, rows, head),
        scratch(heads, rows, head),
        scratch(4, rows, 2 * head),
        scratch(head, 4 * rows),
        scratch(head, 4 * rows),
        scratch(heads, 4 * rows, rows),
        scratch(rows, wide),
        scratch32(rows, width),
        scratch32(rows, width),
        scratch(rows, width),
        scratch(width, rows),
        scratch32(tiles_ff, rows, head),
        scratch32(tiles_ff, rows, head),
        scratch(rows, ff),
        scratch32(rows, width),
        scratch(rows, width),
        scratch32(rows, width),
        scratch(rows, width),
        scratch(heads, rows, head),
        scratch(4, rows, 2 * head),
        scratch(2, rows, 2 * head),
        scratch(rows, 2 * head),
        scratch(rows, wide + 2 * head),
        scratch32(rows, 128),
        scratch32(rows, 128),
        scratch(4 * rows, rows),
        scratch32(8, width),
        scratch32(32, 128),
        scratch(2, 16, total, 128),
        scratch(2, 8, total, 128),
        scratch(8, total, 128),
        scratch(4, total, 128),
        scratch(3, total, 128),
        dma(7),
        dma(3 * len(WEIGHTS)),
        dma(3 * len(WEIGHTS)),
        dma(len(WEIGHTS), 7),
        dma(len(WEIGHTS), 7),
        dma(6),
        dma(6),
        dma(3),
        dma(3),
        dma(1),
        dma(1),
        dma(chunks, 16),
        dma(chunks, 16),
        dma(chunks, 2),
        pltpu.SemaphoreType.REGULAR((chunks,)),
        scratch(16, 2 * plan.token_rows, 128),
        dma(1),
    ]
    flat = pl.pallas_call(
        functools.partial(layer_kernel, plan),
        out_shape=pltpu.VMEM((16, total + 2 * plan.token_rows, 128), BF),
        in_specs=[pl.BlockSpec(memory_space=pltpu.SMEM)] + [vmem] * 9 + [far] * 7,
        out_specs=far,
        scratch_shapes=scratch_shapes,
        compiler_params=pltpu.CompilerParams(
            collective_id=0, has_side_effects=True, vmem_limit_bytes=55 * 2**20
        ),
        name="layer",
    )(doc_lengths, freq, *gains, tokens[0], d_out[0], w_query, w_key, w_value, w_out, w_gate, w_up, w_down)
    half, block = plan.half, plan.block
    whole = lambda *shape: pl.BlockSpec(shape, lambda p: (0,) * len(shape))
    shape32 = lambda *shape: jax.ShapeDtypeStruct(shape, F32)
    outs = pl.pallas_call(
        functools.partial(spread_kernel, plan),
        grid=(4,),
        out_shape=[
            jax.ShapeDtypeStruct((rows, width), BF),
            jax.ShapeDtypeStruct((rows, width), BF),
            shape32(half, wide),
            shape32(half, head),
            shape32(half, head),
            shape32(wide // 2, width),
            shape32(half, ff),
            shape32(half, ff),
            shape32(ff // 2, width),
            shape32(half),
            shape32(head // 2),
            shape32(head // 2),
            shape32(half),
            shape32(half),
            shape32(half),
        ],
        in_specs=[
            pl.BlockSpec((4, total + 2 * plan.token_rows, 128), lambda p: (p, 0, 0)),
        ],
        out_specs=[
            pl.BlockSpec((rows // 4, width), lambda p: (p, 0)),
            pl.BlockSpec((rows // 4, width), lambda p: (p, 0)),
            pl.BlockSpec((half, head), lambda p: (0, p)),
            pl.BlockSpec((half, 128), lambda p: (0, jnp.minimum(p, 1))),
            pl.BlockSpec((half, 128), lambda p: (0, jnp.maximum(p, 2) - 2)),
            pl.BlockSpec((wide // 8, width), lambda p: (p, 0)),
            pl.BlockSpec((half, ff // 4), lambda p: (0, p)),
            pl.BlockSpec((half, ff // 4), lambda p: (0, p)),
            pl.BlockSpec((ff // 8, width), lambda p: (p, 0)),
            whole(half),
            whole(head // 2),
            whole(head // 2),
            whole(half),
            whole(half),
            whole(half),
        ],
        scratch_shapes=[scratch32(8, width)],
        compiler_params=pltpu.CompilerParams(vmem_limit_bytes=24 * 2**20),
        name="spread",
    )(flat)
    return (outs[0][None], outs[1][None]) + tuple(outs[2:])


def solution(mesh):
    whole = mesh.shape
    small = whole["rep"] == 4 and whole["fsdp"] == 2 and whole["seq"] == 4
    body = fused if small else general
    in_specs = (
        P(("rep", "fsdp"), "seq", None),
        P(("rep", "fsdp"), "seq", None),
        P(("rep", "fsdp"), None),
        P("fsdp", None),
        P("fsdp", None),
        P("fsdp", None),
        P("fsdp", None),
        P("fsdp", None),
        P("fsdp", None),
        P("fsdp", None),
        P("fsdp"),
        P("fsdp"),
        P("fsdp"),
        P("fsdp"),
        P("fsdp"),
        P("fsdp"),
    )
    out_specs = (
        P(("rep", "fsdp"), "seq", None),
        P(("rep", "fsdp"), "seq", None),
        P("fsdp", None),
        P("fsdp", None),
        P("fsdp", None),
        P("fsdp", None),
        P("fsdp", None),
        P("fsdp", None),
        P("fsdp", None),
        P("fsdp"),
        P("fsdp"),
        P("fsdp"),
        P("fsdp"),
        P("fsdp"),
        P("fsdp"),
    )
    return jax.shard_map(body, mesh=mesh, in_specs=in_specs, out_specs=out_specs, check_vma=False)
```

```python
import functools

import jax
import jax.numpy as jnp
import numpy as np
from jax import lax
from jax.experimental import pallas as pl
from jax.experimental.pallas import tpu as pltpu
from jax.sharding import PartitionSpec as P

EPS = 1e-06
ROPE_BASE = 1000000.0
MASKED = -1e30
MESH = pl.DeviceIdType.MESH
BF, F32 = jnp.bfloat16, jnp.float32


def rms_norm(values, gain_vec):
    return values * lax.rsqrt(jnp.mean(values * values, axis=-1, keepdims=True) + EPS) * gain_vec


def rotate(values, angles):
    half_width = values.shape[-1] // 2
    front_half = values[..., :half_width]
    back_half = values[..., half_width:]
    cos_part = jnp.cos(angles)
    sin_part = jnp.sin(angles)
    return jnp.concatenate(
        [
            front_half * cos_part - back_half * sin_part,
            back_half * cos_part + front_half * sin_part,
        ],
        axis=-1,
    )


def frequencies(head_size):
    return jnp.power(
        jnp.float32(ROPE_BASE), -2.0 * jnp.arange(head_size // 2, dtype=jnp.float32) / head_size
    )


def layout(lengths_row, total_len):
    count = lengths_row.shape[0]
    before = jnp.arange(count)[None, :] <= jnp.arange(count)[:, None]
    doc_ends = jnp.sum(jnp.where(before, lengths_row[None, :], 0), axis=1)
    starts = doc_ends - lengths_row
    indices = jnp.arange(total_len, dtype=jnp.int32)
    segment = jnp.sum((indices[:, None] >= doc_ends[None, :]).astype(jnp.int32), axis=1)
    onehot = segment[:, None] == jnp.arange(count, dtype=jnp.int32)[None, :]
    doc_begin = jnp.sum(jnp.where(onehot, starts[None, :], 0), axis=1)
    return (segment, indices - doc_begin)


def matmul(left_side, right_side):
    return jnp.dot(left_side, right_side, preferred_element_type=jnp.float32)


def times_transpose(left_side, right_side):
    return lax.dot_general(
        left_side, right_side, (((1,), (1,)), ((), ())), preferred_element_type=jnp.float32
    )


def transpose_times(left_side, right_side):
    return lax.dot_general(
        left_side, right_side, (((0,), (0,)), ((), ())), preferred_element_type=jnp.float32
    )


def gated(gate_proj, up_proj):
    return jax.nn.gelu(gate_proj, approximate=True) * up_proj


def gather_rows(shard):
    return lax.all_gather(shard, "fsdp", axis=0, tiled=True)


def reduce_rows(grad):
    low = grad.astype(jnp.bfloat16)
    own = lax.psum_scatter(low, "fsdp", scatter_dimension=0, tiled=True)
    return lax.psum(own, ("rep", "seq")).astype(jnp.float32)


def general(
    tokens,
    d_out,
    doc_lengths,
    w_query,
    w_key,
    w_value,
    w_out,
    w_gate,
    w_up,
    w_down,
    g_input,
    g_query,
    g_key,
    g_attn,
    g_ffin,
    g_ffout,
):
    shards = lax.axis_size("fsdp")
    gain_shards = (g_input, g_query, g_key, g_attn, g_ffin, g_ffout)
    widths = [entry.shape[0] for entry in gain_shards]
    starts = [sum(widths[:i]) for i in range(len(widths))]
    gain_rows = lax.all_gather(jnp.concatenate(gain_shards)[None], "fsdp", axis=0, tiled=True)
    gain_input, gain_query, gain_key, gain_attn, gain_ffin, gain_ffout = [
        gain_rows[:, at : at + width].reshape(-1).astype(jnp.float32)
        for at, width in zip(starts, widths)
    ]
    qkv_mat = gather_rows(jnp.concatenate([w_query, w_key, w_value], axis=1))
    out_mat = gather_rows(w_out)
    gate_up_mat = gather_rows(jnp.concatenate([w_gate, w_up], axis=1))
    down_mat = gather_rows(w_down)
    row_count = tokens.shape[1]
    head_size = gain_query.shape[0]
    query_width = w_query.shape[1]
    head_count = query_width // head_size
    ff_width = w_gate.shape[1]
    total_len = row_count * lax.axis_size("seq")
    segment, position = layout(doc_lengths[0], total_len)
    offset = lax.axis_index("seq") * row_count
    query_seg = lax.dynamic_slice_in_dim(segment, offset, row_count)
    query_pos = lax.dynamic_slice_in_dim(position, offset, row_count)
    places = offset + jnp.arange(row_count, dtype=jnp.int32)
    allowed = (query_seg[:, None] == segment[None, :]) & (
        places[:, None] >= jnp.arange(total_len, dtype=jnp.int32)[None, :]
    )
    angles = query_pos.astype(jnp.float32)[:, None] * frequencies(head_size)[None, :]
    scaling = head_size ** (-0.5)
    inputs = tokens[0].astype(jnp.float32)
    cotangent = d_out[0].astype(jnp.float32)
    input_norm, input_pull = jax.vjp(rms_norm, inputs, gain_input)
    attn_input = input_norm.astype(jnp.bfloat16)
    qkv_proj = matmul(attn_input, qkv_mat)
    q_proj = qkv_proj[:, :query_width]
    k_proj = qkv_proj[:, query_width : query_width + head_size]
    v_proj = qkv_proj[:, query_width + head_size :]

    def query_fn(projected, gain_vec):
        shaped = projected.reshape(projected.shape[0], -1, gain_vec.shape[0])
        return rotate(rms_norm(shaped, gain_vec), angles[:, None, :])

    def key_fn(projected, gain_vec):
        return rotate(rms_norm(projected, gain_vec), angles)

    queries, query_pull = jax.vjp(query_fn, q_proj, gain_query)
    keys_own, key_pull = jax.vjp(key_fn, k_proj, gain_key)
    query_rows = queries.astype(jnp.bfloat16).reshape(row_count * head_count, head_size)
    key_value_rows = lax.all_gather(
        jnp.concatenate([keys_own.astype(jnp.bfloat16), v_proj.astype(jnp.bfloat16)], axis=1),
        "seq",
        axis=0,
        tiled=True,
    )
    key_rows = key_value_rows[:, :head_size]
    value_rows = key_value_rows[:, head_size:]

    def masked_scores():
        raw_scores = times_transpose(query_rows, key_rows).reshape(row_count, head_count, total_len)
        return jnp.where(allowed[:, None, :], raw_scores * scaling, MASKED)

    scores = masked_scores()
    top_score = jnp.max(scores, axis=-1, keepdims=True)
    shifted = jnp.exp(scores - top_score)
    denominator = jnp.sum(shifted, axis=-1, keepdims=True)
    log_total = top_score + jnp.log(denominator)
    probs_low = (
        (shifted / denominator).astype(jnp.bfloat16).reshape(row_count * head_count, total_len)
    )
    mixed_rows = (
        matmul(probs_low, value_rows)
        .reshape(row_count, head_count * head_size)
        .astype(jnp.bfloat16)
    )
    out_proj = matmul(mixed_rows, out_mat)
    attn_norm, attn_pull = jax.vjp(rms_norm, out_proj, gain_attn)
    hidden_one = inputs + attn_norm
    ffin_norm, ffin_pull = jax.vjp(rms_norm, hidden_one, gain_ffin)
    ff_input = ffin_norm.astype(jnp.bfloat16)
    gate_up_proj = matmul(ff_input, gate_up_mat)
    gate_proj = gate_up_proj[:, :ff_width]
    up_proj = gate_up_proj[:, ff_width:]
    activated, gated_pull = jax.vjp(gated, gate_proj, up_proj)
    hidden = activated.astype(jnp.bfloat16)
    down_proj = matmul(hidden, down_mat)
    ffout_norm, ffout_pull = jax.vjp(rms_norm, down_proj, gain_ffout)
    result = hidden_one + ffout_norm
    d_down, grad_gffout = ffout_pull(cotangent)
    d_down_low = d_down.astype(jnp.bfloat16)
    total_down = reduce_rows(transpose_times(hidden, d_down_low))
    d_hidden = times_transpose(d_down_low, down_mat)
    d_gate, d_up = gated_pull(d_hidden)
    d_gate_up_low = jnp.concatenate(
        [d_gate.astype(jnp.bfloat16), d_up.astype(jnp.bfloat16)], axis=1
    )
    total_gate_up = reduce_rows(transpose_times(ff_input, d_gate_up_low))
    d_ffin = times_transpose(d_gate_up_low, gate_up_mat)
    d_hidden_part, grad_gffin = ffin_pull(d_ffin)
    d_hidden_one = cotangent + d_hidden_part
    d_out_proj, grad_gattn = attn_pull(d_hidden_one)
    d_out_low = d_out_proj.astype(jnp.bfloat16)
    total_out = reduce_rows(transpose_times(mixed_rows, d_out_low))
    d_mixed = (
        times_transpose(d_out_low, out_mat)
        .astype(jnp.bfloat16)
        .reshape(row_count * head_count, head_size)
    )
    probs_full = jnp.exp(masked_scores() - log_total)
    d_probs = times_transpose(d_mixed, value_rows).reshape(row_count, head_count, total_len)
    row_dot = jnp.sum(probs_full * d_probs, axis=-1, keepdims=True)
    d_raw = (
        (probs_full * (d_probs - row_dot) * scaling)
        .astype(jnp.bfloat16)
        .reshape(row_count * head_count, total_len)
    )
    grad_rows = jnp.concatenate(
        [
            transpose_times(d_raw, query_rows).astype(jnp.bfloat16),
            transpose_times(probs_low, d_mixed).astype(jnp.bfloat16),
        ],
        axis=1,
    )
    d_queries = matmul(d_raw, key_rows).reshape(row_count, head_count, head_size)
    grad_own = lax.psum_scatter(grad_rows, "seq", scatter_dimension=0, tiled=True).astype(
        jnp.float32
    )
    d_q_proj, grad_gquery = query_pull(d_queries)
    d_k_proj, grad_gkey = key_pull(grad_own[:, :head_size])
    d_qkv_low = jnp.concatenate(
        [
            d_q_proj.astype(jnp.bfloat16),
            d_k_proj.astype(jnp.bfloat16),
            grad_own[:, head_size:].astype(jnp.bfloat16),
        ],
        axis=1,
    )
    grad_qkv = transpose_times(attn_input, d_qkv_low)
    d_attn_input = times_transpose(d_qkv_low, qkv_mat)
    d_inputs_part, grad_ginput = input_pull(d_attn_input)
    d_inputs = d_hidden_one + d_inputs_part
    grad_gains = (grad_ginput, grad_gquery, grad_gkey, grad_gattn, grad_gffin, grad_gffout)
    packed_gains = jnp.concatenate([entry.reshape(shards, -1) for entry in grad_gains], axis=1)
    total_qkv = reduce_rows(grad_qkv)
    total_gains = lax.psum_scatter(
        packed_gains.astype(jnp.bfloat16), "fsdp", scatter_dimension=0, tiled=True
    )
    total_gains = lax.psum(total_gains, ("rep", "seq")).astype(jnp.float32)[0]
    return (
        result.astype(jnp.bfloat16)[None],
        d_inputs.astype(jnp.bfloat16)[None],
        total_qkv[:, :query_width],
        total_qkv[:, query_width : query_width + head_size],
        total_qkv[:, query_width + head_size :],
        total_out,
        total_gate_up[:, :ff_width],
        total_gate_up[:, ff_width:],
        total_down,
    ) + tuple(total_gains[at : at + width] for at, width in zip(starts, widths))


def dot(left_side, right_side):
    return jnp.dot(left_side, right_side, preferred_element_type=F32)


def dot_nt(left_side, right_side):
    return lax.dot_general(
        left_side, right_side, (((1,), (1,)), ((), ())), preferred_element_type=F32
    )


def loop(count, step):
    lax.fori_loop(0, count, lambda i, carry: (step(i), carry)[1], 0)


def at_block(i, size):
    return pl.ds(pl.multiple_of(i * size, size), size)


def inverse_rms(values):
    return lax.rsqrt(jnp.mean(values * values, axis=-1, keepdims=True) + EPS)


def rms_pull(values, gain_row, grad):
    inv = inverse_rms(values)
    scaled = values * inv
    pulled = grad * gain_row
    along = jnp.mean(pulled * scaled, axis=-1, keepdims=True)
    return inv * (pulled - scaled * along), jnp.sum(grad * scaled, axis=0, keepdims=True)


def turn(values, cos_part, sin_part):
    half_width = values.shape[-1] // 2
    front, back = values[:, :half_width], values[:, half_width:]
    return jnp.concatenate(
        [front * cos_part - back * sin_part, back * cos_part + front * sin_part], axis=1
    )


class Plan:
    def __init__(self, rows, width, heads, head, ff):
        self.rows, self.width, self.heads, self.head, self.ff = rows, width, heads, head, ff
        self.half = width // 2
        block = self.half // 4
        sizes = (
            ff * width // (32 * 128),
            self.half * ff // (16 * 128),
            self.half * ff // (16 * 128),
            heads * head * width // (32 * 128),
            block * head // 128,
            block + 16,
        )
        self.starts = [sum(sizes[:i]) for i in range(len(sizes))]
        self.chunks = tuple(
            (start + size * a // 10, size * (b - a) // 10)
            for start, size, cuts in zip(self.starts, sizes, CUTS)
            for a, b in zip(cuts, cuts[1:])
        )
        self.block = block
        self.total = sum(sizes)
        self.gains_at = self.total - 16
        self.token_rows = rows * width // (16 * 128)
        self.tiles = width // 128


CUTS = ((0, 2, 6, 10), (0, 6, 10), (0, 5, 10), (0, 10), (0, 5, 10), (0, 10))
FIRST = tuple("yxyxyyxxyxx")
DIRECT = tuple("vddddtttvud")
WEIGHTS = ((0, 0, 3, "z", None), (0, 3, None, "y", None), (1, 0, None, "y", "rows"), (2, 0, None, "y", "columns"), (3, 0, None, "z", "columns"), (4, 0, None, "z", None))

SCHEDULE = (
    ("init",), ("wx", 1), ("norm",), ("wx", 2), ("wa", 0), ("wx", 3), ("wa", 1), ("wx", 4), ("wa", 2), ("wb", 0),
    ("wb", 1), ("wx", 5), ("wa", 3), ("kv",), ("wb", 2), ("wc", 2), ("q",), ("wa", 4), ("wb", 3), ("wc", 3),
    ("wd", 2), ("kvf", 0), ("wa", 5), ("keys",), ("at", 0), ("wb", 4), ("kvf", 1), ("at", 1), ("kvt",), ("wd", 3),
    ("outp",), ("wc", 4), ("wd", 4), ("ff", 0), ("wb", 5), ("ff", 1), ("down",), ("nout",), ("gd", 0), ("sum", 0, 0),
    ("sum", 1, 0), ("sum", 2, 0), ("gd", 1), ("fb", 0), ("sum", 0, 1), ("sum", 1, 1), ("fb", 1), ("sum", 3, 0),
    ("sum", 4, 0), ("sum", 5, 0), ("sum", 2, 1), ("sum", 6, 0), ("fb", 2), ("sum", 0, 2), ("fb", 3), ("sum", 1, 2),
    ("sum", 3, 1), ("sum", 4, 1), ("sum", 5, 1), ("sum", 0, 3), ("mid",), ("sum", 2, 2), ("sum", 6, 1), ("gout",),
    ("sum", 0, 4), ("sum", 1, 3), ("sum", 7, 0), ("ab", 0), ("ab", 1), ("sum", 3, 2), ("sum", 4, 2), ("sum", 1, 4),
    ("sum", 7, 1), ("dks",), ("sum", 2, 3), ("gq",), ("sum", 8, 0), ("sum", 9, 0), ("dky",), ("sum", 8, 1),
    ("sum", 1, 5), ("sum", 5, 2), ("sum", 0, 5), ("sum", 9, 1), ("sum", 6, 2), ("sum", 2, 4), ("sum", 0, 6),
    ("sum", 3, 3), ("sum", 4, 3), ("sum", 2, 5), ("sum", 0, 7), ("gkv",), ("last",), ("sum", 7, 2), ("sum", 3, 4),
    ("sum", 10, 0), ("sum", 0, 8), ("sum", 8, 2), ("sum", 10, 1), ("sum", 5, 3), ("sum", 4, 4), ("sum", 1, 6),
    ("sum", 1, 7), ("sum", 9, 2), ("sum", 6, 3), ("sum", 3, 5), ("sum", 5, 4), ("sum", 8, 3), ("sum", 2, 6),
    ("sum", 4, 5), ("sum", 2, 7), ("sum", 6, 4), ("sum", 10, 2), ("sum", 7, 3), ("sum", 5, 5), ("sum", 9, 3),
    ("sum", 8, 4), ("sum", 6, 5), ("sum", 7, 4), ("sum", 3, 6), ("sum", 5, 6), ("sum", 9, 4), ("sum", 3, 7),
    ("sum", 6, 6), ("sum", 4, 6), ("sum", 7, 5), ("sum", 4, 7), ("sum", 5, 7), ("sum", 10, 3), ("sum", 8, 5),
    ("sum", 9, 5), ("sum", 6, 7), ("sum", 7, 6), ("sum", 10, 4), ("sum", 5, 8), ("sum", 9, 6), ("sum", 8, 6),
    ("sum", 5, 9), ("sum", 7, 7), ("sum", 6, 8), ("sum", 10, 5), ("sum", 6, 9), ("sum", 9, 7), ("sum", 8, 7),
    ("sum", 7, 8), ("sum", 8, 8), ("sum", 7, 9), ("sum", 9, 8), ("sum", 10, 6), ("sum", 9, 9), ("sum", 10, 7),
)


SECOND = {"y": "z", "z": "y"}


def layer_kernel(plan, doc, freq, *refs):
    shards, refs = refs[:6], refs[6:]
    (tok, dout, wq, wk, wv, wo, wg, wu, wd, flat_out) = refs[:10]
    (qkv_mat, out_mat, gate_mat, up_mat, down_mat, gain_own, gain_far, gain_full, attn_in, attn_in_t, qkv_f, queries, kv, keys_t) = refs[10:24]
    (values_t, probs, mixed, out_f, h1, ff_in, ff_in_t, gate_f, up_f, hidden, down_f, d_down, d_h1) = refs[24:37]
    scores = gate_f
    (d_outp, d_mixed, dkv, dkv_c, dkv_y, d_qkv, cos_t, sin_t, d_raw, gain_acc, gain_rows) = refs[37:48]
    (grads, from_c, from_1, from_2, from_z) = refs[48:53]
    (w_local, wx_s, wx_r, wf_s, wf_r, kv_s, kv_r, dk_s, dk_r, gs_, gr_, rs_s, rs_r, fin, free, packed, out_sem) = refs[53:70]
    rows, width, heads, head, ff = plan.rows, plan.width, plan.heads, plan.head, plan.ff
    half, block = plan.half, plan.block
    rep, x, s = lax.axis_index("rep"), lax.axis_index("fsdp"), lax.axis_index("seq")
    y, c = s // 2, s % 2
    zh, zl = rep // 2, rep % 2
    to = {
        "x": (rep, 1 - x, s),
        "c": (rep, x, y * 2 + 1 - c),
        "y": (rep, x, (1 - y) * 2 + c),
        "z": (zh * 2 + 1 - zl, x, s),
        "z2": ((1 - zh) * 2 + zl, x, s),
        "z3": ((1 - zh) * 2 + 1 - zl, x, s),
    }
    sends = []

    def send(source, target, send_sem, recv_sem, axis):
        copy = pltpu.make_async_remote_copy(
            src_ref=source,
            dst_ref=target,
            send_sem=send_sem,
            recv_sem=recv_sem,
            device_id=to[axis],
            device_id_type=MESH,
        )
        copy.start()
        sends.append(copy)
        return copy

    parts = (
        ((wq, 0), (wk, heads * head), (wv, heads * head + head)),
        ((wo, 0),),
        ((wg, 0),),
        ((wu, 0),),
        ((wd, 0),),
    )
    mats = (qkv_mat, out_mat, gate_mat, up_mat, down_mat)
    locals_of, x_of, f_of = {}, {}, {}
    slot = 0
    slots = []
    for i, (mat, entries) in enumerate(zip(mats, parts)):
        shard_rows = mat.shape[0] // 2
        locals_of[i] = []
        for ref, col in entries:
            copy = pltpu.make_async_copy(
                ref, mat.at[pl.ds(x * shard_rows, shard_rows), pl.ds(col, ref.shape[1])], w_local.at[slot]
            )
            copy.start()
            locals_of[i].append(copy)
            slot += 1

    barrier = pltpu.get_barrier_semaphore()
    for axis in to:
        pl.semaphore_signal(barrier, inc=1, device_id=to[axis], device_id_type=MESH)
    pl.semaphore_wait(barrier, len(to))

    for m, *_ in WEIGHTS:
        slots.append(sum(len(parts[n]) for n, *_ in WEIGHTS[: len(slots)]))

    def region(i, far_bit, far_z):
        m, first, last, axis, cut = WEIGHTS[i]
        bit = y if axis == "y" else zl
        quarter = (1 - bit if far_bit else bit) * 2 + c
        low = zl if axis == "y" else y
        low = 1 - low if far_z else low
        size, columns = mats[m].shape[0] // 8, mats[m].shape[1]
        skip, size, at = 16 * first, (size if last is None else 16 * last) - 16 * first, quarter * size
        if cut == "rows":
            return at + low * (size // 2), size // 2, None
        if cut == "columns":
            return at + skip, size, at_block(low, columns // 2)
        return at + skip, size, None

    def weight_x(i):
        shard_rows = mats[WEIGHTS[i][0]].shape[0] // 2
        at, size, columns = region(i, False, False)
        x_of[i] = []
        for j, (ref, col) in enumerate(parts[WEIGHTS[i][0]]):
            here = pl.ds(0, ref.shape[1]) if columns is None else columns
            there = pl.ds(col, ref.shape[1]) if columns is None else columns
            x_of[i].append(
                send(
                    ref.at[pl.ds(at, size), here],
                    mats[WEIGHTS[i][0]].at[pl.ds(x * shard_rows + at, size), there],
                    wx_s.at[slots[i] + j],
                    wx_r.at[slots[i] + j],
                    "x",
                )
            )

    def weight_forward(i, n, axis, far_bit, far_z=False):
        shard_rows = mats[WEIGHTS[i][0]].shape[0] // 2
        at, size, columns = region(i, far_bit, far_z)
        where = mats[WEIGHTS[i][0]].at[pl.ds((1 - x) * shard_rows + at, size)]
        if columns is not None:
            where = mats[WEIGHTS[i][0]].at[pl.ds((1 - x) * shard_rows + at, size), columns]
        f_of[i, n] = send(where, where, wf_s.at[i, n], wf_r.at[i, n], axis)

    def weight_a(i):
        for copy in x_of[i]:
            copy.wait_recv()
        weight_forward(i, 0, WEIGHTS[i][3], False)
        if WEIGHTS[i][4]:
            weight_forward(i, 3, SECOND[WEIGHTS[i][3]], False)
        weight_forward(i, 1, "c", False)

    def weight_b(i):
        f_of[i, 0].wait_recv()
        if WEIGHTS[i][4]:
            weight_forward(i, 4, SECOND[WEIGHTS[i][3]], True)
        weight_forward(i, 2, "c", True)

    def weight_c(i):
        f_of[i, 3].wait_recv()
        weight_forward(i, 5, "c", False, True)

    def weight_d(i):
        f_of[i, 4].wait_recv()
        weight_forward(i, 6, "c", True, True)

    def weight_done(m):
        for i in range(len(WEIGHTS)):
            if WEIGHTS[i][0] == m:
                for n in (1, 2, 5, 6) if WEIGHTS[i][4] else (1, 2):
                    f_of[i, n].wait_recv()
        for copy in locals_of[m]:
            copy.wait()

    mine_c, mine_y = c * 8, c * 8 + y * 4
    gathered = from_c.at[1 - x]
    piece_of = lambda high, low: mine_y + 2 * high + low
    hops = {}

    def hop(k, n, source, target, axis):
        hops[k, n] = send(source, target, rs_s.at[k, n], rs_r.at[k, n], axis)

    def span(k):
        return pl.ds(*plan.chunks[k])

    def total_of(k, m, last=False, z=()):
        r = span(k)
        place = y * 4 + m
        value = grads[x, mine_c + place, r, :].astype(F32) + from_c[x, place, r, :].astype(F32)
        first = place if FIRST[k] == "x" else 4 * x + m
        value = value + from_1[first, r, :].astype(F32) + from_2[m, r, :].astype(F32)
        for i in z:
            value = value + from_z[i, r, :].astype(F32)
        if last:
            gathered[place, r, :] = value.astype(BF)
        else:
            grads[x, mine_c + place, r, :] = value.astype(BF)

    def add_core(k, h, place, first=None):
        r = span(k)
        value = grads[h, mine_c + place, r, :].astype(F32) + from_c[h, place, r, :].astype(F32)
        if first is not None:
            value = value + from_1[first, r, :].astype(F32)
        grads[h, mine_c + place, r, :] = value.astype(BF)

    z_ways = (("z", zh, 1 - zl), ("z2", 1 - zh, zl), ("z3", 1 - zh, 1 - zl))

    def sum_c(k):
        r = span(k)
        hop(k, 0, grads.at[:, pl.ds((1 - c) * 8, 8), r], from_c.at[:, :, r], "c")

    def sum_1(k):
        r = span(k)
        hops[k, 0].wait_recv()
        if FIRST[k] == "x":
            loop(8, lambda i: add_core(k, 1 - x, i))
            for i in range(2):
                hop(k, (1, 12)[i], grads.at[1 - x, pl.ds(mine_c + 4 * i, 4), r], from_1.at[pl.ds(4 * i, 4), r], "x")
        else:
            far = (1 - y) * 4
            for h in range(2):
                loop(4, lambda i: add_core(k, h, far + i))
                hop(k, (1, 12)[h], grads.at[h, pl.ds(mine_c + far, 4), r], from_1.at[pl.ds(4 * h, 4), r], "y")

    def sum_2(k):
        r = span(k)
        hops[k, 1].wait_recv()
        hops[k, 12].wait_recv()
        hops[k, 0].wait_send()
        pl.semaphore_signal(free.at[k], inc=1, device_id=to["c"], device_id_type=MESH)
        if FIRST[k] == "x":
            far = (1 - y) * 4
            loop(4, lambda i: add_core(k, x, far + i, far + i))
            hop(k, 2, grads.at[x, pl.ds(mine_c + far, 4), r], from_2.at[:, r], "y")
        else:
            loop(4, lambda i: add_core(k, 1 - x, y * 4 + i, 4 * (1 - x) + i))
            hop(k, 2, grads.at[1 - x, pl.ds(mine_y, 4), r], from_2.at[:, r], "x")

    def sum_z(k):
        r = span(k)
        hops[k, 2].wait_recv()
        for i, (axis, high, low) in enumerate(z_ways):
            total_of(k, 2 * high + low)
            hop(k, 3 + i, grads.at[x, piece_of(high, low), r], from_z.at[i, r], axis)

    def sum_z1(k):
        r = span(k)
        hops[k, 2].wait_recv()
        for i in range(2):
            total_of(k, 2 * i + 1 - zl)
            hop(k, 3 + i, grads.at[x, piece_of(i, 1 - zl), r], from_z.at[i, r], "z")

    def sum_z2(k):
        r = span(k)
        hops[k, 3].wait_recv()
        hops[k, 4].wait_recv()
        total_of(k, 2 * (1 - zh) + zl, z=(1 - zh,))
        hop(k, 5, grads.at[x, piece_of(1 - zh, zl), r], from_z.at[2, r], "z2")

    def back_z2(k):
        hops[k, 5].wait_recv()
        near = 2 * zh + zl
        total_of(k, near, last=True, z=(zh, 2))
        where = gathered.at[near + y * 4, span(k)]
        hop(k, 6, where, where, "z2")

    def back_z1(k):
        hops[k, 6].wait_recv()
        for i in range(2):
            where = gathered.at[y * 4 + 2 * i + zl, span(k)]
            hop(k, 7 + i, where, where, "z")

    def back_z(k):
        r = span(k)
        for i in range(3):
            hops[k, 3 + i].wait_recv()
        near = 2 * zh + zl
        total_of(k, near, last=True, z=(0, 1, 2))
        where = gathered.at[near + y * 4, r]
        for i, (axis, _, _) in enumerate(z_ways):
            hop(k, 6 + i, where, where, axis)

    def back_y(k):
        for i in range(3) if DIRECT[k] == "d" else (1, 2):
            hops[k, 6 + i].wait_recv()
        where = gathered.at[pl.ds(y * 4, 4), span(k)]
        hop(k, 9, where, where, "y")
        pl.semaphore_wait(free.at[k], 1)
        hop(k, 10, where, grads.at[x, pl.ds(mine_c + y * 4, 4), span(k)], "c")

    def back_c(k):
        hops[k, 9].wait_recv()
        where = gathered.at[pl.ds((1 - y) * 4, 4), span(k)]
        hop(k, 11, where, grads.at[x, pl.ds(mine_c + (1 - y) * 4, 4), span(k)], "c")

    outs = []

    def finish(k):
        hops[k, 10].wait_recv()
        if (k, 11) in hops:
            hops[k, 11].wait_recv()
        r = span(k)
        for i, source, first in ((0, gathered, mine_c), (1, grads.at[x, pl.ds((1 - c) * 8, 8)], (1 - c) * 8)):
            copy = pltpu.make_async_copy(source.at[:, r], flat_out.at[pl.ds(first, 8), r], fin.at[k, i])
            copy.start()
            outs.append(copy)

    def home_y(k):
        for i in range(3, 6) if DIRECT[k] == "v" else (5,):
            hops[k, i].wait_recv()
        near = 2 * zh + zl
        total_of(k, near, last=True, z=(0, 1, 2) if DIRECT[k] == "v" else (zh, 2))
        where = gathered.at[near + y * 4, span(k)]
        hop(k, 9, where, where, "y")

    def home_z2(k):
        hops[k, 9].wait_recv()
        for i in range(2):
            where = gathered.at[4 * i + 2 * zh + zl, span(k)]
            hop(k, 6 + i, where, where, "z2")

    def home_z1(k):
        hops[k, 6].wait_recv()
        hops[k, 7].wait_recv()
        for i, n in enumerate((8, 13, 14, 15)):
            where = gathered.at[2 * i + zl, span(k)]
            hop(k, n, where, where, "z")

    def home_c(k):
        for n in (8, 13, 14, 15):
            hops[k, n].wait_recv()
        pl.semaphore_wait(free.at[k], 1)
        hop(k, 10, gathered.at[:, span(k)], grads.at[x, pl.ds(mine_c, 8), span(k)], "c")

    ends_with = (back_y, back_c, finish)
    home = (home_y, home_z2, home_z1, home_c, finish)
    steps_of = {
        "d": (sum_c, sum_1, sum_2, sum_z, back_z) + ends_with,
        "t": (sum_c, sum_1, sum_2, sum_z1, sum_z2, back_z2, back_z1) + ends_with,
        "u": (sum_c, sum_1, sum_2, sum_z1, sum_z2) + home,
        "v": (sum_c, sum_1, sum_2, sum_z) + home,
    }

    ends = [doc[0, 0]]
    for i in range(1, doc.shape[1]):
        ends.append(ends[-1] + doc[0, i])

    def start_of(places):
        start = jnp.zeros_like(places)
        for i, end in enumerate(ends):
            start = jnp.where(places >= end, end, start)
        return start

    gain_own[...] = jnp.zeros_like(gain_own)
    for i, ref in enumerate(shards):
        gain_own[i : i + 1, 0 : ref.shape[0]] = ref[...].astype(F32).reshape(1, ref.shape[0])
    gain_copy = send(gain_own, gain_far, gs_.at[0], gr_.at[0], "x")
    weight_x(0)
    place_row = s * rows + lax.broadcasted_iota(jnp.int32, (1, rows), 1)
    start_row = start_of(place_row)
    gain = lambda i, size: gain_full[i : i + 1, 0:size]
    scaling = head ** (-0.5)
    blocks = 4
    root = 0.7978845608028654
    tiles_ff = ff // head
    tiles = plan.tiles
    wide = heads * head
    at_down, at_gate, at_up, at_out, at_q, at_kv = plan.starts
    held = {}

    def pack(n, r0, size, value):
        value = value.astype(BF)
        for i in range(size // 16):
            for t in range(tiles):
                at = n * plan.token_rows + 16 * t
                packed[r0 // 16 + i, at : at + 16, :] = value[16 * i : 16 * (i + 1), 128 * t : 128 * (t + 1)]

    def by_number(size, step):
        loop(rows // size, lambda i: step(i * size, pl.ds(pl.multiple_of(i * size, size), size)))

    def by_rows(size, step):
        loop(rows // size, lambda i: step(pl.ds(pl.multiple_of(i * size, size), size)))

    def task_init():
        place_col = s * rows + lax.broadcasted_iota(jnp.int32, (rows, 128), 0)
        angles = (place_col - start_of(place_col)).astype(F32) * freq[...]
        cos_t[...] = jnp.cos(angles)
        sin_t[...] = jnp.sin(angles)
        none = jnp.zeros((16, 128), BF)
        for h in range(2):
            for p in range(2, 16):
                grads[h, p, plan.gains_at : plan.gains_at + 16, :] = none
        gain_rows[...] = jnp.zeros_like(gain_rows)
        gain_acc[...] = jnp.zeros_like(gain_acc)

    def norm_in(r):
        v = tok[r, :].astype(F32)
        attn_in[r, :] = (v * inverse_rms(v) * gain(0, width)).astype(BF)

    def task_norm():
        gain_copy.wait_recv()
        own, far = gain_own[...], gain_far[...]
        first, second = jnp.where(x == 0, own, far), jnp.where(x == 0, far, own)
        line = lax.broadcasted_iota(jnp.int32, own.shape, 0)
        short = (line == 1) | (line == 2)
        moved = jnp.where(short, pltpu.roll(second, head // 2, 1), pltpu.roll(second, half, 1))
        gain_full[...] = first + moved
        by_rows(64, norm_in)
        attn_in_t[...] = attn_in[...].T

    def project(j):
        qkv_f[j] = dot(attn_in[...], qkv_mat[:, at_block(j, head)])

    def task_kv():
        weight_done(0)
        project(heads)
        project(heads + 1)
        k_f = qkv_f[heads]
        kv[s, :, 0:head] = turn(k_f * inverse_rms(k_f) * gain(2, head), cos_t[...], sin_t[...]).astype(BF)
        kv[s, :, head : 2 * head] = qkv_f[heads + 1].astype(BF)
        for n in range(2):
            where = kv.at[s, :, n * head : (n + 1) * head]
            held["y", n] = send(where, where, kv_s.at[n], kv_r.at[n], "y")
            held["c", n] = send(where, where, kv_s.at[2 + n], kv_r.at[2 + n], "c")

    def turn_query(h):
        project(h)
        q_f = qkv_f[h]
        queries[h] = turn(q_f * inverse_rms(q_f) * gain(1, head), cos_t[...], sin_t[...]).astype(BF)

    def task_q():
        loop(heads, turn_query)

    def task_kvf(n):
        held["y", n].wait_recv()
        where = kv.at[(1 - y) * 2 + c, :, n * head : (n + 1) * head]
        held["cc", n] = send(where, where, kv_s.at[4 + n], kv_r.at[4 + n], "c")

    def transpose_keys(i):
        keys_t[:, at_block(i, rows)] = kv[i, :, 0:head].T

    def transpose_values(i):
        values_t[:, at_block(i, rows)] = kv[i, :, head : 2 * head].T

    def task_keys():
        held["c", 0].wait_recv()
        held["cc", 0].wait_recv()

    def task_kvt():
        held["c", 1].wait_recv()
        held["cc", 1].wait_recv()
        loop(blocks, transpose_values)

    def attend(h):
        q = queries[h]
        top = jnp.full((1, rows), MASKED, F32)
        for i in range(blocks):
            u = i * rows + lax.broadcasted_iota(jnp.int32, (rows, rows), 0)
            raw = dot_nt(kv[i, :, 0:head], q) * scaling
            raw = jnp.where((u <= place_row) & (u >= start_row), raw, MASKED)
            scores[i] = raw
            top = jnp.maximum(top, jnp.max(raw, axis=0, keepdims=True))
        denominator = jnp.zeros((1, rows), F32)
        for i in range(blocks):
            e = jnp.exp(scores[i] - top)
            scores[i] = e
            denominator = denominator + jnp.sum(e, axis=0, keepdims=True)
        inv = 1.0 / denominator
        for i in range(blocks):
            probs[h, i * rows : (i + 1) * rows, :] = (scores[i] * inv).astype(BF)

    def mix(h):
        mixed[:, at_block(h, head)] = dot(values_t[...], probs[h]).T.astype(BF)

    def task_at(n):
        loop(2, lambda i: attend(2 * n + i))

    def norm_ff(r):
        o = out_f[r, :]
        h = tok[r, :].astype(F32) + o * inverse_rms(o) * gain(3, width)
        h1[r, :] = h
        ff_in[r, :] = (h * inverse_rms(h) * gain(4, width)).astype(BF)

    def task_outp():
        loop(heads, mix)
        weight_done(1)
        out_f[...] = dot(mixed[...], out_mat[...])
        by_rows(64, norm_ff)
        ff_in_t[...] = ff_in[...].T

    def feed(j):
        g = dot(ff_in[...], gate_mat[:, at_block(j, head)])
        u = dot(ff_in[...], up_mat[:, at_block(j, head)])
        gate_f[j] = g
        up_f[j] = u
        t = jnp.tanh(root * (g + 0.044715 * (g * g * g)))
        hidden[:, at_block(j, head)] = (0.5 * g * (1.0 + t) * u).astype(BF)

    def task_ff(n):
        if n == 0:
            weight_done(2)
            weight_done(3)
        loop(tiles_ff // 2, lambda j: feed(j + n * (tiles_ff // 2)))

    def task_down():
        weight_done(4)
        down_f[...] = dot(hidden[...], down_mat[...])

    def gain_add(i, size, row):
        gain_acc[i : i + 1, 0:size] = gain_acc[i : i + 1, 0:size] + row

    def norm_out(r0, r):
        d = down_f[r, :]
        pack(0, r0, 64, h1[r, :] + d * inverse_rms(d) * gain(5, width))
        pulled, g_row = rms_pull(d, gain(5, width), dout[r, :].astype(F32))
        d_down[r, :] = pulled.astype(BF)
        gain_add(5, width, g_row)

    def task_nout():
        by_number(64, norm_out)

    def grad_down(j):
        value = dot(hidden[:, at_block(j, head)].T, d_down[...]).astype(BF)
        high, low = j // (tiles_ff // 2), j % (tiles_ff // 2)
        size = ff // 32
        for i in range(head // size):
            for t in range(tiles):
                grads[high, low * (head // size) + i, at_down + size * t : at_down + size * (t + 1), :] = value[
                    size * i : size * (i + 1), 128 * t : 128 * (t + 1)
                ]

    def task_gd(n):
        side, per = (1 - c, c)[n], tiles_ff // 4
        loop(2 * per, lambda i: grad_down((i // per) * 2 * per + side * per + i % per))

    def feed_back(j):
        d_hidden = dot_nt(d_down[...], down_mat[at_block(j, head), :])
        g, u = gate_f[j], up_f[j]
        t = jnp.tanh(root * (g + 0.044715 * (g * g * g)))
        act = 0.5 * g * (1.0 + t)
        slope = 0.5 * (1.0 + t) + 0.5 * g * (1.0 - t * t) * (root * (1.0 + 3 * 0.044715 * (g * g)))
        d_gate = (d_hidden * u * slope).astype(BF)
        d_up = (d_hidden * act).astype(BF)
        for at, value in ((at_gate, d_gate), (at_up, d_up)):
            full = dot(ff_in_t[...], value).astype(BF)
            for h in range(2):
                for t_ in range(2):
                    grads[h, 2 * j + t_, at : at + half, :] = full[half * h : half * (h + 1), 128 * t_ : 128 * (t_ + 1)]
        more = dot_nt(d_gate, gate_mat[:, at_block(j, head)]) + dot_nt(d_up, up_mat[:, at_block(j, head)])
        down_f[...] = down_f[...] + more

    def task_fb(n):
        if n == 0:
            down_f[...] = jnp.zeros_like(down_f)
        side, per = (1 - c, c)[n // 2], tiles_ff // 4
        loop(per, lambda i: feed_back(side * 2 * per + (n % 2) * per + i))

    def norm_mid(r):
        pulled, g_row = rms_pull(h1[r, :], gain(4, width), down_f[r, :])
        gain_add(4, width, g_row)
        d_mid = dout[r, :].astype(F32) + pulled
        d_h1[r, :] = d_mid
        pulled, g_row = rms_pull(out_f[r, :], gain(3, width), d_mid)
        gain_add(3, width, g_row)
        d_outp[r, :] = pulled.astype(BF)

    def task_mid():
        by_rows(64, norm_mid)

    def grad_out(j):
        value = dot(mixed[:, at_block(j, head)].T, d_outp[...]).astype(BF)
        size = heads * head // 32
        high, low = j // (heads // 2), j % (heads // 2)
        for i in range(head // size):
            for t in range(tiles):
                grads[high, low * (head // size) + i, at_out + size * t : at_out + size * (t + 1), :] = value[
                    size * i : size * (i + 1), 128 * t : 128 * (t + 1)
                ]
        d_mixed[j] = dot_nt(d_outp[...], out_mat[at_block(j, head), :]).astype(BF)

    def task_gout():
        loop(blocks, transpose_keys)
        loop(heads, grad_out)

    def attend_back(h):
        dm = d_mixed[h]
        along = jnp.zeros((1, rows), F32)
        for i in range(blocks):
            d_probs = dot_nt(kv[i, :, head : 2 * head], dm)
            scores[i] = d_probs
            p = probs[h, i * rows : (i + 1) * rows, :].astype(F32)
            along = along + jnp.sum(p * d_probs, axis=0, keepdims=True)
        for i in range(blocks):
            low = probs[h, i * rows : (i + 1) * rows, :]
            ds = (low.astype(F32) * (scores[i] - along) * scaling).astype(BF)
            d_raw[i * rows : (i + 1) * rows, :] = ds
            up_f[i] = up_f[i] + dot(ds, queries[h])
            up_f[blocks + i] = up_f[blocks + i] + dot(low, dm)
        dq = dot(keys_t[...], d_raw[...]).T
        turned = turn(dq, cos_t[...], -sin_t[...])
        pulled, g_row = rms_pull(qkv_f[h], gain(1, head), turned)
        gain_add(1, head, g_row)
        d_qkv[:, at_block(h, head)] = pulled.astype(BF)

    def task_ab(n):
        if n == 0:
            up_f[...] = jnp.zeros_like(up_f)
        loop(2, lambda i: attend_back(2 * n + i))

    def task_dks():
        for i in range(blocks):
            dkv[i, :, 0:head] = up_f[i].astype(BF)
            dkv[i, :, head : 2 * head] = up_f[blocks + i].astype(BF)
        held["dk_c"] = [
            send(dkv.at[2 * i + 1 - c], dkv_c.at[i], dk_s.at[i], dk_r.at[i], "c") for i in range(2)
        ]

    def grad_query(h):
        full = dot(attn_in_t[...], d_qkv[:, at_block(h, head)]).astype(BF)
        for n in range(2):
            for i in range(4):
                for t in range(2):
                    grads[n, 4 * h + i, at_q + block * t : at_q + block * (t + 1), :] = full[
                        half * n + block * i : half * n + block * (i + 1), 128 * t : 128 * (t + 1)
                    ]

    def task_dky():
        for copy in held["dk_c"]:
            copy.wait_recv()
        far = (1 - y) * 2 + c
        dkv[far] = (dkv[far].astype(F32) + dkv_c[1 - y].astype(F32)).astype(BF)
        held["dk_y"] = send(dkv.at[far], dkv_y, dk_s.at[2], dk_r.at[2], "y")

    def task_gq():
        loop(heads, grad_query)

    def task_gkv():
        held["dk_y"].wait_recv()
        d_own = dkv[s].astype(F32) + dkv_c[y].astype(F32) + dkv_y[...].astype(F32)
        turned = turn(d_own[:, 0:head], cos_t[...], -sin_t[...])
        pulled, g_row = rms_pull(qkv_f[heads], gain(2, head), turned)
        gain_add(2, head, g_row)
        d_qkv[:, wide : wide + head] = pulled.astype(BF)
        d_qkv[:, wide + head : wide + 2 * head] = d_own[:, head : 2 * head].astype(BF)
        full = dot(attn_in_t[...], d_qkv[:, wide : wide + 2 * head]).astype(BF)
        for n in range(2):
            for j in range(4):
                for i in range(4):
                    grads[n, 4 * j + i, at_kv : at_kv + block, :] = full[
                        half * n + block * i : half * n + block * (i + 1), 128 * j : 128 * (j + 1)
                    ]
        down_f[...] = dot_nt(d_qkv[...], qkv_mat[...])


    def norm_first(r0, r):
        pulled, g_row = rms_pull(tok[r, :].astype(F32), gain(0, width), down_f[r, :])
        gain_add(0, width, g_row)
        pack(1, r0, 64, d_h1[r, :] + pulled)

    def task_last():
        by_number(64, norm_first)
        copy = pltpu.make_async_copy(packed, flat_out.at[:, pl.ds(plan.total, 2 * plan.token_rows)], out_sem.at[0])
        copy.start()
        outs.append(copy)
        for i in range(6):
            for t in range(tiles):
                gain_rows[i * tiles + t : i * tiles + t + 1, :] = gain_acc[i : i + 1, 128 * t : 128 * (t + 1)]
        for p in range(2):
            low = gain_rows[16 * p : 16 * (p + 1), :].astype(BF)
            for h in range(2):
                grads[h, p, plan.gains_at : plan.gains_at + 16, :] = low

    def task_w(way, i):
        {"x": weight_x, "a": weight_a, "b": weight_b, "c": weight_c, "d": weight_d}[way](i)

    named = {
        "init": task_init, "norm": task_norm, "kv": task_kv, "q": task_q, "kvf": task_kvf, "keys": task_keys, "kvt": task_kvt, "at": task_at,
        "outp": task_outp, "ff": task_ff, "down": task_down, "nout": task_nout, "gd": task_gd, "fb": task_fb,
        "mid": task_mid, "gout": task_gout, "ab": task_ab, "dks": task_dks, "dky": task_dky, "gq": task_gq,
        "gkv": task_gkv, "last": task_last,
    }
    for entry in SCHEDULE:
        name, *rest = entry
        if name == "sum":
            steps_of[DIRECT[rest[0]]][rest[1]](rest[0])
        elif name[0] == "w":
            task_w(name[1], *rest)
        else:
            named[name](*rest)
    freed = [hops[k, 0] for k in range(len(plan.chunks))]
    for copy in sends:
        if not any(copy is other for other in freed):
            copy.wait_send()
    for copy in outs:
        copy.wait()


def spread_kernel(plan, flat, *refs):
    (res_o, dtok_o, q_o, k_o, v_o, o_o, g_o, u_o, d_o, gin, gq, gk, ga, gf, go, gains_f) = refs
    step = pl.program_id(0)
    at_down, at_gate, at_up, at_out, at_q, at_kv = plan.starts
    half, block, head, tiles = plan.half, plan.block, plan.head, plan.tiles

    def put(ref, rows, size, col, i, at):
        ref[rows : rows + size, col : col + 128] = flat[i, at : at + size, :].astype(F32)

    for i in range(4):
        for n, ref in enumerate((res_o, dtok_o)):
            for t in range(tiles):
                at = plan.total + n * plan.token_rows + 16 * t
                ref[16 * i : 16 * (i + 1), 128 * t : 128 * (t + 1)] = flat[i, at : at + 16, :]
        for at, ref, size in ((at_down, d_o, plan.ff // 32), (at_out, o_o, plan.heads * head // 32)):
            for t in range(tiles):
                put(ref, size * i, size, 128 * t, i, at + size * t)
        put(g_o, 0, half, 128 * i, i, at_gate)
        put(u_o, 0, half, 128 * i, i, at_up)
        for t in range(2):
            put(q_o, block * i, block, 128 * t, i, at_q + block * t)

    @pl.when(step < 2)
    def _():
        for i in range(4):
            put(k_o, block * i, block, 0, i, at_kv)

    @pl.when(step >= 2)
    def _():
        for i in range(4):
            put(v_o, block * i, block, 0, i, at_kv)

    @pl.when(step == 0)
    def _():
        gains_f[...] = jnp.zeros_like(gains_f)
        for p in range(2):
            lines = flat[p, plan.gains_at : plan.gains_at + 16, :].astype(F32)
            for n in range(16):
                i, t = (16 * p + n) // tiles, (16 * p + n) % tiles
                if i < 6:
                    gains_f[i : i + 1, 128 * t : 128 * (t + 1)] = lines[n : n + 1, :]
        first = lax.axis_index("fsdp") == 0
        values = gains_f[...]
        own = jnp.where(first, values, pltpu.roll(values, half, 1))
        for i, ref in ((0, gin), (3, ga), (4, gf), (5, go)):
            ref[...] = own[i, 0:half]
        own = jnp.where(first, values[:, 0 : head // 2], values[:, head // 2 : head])
        gq[...] = own[1, :]
        gk[...] = own[2, :]


def fused(tokens, d_out, doc_lengths, *weights):
    w_query, w_key, w_value, w_out, w_gate, w_up, w_down = weights[:7]
    gains = weights[7:]
    rows, width = tokens.shape[1:]
    head = 2 * weights[8].shape[0]
    heads = w_query.shape[1] // head
    ff = w_gate.shape[1]
    plan = Plan(rows, width, heads, head, ff)
    freq = jnp.asarray(
        np.power(ROPE_BASE, -2.0 * np.arange(head // 2) / head).astype(np.float32)[None]
    )
    vmem, far = pl.BlockSpec(memory_space=pltpu.VMEM), pl.BlockSpec(memory_space=pl.ANY)
    scratch = lambda *shape: pltpu.VMEM(shape, BF)
    scratch32 = lambda *shape: pltpu.VMEM(shape, F32)
    wide = heads * head
    total, chunks = plan.total, len(plan.chunks)
    dma = lambda *shape: pltpu.SemaphoreType.DMA(shape)
    tiles_ff = ff // head
    scratch_shapes = [
        scratch(width, wide + 2 * head),
        scratch(wide, width),
        scratch(width, ff),
        scratch(width, ff),
        scratch(ff, width),
        scratch32(8, width),
        scratch32(8, width),
        scratch32(8, width),
        scratch(rows, width),
        scratch(width, rows),
        scratch32(heads + 2, rows, head),
        scratch(heads, rows, head),
        scratch(4, rows, 2 * head),
        scratch(head, 4 * rows),
        scratch(head, 4 * rows),
        scratch(heads, 4 * rows, rows),
        scratch(rows, wide),
        scratch32(rows, width),
        scratch32(rows, width),
        scratch(rows, width),
        scratch(width, rows),
        scratch32(tiles_ff, rows, head),
        scratch32(tiles_ff, rows, head),
        scratch(rows, ff),
        scratch32(rows, width),
        scratch(rows, width),
        scratch32(rows, width),
        scratch(rows, width),
        scratch(heads, rows, head),
        scratch(4, rows, 2 * head),
        scratch(2, rows, 2 * head),
        scratch(rows, 2 * head),
        scratch(rows, wide + 2 * head),
        scratch32(rows, 128),
        scratch32(rows, 128),
        scratch(4 * rows, rows),
        scratch32(8, width),
        scratch32(32, 128),
        scratch(2, 16, total, 128),
        scratch(2, 8, total, 128),
        scratch(8, total, 128),
        scratch(4, total, 128),
        scratch(3, total, 128),
        dma(7),
        dma(3 * len(WEIGHTS)),
        dma(3 * len(WEIGHTS)),
        dma(len(WEIGHTS), 7),
        dma(len(WEIGHTS), 7),
        dma(6),
        dma(6),
        dma(3),
        dma(3),
        dma(1),
        dma(1),
        dma(chunks, 16),
        dma(chunks, 16),
        dma(chunks, 2),
        pltpu.SemaphoreType.REGULAR((chunks,)),
        scratch(16, 2 * plan.token_rows, 128),
        dma(1),
    ]
    flat = pl.pallas_call(
        functools.partial(layer_kernel, plan),
        out_shape=pltpu.VMEM((16, total + 2 * plan.token_rows, 128), BF),
        in_specs=[pl.BlockSpec(memory_space=pltpu.SMEM)] + [vmem] * 9 + [far] * 7,
        out_specs=far,
        scratch_shapes=scratch_shapes,
        compiler_params=pltpu.CompilerParams(
            collective_id=0, has_side_effects=True, vmem_limit_bytes=55 * 2**20
        ),
        name="layer",
    )(doc_lengths, freq, *gains, tokens[0], d_out[0], w_query, w_key, w_value, w_out, w_gate, w_up, w_down)
    half, block = plan.half, plan.block
    whole = lambda *shape: pl.BlockSpec(shape, lambda p: (0,) * len(shape))
    shape32 = lambda *shape: jax.ShapeDtypeStruct(shape, F32)
    outs = pl.pallas_call(
        functools.partial(spread_kernel, plan),
        grid=(4,),
        out_shape=[
            jax.ShapeDtypeStruct((rows, width), BF),
            jax.ShapeDtypeStruct((rows, width), BF),
            shape32(half, wide),
            shape32(half, head),
            shape32(half, head),
            shape32(wide // 2, width),
            shape32(half, ff),
            shape32(half, ff),
            shape32(ff // 2, width),
            shape32(half),
            shape32(head // 2),
            shape32(head // 2),
            shape32(half),
            shape32(half),
            shape32(half),
        ],
        in_specs=[
            pl.BlockSpec((4, total + 2 * plan.token_rows, 128), lambda p: (p, 0, 0)),
        ],
        out_specs=[
            pl.BlockSpec((rows // 4, width), lambda p: (p, 0)),
            pl.BlockSpec((rows // 4, width), lambda p: (p, 0)),
            pl.BlockSpec((half, head), lambda p: (0, p)),
            pl.BlockSpec((half, 128), lambda p: (0, jnp.minimum(p, 1))),
            pl.BlockSpec((half, 128), lambda p: (0, jnp.maximum(p, 2) - 2)),
            pl.BlockSpec((wide // 8, width), lambda p: (p, 0)),
            pl.BlockSpec((half, ff // 4), lambda p: (0, p)),
            pl.BlockSpec((half, ff // 4), lambda p: (0, p)),
            pl.BlockSpec((ff // 8, width), lambda p: (p, 0)),
            whole(half),
            whole(head // 2),
            whole(head // 2),
            whole(half),
            whole(half),
            whole(half),
        ],
        scratch_shapes=[scratch32(8, width)],
        compiler_params=pltpu.CompilerParams(vmem_limit_bytes=24 * 2**20),
        name="spread",
    )(flat)
    return (outs[0][None], outs[1][None]) + tuple(outs[2:])


def solution(mesh):
    whole = mesh.shape
    small = whole["rep"] == 4 and whole["fsdp"] == 2 and whole["seq"] == 4
    body = fused if small else general
    in_specs = (
        P(("rep", "fsdp"), "seq", None),
        P(("rep", "fsdp"), "seq", None),
        P(("rep", "fsdp"), None),
        P("fsdp", None),
        P("fsdp", None),
        P("fsdp", None),
        P("fsdp", None),
        P("fsdp", None),
        P("fsdp", None),
        P("fsdp", None),
        P("fsdp"),
        P("fsdp"),
        P("fsdp"),
        P("fsdp"),
        P("fsdp"),
        P("fsdp"),
    )
    out_specs = (
        P(("rep", "fsdp"), "seq", None),
        P(("rep", "fsdp"), "seq", None),
        P("fsdp", None),
        P("fsdp", None),
        P("fsdp", None),
        P("fsdp", None),
        P("fsdp", None),
        P("fsdp", None),
        P("fsdp", None),
        P("fsdp"),
        P("fsdp"),
        P("fsdp"),
        P("fsdp"),
        P("fsdp"),
        P("fsdp"),
    )
    return jax.shard_map(body, mesh=mesh, in_specs=in_specs, out_specs=out_specs, check_vma=False)
```
